128 devices in a mesh: rep: 4 (over z), fsdp: 16 (over y, x), cp: 2 (over core).
Axes of the slice: x: 4, y: 4, z: 4, core: 2. Of those that a mesh axis runs over, the one named last changes fastest.
Arguments:
- inputs: bfloat16 [64, 512, 1536], P(('rep', 'fsdp'), 'cp'), may hold values from -6 to 6
- segments: int32 [64, 512], P(('rep', 'fsdp')), may hold values from 0 to 3, as said below
- norm_gain: bfloat16 [1536], P('fsdp'), may hold values from 0.5 to 1.5
- w_in: bfloat16 [1536, 6448], P('fsdp'), may hold values from -0.15625 to 0.15625
- conv_w: bfloat16 [4, 3328], P(None, 'fsdp'), may hold values from -3 to 3
- conv_b: bfloat16 [3328], P('fsdp'), may hold values from -0.5 to 0.5
- dt_bias: bfloat16 [48], P('fsdp'), may hold values from -6.5 to -2.5
- a_log: bfloat16 [48], P('fsdp'), may hold values from 0 to 2.5
- d_skip: bfloat16 [48], P('fsdp'), may hold values from 0.5 to 1.5
- out_gain: bfloat16 [3072], P('fsdp'), may hold values from 0.5 to 1.5
- w_out: bfloat16 [3072, 1536], P('fsdp'), may hold values from -0.109375 to 0.109375
- cotangent: bfloat16 [64, 512, 1536], P(('rep', 'fsdp'), 'cp'), may hold values from -6 to 6
Outputs:
- output: bfloat16 [64, 512, 1536], P(('rep', 'fsdp'), 'cp')
- input_grad: bfloat16 [64, 512, 1536], P(('rep', 'fsdp'), 'cp')
- norm_gain_grad: float32 [1536], P('fsdp')
- w_in_grad: float32 [1536, 6448], P('fsdp')
- conv_w_grad: float32 [4, 3328], P(None, 'fsdp')
- conv_b_grad: float32 [3328], P('fsdp')
- dt_bias_grad: float32 [48], P('fsdp')
- a_log_grad: float32 [48], P('fsdp')
- d_skip_grad: float32 [48], P('fsdp')
- out_gain_grad: float32 [3072], P('fsdp')
- w_out_grad: float32 [3072, 1536], P('fsdp')
The draws below stay inside these ranges and needn't reach their ends.
Inputs may be any that keep to these rules, and one draw needn't show every extreme that they name: `segments`: within a sequence the numbers start at 0, never fall and rise by at most one from token to token; a document that neither begins nor ends a sequence spans at least 204 tokens.
All inputs are finite; a program needn't handle non-finite values.
Results may differ from the reference program's by a relative error of at most 0.0068.
Values may be sent and summed in bfloat16 or wider, within the bound.
No kernel may reach another device: no remote copies, remote signals or barrier semaphores. Data moves between devices by JAX's collectives and lax.ppermute only.
A program may use at most 256 MiB of HBM per device.

```python
import jax
import jax.numpy as jnp
from jax import lax

D = 1536
INNER = 3072
HEADS = 48
CONV = 4
SEQ = 512
BATCH = 64
XBC = 3328
EXTRA = 6448


def draw_segments(key, part):
    first_key, second_key = jax.random.split(jax.random.fold_in(key, 17))
    shortest = 2 * SEQ // 5
    doc_length = jax.random.randint(first_key, (BATCH, 1), shortest, 4 * SEQ + 1)
    doc_length = doc_length.at[0, 0].set(shortest)
    raw_offset = jax.random.randint(second_key, (BATCH, 1), 0, 4 * SEQ)
    doc_offset = raw_offset % doc_length
    doc_offset = doc_offset.at[0, 0].set(shortest - 1)
    positions = jnp.arange(SEQ, dtype=jnp.int32)[None, :]
    return ((positions + doc_offset) // doc_length - doc_offset // doc_length).astype(jnp.int32)


def steps_of(key, dims, cuts, low, largest):
    gain = 1.0
    for axis_at, shards_of in cuts:
        heights = jax.random.uniform(jax.random.fold_in(jax.random.fold_in(key, 6), axis_at), (shards_of,), jnp.float32, low / len(cuts), largest / len(cuts))
        gain = gain * jnp.repeat(jnp.exp(heights), dims[axis_at] // shards_of).reshape((-1,) + (1,) * (len(dims) - 1 - axis_at))
    return gain


def gaussian(stream_key, dims, width, reach, cuts=(), kind=jnp.bfloat16):
    values = width * jax.random.normal(stream_key, dims, jnp.float32)
    if cuts:
        values = values * steps_of(stream_key, dims, cuts, -0.22, 0.18)
    return jnp.clip(values, -reach, reach).astype(kind)


def setup_inputs(seed: int = 0) -> dict:
    keys = jax.random.split(jax.random.key(seed), 13)
    inputs = gaussian(keys[0], (BATCH, SEQ, D), 1.0, 6.0, ((0, 64), (1, 2)))
    segments = draw_segments(jax.random.fold_in(keys[12], 71), 0)
    norm_gain = jnp.clip(1.0 + 0.1 * jax.random.normal(keys[2], (D,), jnp.float32), 0.5, 1.5).astype(jnp.bfloat16)
    w_in = gaussian(keys[3], (D, EXTRA), D ** -0.5, 0.15625, ((0, 16),))
    conv_w = gaussian(keys[4], (CONV, XBC), CONV ** -0.5, 3.0, ((1, 16),))
    conv_b = jnp.clip(jax.random.uniform(keys[5], (XBC,), jnp.float32, -0.5, 0.5) * steps_of(keys[5], (XBC,), ((0, 16),), -0.4, 0.0), -0.5, 0.5).astype(jnp.bfloat16)
    dt_bias = jnp.clip(-6.5 + 4.0 * jax.random.uniform(keys[6], (HEADS,), jnp.float32) ** steps_of(keys[6], (HEADS,), ((0, 16),), -0.2, 0.2), -6.5, -2.5).astype(jnp.bfloat16)
    a_log = jnp.clip(2.5 * jax.random.uniform(keys[7], (HEADS,), jnp.float32) ** steps_of(keys[7], (HEADS,), ((0, 16),), -0.2, 0.2), 0.0, 2.5).astype(jnp.bfloat16)
    d_skip = jnp.clip(0.5 + 1.0 * jax.random.uniform(keys[8], (HEADS,), jnp.float32) ** steps_of(keys[8], (HEADS,), ((0, 16),), -0.2, 0.2), 0.5, 1.5).astype(jnp.bfloat16)
    out_gain = jnp.clip(1.0 + 0.1 * jax.random.normal(keys[9], (INNER,), jnp.float32), 0.5, 1.5).astype(jnp.bfloat16)
    w_out = gaussian(keys[10], (INNER, D), INNER ** -0.5, 0.109375, ((0, 16),))
    cotangent = gaussian(keys[11], (BATCH, SEQ, D), 1.0, 6.0, ((0, 64), (1, 2)))
    return {"inputs": inputs, "segments": segments, "norm_gain": norm_gain, "w_in": w_in, "conv_w": conv_w, "conv_b": conv_b, "dt_bias": dt_bias, "a_log": a_log, "d_skip": d_skip, "out_gain": out_gain, "w_out": w_out, "cotangent": cotangent}


EPS = 1e-05
HIGHEST_PRECISION = lax.Precision.HIGHEST

def silu_of(values):
    return values * jax.nn.sigmoid(values)

def middle(projected, seg_row, conv_arg, bias_arg, dtb_arg, alog_arg, skip_arg, gain_arg):
    length = projected.shape[0]
    inner_width = gain_arg.shape[0]
    xwidth = bias_arg.shape[0]
    nstate = (xwidth - inner_width) // 2
    head_count = dtb_arg.shape[0]
    conv_taps = conv_arg.shape[0]
    gate_in = projected[:, :inner_width]
    padded = jnp.concatenate([jnp.zeros((conv_taps - 1, xwidth), jnp.float32), projected[:, inner_width:inner_width + xwidth]], 0)
    seg_pad = jnp.concatenate([jnp.full((conv_taps - 1,), -1, jnp.int32), seg_row.astype(jnp.int32)], 0)
    summed = jnp.zeros((length, xwidth), jnp.float32) + bias_arg[None, :]
    for offset in range(conv_taps):
        matching = (seg_pad[offset:offset + length] == seg_row).astype(jnp.float32)[:, None]
        summed = summed + conv_arg[offset][None, :] * padded[offset:offset + length] * matching
    active = silu_of(summed)
    ssd_in = active[:, :inner_width]
    b_mat = active[:, inner_width:inner_width + nstate]
    c_mat = active[:, inner_width + nstate:]
    dt_val = jax.nn.softplus(projected[:, inner_width + xwidth:] + dtb_arg[None, :])
    cum_rate = jnp.cumsum(-jnp.exp(alog_arg)[None, :] * dt_val, axis=0)
    scores = jnp.dot(c_mat, b_mat.T, precision=HIGHEST_PRECISION)
    places = jnp.arange(length)
    allowed = (places[:, None] >= places[None, :]) & (seg_row[:, None] == seg_row[None, :])
    spread = cum_rate.T[:, :, None] - cum_rate.T[:, None, :]
    decay_mat = jnp.where(allowed[None], jnp.exp(jnp.where(allowed[None], spread, 0.0)), 0.0)
    mixing = scores[None] * decay_mat * dt_val.T[:, None, :]
    heads_in = ssd_in.reshape(length, head_count, -1)
    result = jnp.einsum('hts,shp->thp', mixing, heads_in, precision=HIGHEST_PRECISION)
    result = result + skip_arg[None, :, None] * heads_in
    gated_out = result.reshape(length, inner_width) * silu_of(gate_in)
    rms_scale = lax.rsqrt(lax.optimization_barrier(jnp.mean(gated_out * gated_out, axis=-1, keepdims=True)) + EPS)
    return gated_out * rms_scale * gain_arg[None, :]

def reference(inputs, segments, norm_gain, w_in, conv_w, conv_b, dt_bias, a_log, d_skip, out_gain, w_out, cotangent):
    norm_f = norm_gain.astype(jnp.float32)
    conv_f = conv_w.astype(jnp.float32)
    bias_f = conv_b.astype(jnp.float32)
    dtb_f = dt_bias.astype(jnp.float32)
    alog_f = a_log.astype(jnp.float32)
    skip_f = d_skip.astype(jnp.float32)
    gain_f = out_gain.astype(jnp.float32)

    def one_sequence(totals, entries):
        x_seq, seg_row, cot_seq = entries
        x_rows = x_seq.astype(jnp.float32)
        inverse = lax.rsqrt(lax.optimization_barrier(jnp.mean(x_rows * x_rows, axis=-1, keepdims=True)) + EPS)
        normed = (x_rows * inverse * norm_f[None, :]).astype(jnp.bfloat16)
        projected = jnp.dot(normed, w_in, preferred_element_type=jnp.float32)

        def local_fn(proj_arg, conv_arg, bias_arg, dtb_arg, alog_arg, skip_arg, gain_arg):
            return middle(proj_arg, seg_row, conv_arg, bias_arg, dtb_arg, alog_arg, skip_arg, gain_arg)
        mixed, pullback = jax.vjp(local_fn, projected, conv_f, bias_f, dtb_f, alog_f, skip_f, gain_f)
        mixed_b = mixed.astype(jnp.bfloat16)
        output = (x_rows + jnp.dot(mixed_b, w_out, preferred_element_type=jnp.float32)).astype(jnp.bfloat16)
        d_mixed = jnp.dot(cot_seq, w_out.T, preferred_element_type=jnp.float32)
        d_proj, d_conv, d_bias, d_dtb, d_alog, d_skipg, d_gain = pullback(d_mixed)
        d_proj_b = d_proj.astype(jnp.bfloat16)
        g_win = jnp.dot(normed.T, d_proj_b, preferred_element_type=jnp.float32)
        d_normed = jnp.dot(d_proj_b, w_in.T, preferred_element_type=jnp.float32)
        g_wout = jnp.dot(mixed_b.T, cot_seq, preferred_element_type=jnp.float32)
        scaled = x_rows * inverse
        g_norm = lax.optimization_barrier(jnp.sum(d_normed * scaled, axis=0))
        d_hat = d_normed * norm_f[None, :]
        d_x = inverse * (d_hat - scaled * lax.optimization_barrier(jnp.mean(d_hat * scaled, axis=-1, keepdims=True)))
        input_grad = (cot_seq.astype(jnp.float32) + d_x).astype(jnp.bfloat16)
        updated = (totals[0] + g_norm, totals[1] + g_win, totals[2] + d_conv, totals[3] + d_bias, totals[4] + d_dtb, totals[5] + d_alog, totals[6] + d_skipg, totals[7] + d_gain, totals[8] + g_wout)
        return (updated, (output, input_grad))
    starting = (jnp.zeros(norm_gain.shape, jnp.float32), jnp.zeros(w_in.shape, jnp.float32), jnp.zeros(conv_w.shape, jnp.float32), jnp.zeros(conv_b.shape, jnp.float32), jnp.zeros(dt_bias.shape, jnp.float32), jnp.zeros(a_log.shape, jnp.float32), jnp.zeros(d_skip.shape, jnp.float32), jnp.zeros(out_gain.shape, jnp.float32), jnp.zeros(w_out.shape, jnp.float32))
    totals, stacked = lax.scan(one_sequence, starting, (inputs, segments, cotangent))
    return (stacked[0], stacked[1], totals[0], totals[1], totals[2], totals[3], totals[4], totals[5], totals[6], totals[7], totals[8])
```

```python
import functools
import jax
import jax.numpy as jnp
from jax import lax
from jax.experimental import pallas as pl
from jax.experimental.pallas import tpu as pltpu
from jax.sharding import Mesh, PartitionSpec as P

F32 = jnp.float32
BF16 = jnp.bfloat16
Q = 128
CHUNKS = 4
NEG = -1e30


def mm(a, b, dims=((1,), (0,))):
    return lax.dot_general(a.astype(BF16), b.astype(BF16), (dims, ((), ())), preferred_element_type=F32)


def halves(a):
    top = a.astype(BF16)
    return top, (a - top.astype(F32)).astype(BF16)


def mm3(a, b, dims=((1,), (0,))):
    a_top, a_low = halves(a)
    b_top, b_low = halves(b)
    return mm(a_top, b_top, dims) + (mm(a_low, b_top, dims) + mm(a_top, b_low, dims))


def mm_fold(a, b):
    top, low = halves(a)
    return mm(top, b) + mm(low, b)


def mm_tri(tri, b):
    return mm(jnp.concatenate([tri, tri], 1), jnp.concatenate(halves(b), 0))


def iota(shape, axis):
    return lax.broadcasted_iota(jnp.int32, shape, axis)


def gather_mat(width, cols, head):
    return (iota((width, cols), 0) // head == iota((width, cols), 1)).astype(BF16)


def conv_of(ch, ext, aux, par, width):
    conv = ch * par[3:4, :width] + par[4:5, :width]
    shifted = []
    for s in range(1, 4):
        sh = pltpu.roll(ext, s, 0)[8:] * aux[:, s : s + 1]
        shifted.append(sh)
        conv = conv + par[3 - s : 4 - s, :width] * sh
    return conv, shifted


def softplus(v):
    return jnp.maximum(v, 0.0) + jnp.log1p(jnp.exp(-jnp.abs(v)))


def rates(raw, hp):
    pre = raw + hp[0:1]
    dt = softplus(pre)
    tri = (iota((Q, Q), 0) >= iota((Q, Q), 1)).astype(BF16)
    return pre, dt, mm_tri(tri, -hp[1:2] * dt)


def widen(cum, dt, aux, heads, low):
    squares = [jnp.broadcast_to(cum[:, h : h + 1], (Q, Q)) for h in range(heads)]
    pairs = range(0, heads, 2)
    cum_w = jnp.concatenate([jnp.where(low, squares[h], squares[h + 1]) for h in pairs], 1)
    dt_w = jnp.concatenate([jnp.where(low, dt[:, h : h + 1], dt[:, h + 1 : h + 2]) for h in pairs], 1)
    fin_w = cum_w[Q - 1 : Q]
    enter_w = jnp.exp(cum_w) * aux[:, 4:5]
    leave_w = jnp.exp(fin_w - cum_w) * aux[:, 5:6]
    through_w = jnp.exp(fin_w) * aux[0:1, 6:7]
    return squares, dt_w, enter_w, leave_w, through_w


def ssd_fwd_kernel(c_ref, p_ref, aux_ref, seg_ref, par_ref, hp_ref, y_ref, sin_ref, rim, state, *, inner, nst, head):
    width = inner + 2 * nst
    state[...] = jnp.zeros_like(state)
    rim[...] = jnp.zeros_like(rim)
    par = par_ref[...]
    hp = hp_ref[...]
    core = c_ref[0]
    lax.fori_loop(0, CHUNKS, lambda t, _: ssd_fwd_chunk(t, core, p_ref, aux_ref, seg_ref, par, hp, y_ref, sin_ref, rim, state, inner, nst, head), None)


def place_of(t, core):
    return lax.rem(lax.div(t, 2) + core, 2), pl.ds(pl.multiple_of(lax.rem(t, 2) * Q, Q), Q)


def ssd_fwd_chunk(t, core, p_ref, aux_ref, seg_ref, par, hp, y_ref, sin_ref, rim, state, inner, nst, head):
    width = inner + 2 * nst
    side, rows = place_of(t, core)
    aux = aux_ref[pl.ds(pl.multiple_of(t * Q, Q), Q), :]
    ch = p_ref[side, 0, rows, :width]
    conv, _ = conv_of(ch, jnp.concatenate([rim[...], ch], 0), aux, par, width)
    rim[...] = ch[Q - 8 :]
    act = conv / (1.0 + jnp.exp(-conv))
    x_in, bm, cm = act[:, :inner], act[:, inner : inner + nst], act[:, inner + nst :]
    pre, dt, cum = rates(p_ref[side, 0, rows, width:], hp)
    low = iota((Q, 2 * head), 1) < head
    squares, dt_w, enter_w, leave_w, through_w = widen(cum, dt, aux, inner // head, low)
    xdt = x_in * dt_w
    scores = mm3(cm, bm, ((1,), (1,)))
    allowed = (iota((Q, Q), 0) >= iota((Q, Q), 1)) & (aux[:, 0:1] == seg_ref[t, 0:1, :])
    cum_t = cum.T
    s_old = state[...]
    sin_ref[t] = s_old
    result = enter_w * mm(cm, s_old) + par[6:7, :inner] * x_in
    for pair in range(inner // (2 * head)):
        cols = slice(2 * head * pair, 2 * head * (pair + 1))
        xp = xdt[:, cols].astype(BF16)
        none = jnp.zeros_like(xp)
        mixing = []
        for h in (2 * pair, 2 * pair + 1):
            decay = jnp.exp(jnp.where(allowed, squares[h] - cum_t[h : h + 1, :], NEG))
            mixing.append((scores * decay).astype(BF16))
        by_head = jnp.concatenate([jnp.where(low, xp, none), jnp.where(low, none, xp)], 0)
        y_ref[side, 0, rows, cols] = result[:, cols] + mm(jnp.concatenate(mixing, 1), by_head)
    state[...] = through_w * s_old + mm(bm, xdt * leave_w, ((0,), (0,)))


def ssd_bwd_kernel(
    c_ref, p_ref, aux_ref, seg_ref, par_ref, hp_ref, dy_ref, sin_ref,
    dp_ref, gconv_ref, ghead_ref, gskip_ref, rim, state, *, inner, nst, head,
):
    core = c_ref[0]
    state[...] = jnp.zeros_like(state)
    rim[...] = jnp.zeros_like(rim)

    @pl.when(pl.program_id(0) == 0)
    def _():
        gconv_ref[...] = jnp.zeros_like(gconv_ref)
        ghead_ref[...] = jnp.zeros_like(ghead_ref)
        gskip_ref[...] = jnp.zeros_like(gskip_ref)

    par = par_ref[...]
    hp = hp_ref[...]
    lax.fori_loop(
        0,
        CHUNKS,
        lambda t, _: ssd_bwd_chunk(
            CHUNKS - 1 - t, core, p_ref, aux_ref, seg_ref, par, hp, dy_ref, sin_ref, dp_ref, gconv_ref, ghead_ref, gskip_ref, rim, state, inner, nst, head
        ),
        None,
    )


def ssd_bwd_chunk(
    t, core, p_ref, aux_ref, seg_ref, par, hp, dy_ref, sin_ref, dp_ref, gconv_ref, ghead_ref, gskip_ref, rim, state, inner, nst, head
):
    width = inner + 2 * nst
    side, rows = place_of(t, core)
    aux = aux_ref[pl.ds(pl.multiple_of(t * Q, Q), Q), :]
    ch = p_ref[side, 0, rows, :width]
    prior = jnp.maximum(t - 1, 0)
    prev = p_ref[lax.rem(lax.div(prior, 2) + core, 2), 0, pl.ds(pl.multiple_of(lax.rem(prior, 2) * Q + Q - 8, 8), 8), :width]
    prev = prev * jnp.where(t == 0, 0.0, 1.0)
    conv, shifted = conv_of(ch, jnp.concatenate([prev, ch], 0), aux, par, width)
    sig = 1.0 / (1.0 + jnp.exp(-conv))
    act = conv * sig
    x_in, bm, cm = act[:, :inner], act[:, inner : inner + nst], act[:, inner + nst :]
    pre, dt, cum = rates(p_ref[side, 0, rows, width:], hp)
    low = iota((Q, 2 * head), 1) < head
    squares, dt_w, enter_w, leave_w, through_w = widen(cum, dt, aux, inner // head, low)
    xdt = x_in * dt_w
    scores = mm3(cm, bm, ((1,), (1,)))
    allowed = (iota((Q, Q), 0) >= iota((Q, Q), 1)) & (aux[:, 0:1] == seg_ref[t, 0:1, :])
    cum_t = cum.T
    bm = bm.astype(BF16)
    cm = cm.astype(BF16)
    dy = dy_ref[side, 0, rows, :]
    s_in = sin_ref[t]
    d_state = state[...]
    s_in_b = s_in.astype(BF16)
    d_state_b = d_state.astype(BF16)

    dye = (dy * enter_w).astype(BF16)
    inter = mm(cm, s_in_b) * enter_w
    from_state = mm(bm, d_state_b) * leave_w
    state[...] = mm(cm, dye, ((0,), (0,))) + through_w * d_state
    d_c = mm(dye, s_in_b, ((1,), (1,)))
    d_b = mm(xdt * leave_w, d_state_b, ((1,), (1,)))

    lane = iota((Q, Q), 1)
    sub = iota((8, Q), 0)
    d_scores = jnp.zeros((Q, Q), F32)
    row_sums = jnp.zeros((Q, Q), F32)
    col_sums = jnp.zeros((8, Q), F32)
    d_xdt = []
    for pair in range(inner // (2 * head)):
        cols = slice(2 * head * pair, 2 * head * (pair + 1))
        xp = xdt[:, cols]
        dyp = dy[:, cols]
        d_k2 = mm3(dyp, jnp.concatenate([jnp.where(low, xp, 0.0), jnp.where(low, 0.0, xp)], 0), ((1,), (1,)))
        kmats = []
        for k in range(2):
            h = 2 * pair + k
            decay = jnp.exp(jnp.where(allowed, squares[h] - cum_t[h : h + 1, :], NEG))
            d_k = d_k2[:, k * Q : (k + 1) * Q]
            kmat = scores * decay
            d_scores = d_scores + d_k * decay
            both = d_k * kmat
            row_sums = jnp.where(lane == h, jnp.sum(both, 1, keepdims=True), row_sums)
            col_sums = jnp.where(sub == h, jnp.sum(both, 0, keepdims=True), col_sums)
            kmats.append(kmat)
        dy_by_head = jnp.concatenate([jnp.where(low, dyp, 0.0), jnp.where(low, 0.0, dyp)], 0)
        d_xdt.append(mm3(jnp.concatenate(kmats, 0), dy_by_head, ((0,), (0,))))
    z = jnp.concatenate(d_xdt, 1) + from_state
    d_c = d_c + mm(d_scores, bm)
    d_b = d_b + mm(d_scores, cm, ((0,), (0,)))
    d_x = z * dt_w + par[6:7, :inner] * dy

    leaving = xdt * from_state
    ending = jnp.sum(s_in * d_state, 0, keepdims=True) * through_w + jnp.sum(leaving, 0, keepdims=True)
    folded = mm_fold(
        jnp.concatenate([x_in * z, dy * inter - leaving, jnp.broadcast_to(ending, (8, inner))], 0), gather_mat(inner, Q, head)
    )
    col_full = jnp.concatenate([col_sums, jnp.zeros((Q - 8, Q), F32)], 0).T
    d_cum = row_sums - col_full + folded[Q : 2 * Q]
    tri_up = (iota((Q, Q), 0) <= iota((Q, Q), 1)).astype(BF16)
    rev = mm_tri(tri_up, d_cum) + folded[2 * Q : 2 * Q + 1]
    d_dt = folded[:Q] - hp[1:2] * rev
    d_raw = d_dt / (1.0 + jnp.exp(-pre))
    live = (iota((1, Q), 1) < inner // head).astype(F32)
    d_raw = d_raw * live
    ghead_ref[0:1, :] += jnp.sum(d_raw, 0, keepdims=True)
    ghead_ref[1:2, :] += jnp.sum(rev * dt, 0, keepdims=True) * -hp[1:2]
    gskip_ref[0:1, :] += jnp.sum(dy * x_in, 0, keepdims=True)

    d_act = jnp.concatenate([d_x, d_b, d_c], 1)
    d_conv = d_act * (sig * (1.0 + conv * (1.0 - sig)))
    gconv_ref[4:5, :] += jnp.sum(d_conv, 0, keepdims=True)
    gconv_ref[3:4, :] += jnp.sum(d_conv * ch, 0, keepdims=True)
    d_ch = d_conv * par[3:4, :width]
    for s in range(1, 4):
        gconv_ref[3 - s : 4 - s, :] += jnp.sum(d_conv * shifted[s - 1], 0, keepdims=True)
        u = d_conv * aux[:, s : s + 1] * par[3 - s : 4 - s, :width]
        d_ch = d_ch + pltpu.roll(jnp.concatenate([u, rim[s - 1]], 0), Q + 8 - s, 0)[:Q]
        rim[s - 1] = u[:8]
    dp_ref[side, 0, rows, :width] = d_ch.astype(BF16)
    dp_ref[side, 0, rows, width:] = d_raw.astype(BF16)


def rows_spec(cols):
    return pl.BlockSpec((2, 1, CHUNKS * Q // 2, cols), lambda r, c: (0, r, 0, 0))


def common_specs(wide, width):
    return [
        rows_spec(wide),
        pl.BlockSpec((CHUNKS * Q, 128), lambda r, c: (r, 0)),
        pl.BlockSpec((CHUNKS, 8, Q), lambda r, c: (r, 0, 0)),
        pl.BlockSpec((8, width), lambda r, c: (0, 0)),
        pl.BlockSpec((8, 128), lambda r, c: (0, 0)),
    ]


def ssd_fwd(core, proj, aux, seg_rows, par, hp, *, inner, nst, head, interpret=False):
    seqs, half, wide = proj.shape[1:]
    rows = 2 * seqs * half
    width = inner + 2 * nst
    spec = pltpu.PrefetchScalarGridSpec(
        num_scalar_prefetch=1,
        grid=(seqs,),
        in_specs=common_specs(wide, width),
        out_specs=[rows_spec(inner), pl.BlockSpec((CHUNKS, nst, inner), lambda r, c: (r, 0, 0))],
        scratch_shapes=[pltpu.VMEM((8, width), F32), pltpu.VMEM((nst, inner), F32)],
    )
    y, s_in = pl.pallas_call(
        functools.partial(ssd_fwd_kernel, inner=inner, nst=nst, head=head),
        grid_spec=spec,
        out_shape=[
            jax.ShapeDtypeStruct((2, seqs, CHUNKS * Q // 2, inner), F32),
            jax.ShapeDtypeStruct((seqs * CHUNKS, nst, inner), F32),
        ],
        cost_estimate=pl.CostEstimate(flops=rows * 1000000, transcendentals=rows * 1500, bytes_accessed=rows * wide * 8),
        interpret=interpret,
        name="ssd_fwd",
    )(core, proj, aux, seg_rows, par, hp)
    return y, s_in


def ssd_bwd(core, proj, aux, seg_rows, par, hp, dy, s_in, *, inner, nst, head, interpret=False):
    seqs, half, wide = proj.shape[1:]
    rows = 2 * seqs * half
    width = inner + 2 * nst
    spec = pltpu.PrefetchScalarGridSpec(
        num_scalar_prefetch=1,
        grid=(seqs,),
        in_specs=common_specs(wide, width)
        + [rows_spec(inner), pl.BlockSpec((CHUNKS, nst, inner), lambda r, c: (r, 0, 0))],
        out_specs=[
            rows_spec(wide),
            pl.BlockSpec((8, width), lambda r, c: (0, 0)),
            pl.BlockSpec((8, 128), lambda r, c: (0, 0)),
            pl.BlockSpec((8, inner), lambda r, c: (0, 0)),
        ],
        scratch_shapes=[pltpu.VMEM((3, 8, width), F32), pltpu.VMEM((nst, inner), F32)],
    )
    d_proj, g_conv, g_head, g_skip = pl.pallas_call(
        functools.partial(ssd_bwd_kernel, inner=inner, nst=nst, head=head),
        grid_spec=spec,
        out_shape=[
            jax.ShapeDtypeStruct((2, seqs, CHUNKS * Q // 2, wide), BF16),
            jax.ShapeDtypeStruct((8, width), F32),
            jax.ShapeDtypeStruct((8, 128), F32),
            jax.ShapeDtypeStruct((8, inner), F32),
        ],
        cost_estimate=pl.CostEstimate(flops=rows * 2500000, transcendentals=rows * 2000, bytes_accessed=rows * wide * 12),
        interpret=interpret,
        name="ssd_bwd",
    )(core, proj, aux, seg_rows, par, hp, dy, s_in)
    return d_proj, g_conv, g_head, g_skip


def masks_of(seg):
    s_count, length = seg.shape
    cols = [seg.astype(F32)]
    for s in range(1, 4):
        back = jnp.concatenate([jnp.full((s_count, s), -1, seg.dtype), seg[:, :-s]], 1)
        cols.append((back == seg).astype(F32))
    by_chunk = seg.reshape(s_count, length // Q, Q)
    last = by_chunk[:, :, -1:]
    prev = jnp.concatenate([jnp.full((s_count, 1, 1), -1, seg.dtype), last[:, :-1]], 1)
    cols.append((by_chunk == prev).astype(F32).reshape(s_count, length))
    cols.append((by_chunk == last).astype(F32).reshape(s_count, length))
    cols.append(jnp.broadcast_to(prev == last, by_chunk.shape).astype(F32).reshape(s_count, length))
    aux = jnp.stack(cols, -1).reshape(s_count * length, len(cols))
    aux = jnp.pad(aux, ((0, 0), (0, 128 - len(cols))))
    rows = jnp.broadcast_to(seg.astype(F32).reshape(-1, 1, Q), (s_count * length // Q, 8, Q))
    return aux, rows


EPS = 1e-05
AXES = ("z", "y", "x", "c")


def pull(a, axis, d):
    return lax.ppermute(a, axis, [((i + d) % 4, i) for i in range(4)])


def swap(a):
    return lax.ppermute(a, "c", [(0, 1), (1, 0)])


def transpose_zy(a):
    return lax.ppermute(a, ("z", "y"), [(4 * y + z, 4 * z + y) for z in range(4) for y in range(4)])


def ring_all(a):
    half = a.shape[0] // 2
    one, three = pull(a, "z", 1), pull(a, "z", 3)
    two = jnp.concatenate([pull(one[:half], "z", 1), pull(three[half:], "z", 3)], 0)
    return [a, one, two, three]


def ring_sum(q):
    half = q[0].shape[0] // 2
    top = pull(q[2][:half].astype(BF16), "z", 3).astype(F32)
    bottom = pull(q[2][half:].astype(BF16), "z", 1).astype(F32)
    up = jnp.concatenate([q[1][:half].astype(F32) + top, q[1][half:].astype(F32)], 0)
    down = jnp.concatenate([q[3][:half].astype(F32), q[3][half:].astype(F32) + bottom], 0)
    return q[0].astype(F32) + pull(up.astype(BF16), "z", 3).astype(F32) + pull(down.astype(BF16), "z", 1).astype(F32)


def plane_all(a):
    return lax.all_to_all(jnp.broadcast_to(a[None], (16,) + a.shape), ("y", "x"), 0, 0)


def after(value, *others):
    return lax.optimization_barrier((value,) + others)[0]


def cost(flops, bytes_accessed):
    return pl.CostEstimate(flops=int(flops), transcendentals=0, bytes_accessed=int(bytes_accessed))


def whole(shape):
    return pl.BlockSpec(shape, lambda *_: (0,) * len(shape))


def near_spec(rows, cols):
    return pl.BlockSpec((1, rows, cols), lambda h, r: (jnp.where(h == 0, r, 3), 0, 0))


def far_spec(rows, cols):
    return pl.BlockSpec((1, rows, cols), lambda h, r: (jnp.where(h == 0, 0, r), 0, 0))


def block_spec(cols, rows=256):
    return pl.BlockSpec((1, 1, rows, cols), lambda h, r: (h, r, 0, 0))


def pick(near_ref, far_ref, rows):
    return lax.cond(pl.program_id(0) == 0, lambda: near_ref[0, :rows], lambda: far_ref[0, :rows])


def enter_kernel(near_ref, far_ref, gain_ref, w_ref, normed_ref, proj_ref):
    p = pick(near_ref, far_ref, normed_ref.shape[2]).astype(F32)
    inverse = lax.rsqrt(jnp.mean(p * p, -1, keepdims=True) + EPS)
    normed = (p * inverse * gain_ref[...]).astype(BF16)
    normed_ref[0, 0] = normed
    proj_ref[0, 0] = jnp.dot(normed, w_ref[...], preferred_element_type=F32)


def enter(near, far, gain, w):
    padded, model = near.shape[1:]
    rows, cols = 256, w.shape[1]
    return pl.pallas_call(
        enter_kernel,
        grid=(2, 4),
        out_shape=[jax.ShapeDtypeStruct((2, 4, rows, model), BF16), jax.ShapeDtypeStruct((2, 4, rows, cols), F32)],
        in_specs=[near_spec(padded, model), far_spec(padded, model), whole((1, model)), whole(w.shape)],
        out_specs=[block_spec(model), block_spec(cols)],
        cost_estimate=cost(16 * rows * model * cols, 8 * rows * (4 * model + 4 * cols)),
        name="enter",
    )(near, far, gain, w)


def gate_kernel(normed_ref, near_ref, far_ref, wg_ref, wo_ref, y_ref, gain_ref, gate_ref, dm_ref, sums_ref):
    gate = jnp.dot(normed_ref[0, 0], wg_ref[...], preferred_element_type=F32)
    cot = pick(near_ref, far_ref, gate.shape[0])
    d_mixed = lax.dot_general(cot, wo_ref[...], (((1,), (1,)), ((), ())), preferred_element_type=F32)
    gate_ref[0, 0] = gate
    dm_ref[0, 0] = d_mixed
    gated = y_ref[0, 0] * gate / (1.0 + jnp.exp(-gate))
    ones = jnp.ones((8, gate.shape[1]), BF16)

    def total(v):
        top, low = halves(v)
        return (mm(ones, top, ((1,), (1,))) + mm(ones, low, ((1,), (1,))))[:1]

    sums_ref[0, 0] = jnp.concatenate([total(gated * gated), total(d_mixed * gain_ref[...] * gated)], 0)


def gate_stage(normed, near, far, w_g, w_o, y, gain):
    rows, model = normed.shape[2:]
    mine = w_g.shape[1]
    return pl.pallas_call(
        gate_kernel,
        grid=(2, 4),
        out_shape=[jax.ShapeDtypeStruct((2, 4, rows, mine), F32)] * 2 + [jax.ShapeDtypeStruct((2, 4, 2, rows), F32)],
        in_specs=[
            block_spec(model),
            near_spec(rows, model),
            far_spec(rows, model),
            whole(w_g.shape),
            whole(w_o.shape),
            block_spec(mine),
            whole((1, mine)),
        ],
        out_specs=[block_spec(mine), block_spec(mine), block_spec(rows, 2)],
        cost_estimate=cost(32 * rows * model * mine, 8 * rows * (4 * model + 12 * mine)),
        name="gate_stage",
    )(normed, near, far, w_g, w_o, y, gain)


def turn_kernel(
    normed_ref, near_ref, far_ref, wo_ref, y_ref, gate_ref, dm_ref, sums_ref, gain_ref,
    out_near_ref, out_far_ref, dy_ref, dgate_ref, gwo_ref, ggate_ref, ggain_ref, acc_o, acc_g, *, inner,
):
    h, r = pl.program_id(0), pl.program_id(1)
    rows, mine = gate_ref.shape[2:]
    gate, d_mixed, y, gain = gate_ref[0, 0], dm_ref[0, 0], y_ref[0, 0], gain_ref[...]
    cot = pick(near_ref, far_ref, rows)
    sums = jnp.concatenate([sums_ref[0, 0], jnp.zeros((6, rows), F32)], 0).T
    scale = lax.rsqrt(sums[:, 0:1] / inner + EPS)
    lean = sums[:, 1:2] / inner * scale * scale
    sig = 1.0 / (1.0 + jnp.exp(-gate))
    act = gate * sig
    gated = y * act
    mixed = (gated * scale * gain).astype(BF16)
    d_gated = scale * (d_mixed * gain - gated * lean)
    dy_ref[0, 0] = d_gated * act
    d_gate = (d_gated * y * (sig * (1.0 + gate * (1.0 - sig)))).astype(BF16)
    dgate_ref[0, 0] = d_gate
    out = jnp.dot(mixed, wo_ref[...], preferred_element_type=F32).astype(BF16)

    @pl.when(h == 0)
    def _():
        out_near_ref[0] = out

    @pl.when(h == 1)
    def _():
        out_far_ref[0] = out

    @pl.when((h == 0) & (r == 0))
    def _():
        acc_o[...] = jnp.zeros_like(acc_o)
        acc_g[...] = jnp.zeros_like(acc_g)
        ggain_ref[...] = jnp.zeros_like(ggain_ref)

    ggain_ref[0:1, :] += jnp.sum(d_mixed * gated * scale, 0, keepdims=True)
    acc_o[...] += lax.dot_general(mixed, cot, (((0,), (0,)), ((), ())), preferred_element_type=F32)
    acc_g[...] += lax.dot_general(normed_ref[0, 0], d_gate, (((0,), (0,)), ((), ())), preferred_element_type=F32)

    @pl.when((h == 1) & (r == 3))
    def _():
        gwo_ref[...] = acc_o[...].astype(BF16)
        ggate_ref[...] = acc_g[...].astype(BF16)


def turn_stage(normed, near, far, w_o, y, gate, d_mixed, sums, gain, inner):
    rows, model = normed.shape[2:]
    mine = w_o.shape[0]
    return pl.pallas_call(
        functools.partial(turn_kernel, inner=inner),
        grid=(2, 4),
        out_shape=[
            jax.ShapeDtypeStruct((4, rows, model), BF16),
            jax.ShapeDtypeStruct((4, rows, model), BF16),
            jax.ShapeDtypeStruct((2, 4, rows, mine), F32),
            jax.ShapeDtypeStruct((2, 4, rows, mine), BF16),
            jax.ShapeDtypeStruct((mine, model), BF16),
            jax.ShapeDtypeStruct((model, mine), BF16),
            jax.ShapeDtypeStruct((8, mine), F32),
        ],
        in_specs=[
            block_spec(model),
            near_spec(rows, model),
            far_spec(rows, model),
            whole(w_o.shape),
            block_spec(mine),
            block_spec(mine),
            block_spec(mine),
            block_spec(rows, 2),
            whole((1, mine)),
        ],
        out_specs=[
            near_spec(rows, model),
            far_spec(rows, model),
            block_spec(mine),
            block_spec(mine),
            whole((mine, model)),
            whole((model, mine)),
            whole((8, mine)),
        ],
        scratch_shapes=[pltpu.VMEM((mine, model), F32), pltpu.VMEM((model, mine), F32)],
        cost_estimate=cost(48 * rows * model * mine, 8 * rows * (6 * model + 18 * mine)),
        name="turn_stage",
    )(normed, near, far, w_o, y, gate, d_mixed, sums, gain)


def back_kernel(dp_ref, wa_ref, dg_ref, wg_ref, out_ref):
    t = lax.dot_general(dp_ref[0, 0], wa_ref[...], (((1,), (1,)), ((), ())), preferred_element_type=F32)
    t = t + lax.dot_general(dg_ref[0, 0], wg_ref[...], (((1,), (1,)), ((), ())), preferred_element_type=F32)
    out_ref[0] = t.astype(BF16)


def back_dot(d_proj, w_a, d_gate, w_g, side):
    rows, ka = d_proj.shape[2:]
    m, kg = w_g.shape
    return pl.pallas_call(
        back_kernel,
        grid=(4,),
        out_shape=jax.ShapeDtypeStruct((4, rows, m), BF16),
        in_specs=[
            pl.BlockSpec((1, 1, rows, ka), lambda r: (side, r, 0, 0)),
            whole((m, ka)),
            pl.BlockSpec((1, 1, rows, kg), lambda r: (side, r, 0, 0)),
            whole((m, kg)),
        ],
        out_specs=pl.BlockSpec((1, rows, m), lambda r: (r, 0, 0)),
        cost_estimate=cost(8 * rows * m * (ka + kg), 2 * (4 * rows + m) * (ka + kg) + 8 * rows * m),
        name="back_dot",
    )(d_proj, w_a, d_gate, w_g)


def dot(a, b, dims):
    return lax.dot_general(a, b, (dims, ((), ())), preferred_element_type=F32)


def local(inputs, segments, norm_gain, w_in, conv_w, conv_b, dt_bias, a_log, d_skip, out_gain, w_out, cotangent):
    z, _, _, c = (lax.axis_index(name) for name in AXES)
    member = 2 * z + c
    length, model = inputs.shape[1:]
    inner = 16 * out_gain.shape[0]
    heads = 16 * d_skip.shape[0]
    xwidth = 16 * conv_b.shape[0]
    nst = (xwidth - inner) // 2
    head = inner // heads
    mine = inner // 8
    my_heads = heads // 8
    core = c.astype(jnp.int32).reshape(1)
    rows_in = w_in.shape[0]

    def lanes(a):
        return jnp.pad(a, ((0, 0), (0, -a.shape[1] % 128))).reshape(-1, 128)

    tiny = jnp.concatenate([dt_bias, a_log, d_skip])[None]
    small = jnp.concatenate([lanes(conv_w), lanes(conv_b[None]), lanes(out_gain[None]), lanes(norm_gain[None]), lanes(tiny)], 0)
    small = plane_all(jnp.pad(small, ((0, -small.shape[0] % 16), (0, 0)))).astype(F32)
    k, kn, hn = conv_b.shape[0], out_gain.shape[0], d_skip.shape[0]
    lk, lg = -(-k // 128), -(-kn // 128)
    conv_wf = small[:, : 4 * lk].reshape(16, 4, lk * 128)[:, :, :k].transpose(1, 0, 2).reshape(4, xwidth)
    conv_bf = small[:, 4 * lk : 5 * lk].reshape(16, lk * 128)[:, :k].reshape(1, xwidth)
    gain_f = small[:, 5 * lk : 5 * lk + lg].reshape(16, lg * 128)[:, :kn].reshape(-1)
    norm_f = small[:, 5 * lk + lg, :rows_in].reshape(-1)
    dtb_f, alog_f, skip_f = (small[:, 5 * lk + lg + 1, i * hn : (i + 1) * hn].reshape(-1) for i in range(3))

    def own(a, count):
        return lax.dynamic_slice_in_dim(a, member * count, count, a.ndim - 1)

    conv_all = jnp.concatenate([conv_wf, conv_bf], 0)
    conv_mine = jnp.concatenate([own(conv_all[:, :inner], mine), conv_all[:, inner:]], 1)
    skip_mine = jnp.repeat(own(skip_f, my_heads), head)
    par = jnp.concatenate(
        [conv_mine, jnp.zeros((1, mine + 2 * nst), F32), jnp.pad(skip_mine, (0, 2 * nst))[None], jnp.zeros((1, mine + 2 * nst), F32)], 0
    )
    rates_mine = jnp.stack([own(dtb_f, my_heads), jnp.exp(own(alog_f, my_heads))])
    hp = jnp.pad(rates_mine, ((0, 6), (0, 128 - my_heads)))
    gain_mine = own(gain_f, mine)[None]

    x_mine = inputs[0]
    seg_row = jnp.pad(segments, ((0, 15), (0, model - segments.shape[1]))).astype(BF16)
    x_near = jnp.stack(ring_all(jnp.concatenate([x_mine, seg_row], 0)))
    seg_all = x_near[:, length, : segments.shape[1]].astype(jnp.int32)
    aux, seg_rows = masks_of(seg_all)
    x_far = swap(x_near)

    w_x = lax.dynamic_slice_in_dim(w_in, inner + member * mine, mine, 1)
    w_dt = jnp.pad(
        lax.dynamic_slice_in_dim(w_in[:, inner + xwidth :], member * my_heads, my_heads, 1), ((0, 0), (0, 128 - my_heads))
    )
    w_bc = jnp.concatenate([w_in[:, inner + mine * 8 : inner + xwidth], w_dt], 1)
    all_a = plane_all(jnp.concatenate([w_x, w_bc], 1))
    w_a = all_a.reshape(model, -1)
    w_g = lax.dynamic_slice_in_dim(w_in, member * mine, mine, 1)
    part = w_out.shape[0] // 4
    half = model // 2
    wo_piece = lax.dynamic_slice(w_out, (z * part, c * half), (part, half))
    wo_piece = transpose_zy(jnp.concatenate([wo_piece[:, : half // 2], wo_piece[:, half // 2 :]], 0))
    all_b = plane_all(after(jnp.concatenate([w_g, wo_piece], 1), all_a))
    w_g = all_b[:, :, :mine].reshape(model, mine)
    w_o = all_b[:, :, mine:].reshape(4, 4, 2, part, half // 2).transpose(1, 0, 3, 2, 4).reshape(2, mine, half)
    wo_here = lax.dynamic_index_in_dim(w_o, c, 0, False)
    wo_there = swap(lax.dynamic_index_in_dim(w_o, 1 - c, 0, False))
    w_o = jnp.where(c == 0, jnp.concatenate([wo_here, wo_there], 1), jnp.concatenate([wo_there, wo_here], 1))

    sizes_k = dict(inner=mine, nst=nst, head=head)
    normed, proj = enter(x_near, x_far, norm_f[None], w_a)
    mixed_ssd, s_in = ssd_fwd(core, proj, aux, seg_rows, par, hp, **sizes_k)

    cot_near = jnp.stack(ring_all(after(cotangent[0], x_near)))
    cot_far = swap(cot_near)
    gate, d_mixed, sums = gate_stage(normed, cot_near, cot_far, w_g, w_o, mixed_ssd, gain_mine)
    sums = sums + jnp.flip(swap(sums), 0)
    sums = sums + jnp.roll(pull(sums, "z", 2), 2, 1)
    sums = sums + jnp.roll(pull(sums, "z", 1), 1, 1)
    out_near, out_far, d_y, d_gate, g_wo, g_gate, g_gain = turn_stage(
        normed, cot_near, cot_far, w_o, mixed_ssd, gate, d_mixed, sums, gain_mine, inner
    )

    def to_owners(near, far):
        both = (near.astype(F32) + swap(far).astype(F32)).astype(BF16)
        return ring_sum([both[i] for i in range(4)])

    out_sum = to_owners(out_near, out_far)
    output = (x_mine.astype(F32) + out_sum).astype(BF16)

    wo_keep = lax.dynamic_slice_in_dim(g_wo, c * half, half, 1)
    wo_send = swap(lax.dynamic_slice_in_dim(g_wo, (1 - c) * half, half, 1))
    g_wo = jnp.where(c == 0, jnp.stack([wo_keep, wo_send]), jnp.stack([wo_send, wo_keep]))
    g_wo = g_wo.reshape(4, 4, part, 2, half // 2).transpose(1, 0, 3, 2, 4).reshape(16, rows_in, half // 2)
    g_b = jnp.concatenate([g_gate.reshape(16, rows_in, mine), g_wo], 2)
    sum_b = jnp.sum(lax.all_to_all(g_b, ("y", "x"), 0, 0).astype(F32), 0)

    d_proj, g_conv, g_head, g_skip = ssd_bwd(core, proj, aux, seg_rows, par, hp, after(d_y, g_b), s_in, **sizes_k)
    d_proj, sum_b = lax.optimization_barrier((d_proj, sum_b))
    flat = 8 * length
    g_a = dot(normed.reshape(flat, model), d_proj.reshape(flat, -1), ((0,), (0,))).astype(BF16)
    sum_a = jnp.sum(lax.all_to_all(g_a.reshape(16, rows_in, -1), ("y", "x"), 0, 0).astype(F32), 0)
    d_proj = after(d_proj, g_a, output)
    d_far = back_dot(d_proj, w_a, d_gate, w_g, 1)
    d_near = back_dot(after(d_proj, d_far), w_a, d_gate, w_g, 0)
    d_normed = to_owners(d_near, d_far)

    x_f = x_mine.astype(F32)
    inverse = lax.rsqrt(jnp.mean(x_f * x_f, -1, keepdims=True) + EPS)
    scaled = x_f * inverse
    d_hat = d_normed * norm_f[None]
    d_x = inverse * (d_hat - scaled * jnp.mean(d_hat * scaled, -1, keepdims=True))
    input_grad = (cotangent[0].astype(F32) + d_x).astype(BF16)

    g_conv, g_head, g_skip = after((g_conv, g_head, g_skip), d_near)
    g_conv_full = lax.dynamic_update_slice(jnp.zeros((5, xwidth), F32), g_conv[:5, :mine], (0, member * mine))
    g_conv_full = g_conv_full.at[:, inner:].set(g_conv[:5, mine:])
    g_heads = jnp.stack([g_head[0, :my_heads], g_head[1, :my_heads], g_skip[0].reshape(my_heads, head).sum(1)])
    g_heads = lax.dynamic_update_slice(jnp.zeros((3, heads), F32), g_heads, (0, member * my_heads))
    g_gain_full = lax.dynamic_update_slice(jnp.zeros((inner,), F32), g_gain[0], (member * mine,))
    vec = jnp.concatenate(
        [
            g_conv_full.reshape(5, 16, -1).transpose(1, 0, 2).reshape(16, -1),
            g_heads.reshape(3, 16, -1).transpose(1, 0, 2).reshape(16, -1),
            g_gain_full.reshape(16, -1),
        ],
        1,
    )
    count = vec.shape[1]
    vec = jnp.pad(vec, ((0, 0), (0, -count % 128))).reshape(16, -1, 128)
    vec = jnp.sum(lax.all_to_all(vec, ("y", "x"), 0, 0), 0)
    vec = vec + swap(vec)
    vec = vec + pull(vec, "z", 2)
    vec = (vec + pull(vec, "z", 1)).reshape(-1)
    conv_w_grad = vec[: 4 * k].reshape(4, k)
    conv_b_grad = vec[4 * k : 5 * k]
    h0 = 5 * k
    dt_bias_grad, a_log_grad, d_skip_grad = (vec[h0 + i * hn : h0 + (i + 1) * hn] for i in range(3))
    out_gain_grad = vec[h0 + 3 * hn : h0 + 3 * hn + out_gain.shape[0]]

    def to_holders(a):
        near = jnp.stack([a] + [pull(a, "z", d) for d in (1, 2, 3)])
        far = swap(near)
        both = jnp.where(c == 0, jnp.stack([near, far], 1), jnp.stack([far, near], 1))
        return jnp.roll(both, z, 0)

    last_b = to_holders(jnp.concatenate([sum_b[:, :mine].astype(BF16), transpose_zy(sum_b[:, mine:].astype(BF16))], 1))
    last_a = to_holders(sum_a.astype(BF16)).reshape(8, rows_in, -1)

    def columns(a, lo, hi):
        return a[:, :, lo:hi].astype(F32).transpose(1, 0, 2).reshape(rows_in, -1)

    bc0 = mine + 2 * nst
    w_in_grad = jnp.concatenate(
        [
            columns(last_b.reshape(8, rows_in, -1), 0, mine),
            columns(last_a, 0, mine),
            jnp.sum(last_a[:, :, mine:bc0].astype(F32), 0),
            columns(last_a, bc0, bc0 + my_heads),
        ],
        1,
    )
    w_out_grad = (
        last_b[..., mine:].astype(F32).reshape(4, 2, 2, part, half // 2).transpose(0, 3, 1, 2, 4).reshape(w_out.shape)
    )
    norm_gain_grad = jnp.sum(w_in_grad * w_in.astype(F32), 1) / norm_gain.astype(F32)
    return (
        output[None],
        input_grad[None],
        norm_gain_grad,
        w_in_grad,
        conv_w_grad,
        conv_b_grad,
        dt_bias_grad,
        a_log_grad,
        d_skip_grad,
        out_gain_grad,
        w_out_grad,
    )


def solution(mesh):
    cube = Mesh(mesh.devices.reshape(4, 4, 4, 2), AXES)
    rows, shard = P(("z", "y", "x"), "c", None), ("y", "x")
    return jax.shard_map(
        local,
        mesh=cube,
        in_specs=(
            rows,
            P(("z", "y", "x"), None),
            P(shard),
            P(shard, None),
            P(None, shard),
            P(shard),
            P(shard),
            P(shard),
            P(shard),
            P(shard),
            P(shard, None),
            rows,
        ),
        out_specs=(
            rows,
            rows,
            P(shard),
            P(shard, None),
            P(None, shard),
            P(shard),
            P(shard),
            P(shard),
            P(shard),
            P(shard),
            P(shard, None),
        ),
        check_vma=False,
    )
```

```python
import functools
import jax
import jax.numpy as jnp
from jax import lax
from jax.experimental import pallas as pl
from jax.experimental.pallas import tpu as pltpu
from jax.sharding import Mesh, PartitionSpec as P

F32 = jnp.float32
BF16 = jnp.bfloat16
Q = 128
CHUNKS = 4
NEG = -1e30


def mm(a, b, dims=((1,), (0,))):
    return lax.dot_general(a.astype(BF16), b.astype(BF16), (dims, ((), ())), preferred_element_type=F32)


def halves(a):
    top = a.astype(BF16)
    return top, (a - top.astype(F32)).astype(BF16)


def mm3(a, b, dims=((1,), (0,))):
    a_top, a_low = halves(a)
    b_top, b_low = halves(b)
    return mm(a_top, b_top, dims) + (mm(a_low, b_top, dims) + mm(a_top, b_low, dims))


def mm_fold(a, b):
    top, low = halves(a)
    return mm(top, b) + mm(low, b)


def mm_tri(tri, b):
    return mm(jnp.concatenate([tri, tri], 1), jnp.concatenate(halves(b), 0))


def iota(shape, axis):
    return lax.broadcasted_iota(jnp.int32, shape, axis)


def gather_mat(width, cols, head):
    return (iota((width, cols), 0) // head == iota((width, cols), 1)).astype(BF16)


def conv_of(ch, ext, aux, par, width):
    conv = ch * par[3:4, :width] + par[4:5, :width]
    shifted = []
    for s in range(1, 4):
        sh = pltpu.roll(ext, s, 0)[8:] * aux[:, s : s + 1]
        shifted.append(sh)
        conv = conv + par[3 - s : 4 - s, :width] * sh
    return conv, shifted


def softplus(v):
    return jnp.maximum(v, 0.0) + jnp.log1p(jnp.exp(-jnp.abs(v)))


def rates(raw, hp):
    pre = raw + hp[0:1]
    dt = softplus(pre)
    tri = (iota((Q, Q), 0) >= iota((Q, Q), 1)).astype(BF16)
    return pre, dt, mm_tri(tri, -hp[1:2] * dt)


def widen(cum, dt, aux, heads, low):
    squares = [jnp.broadcast_to(cum[:, h : h + 1], (Q, Q)) for h in range(heads)]
    pairs = range(0, heads, 2)
    cum_w = jnp.concatenate([jnp.where(low, squares[h], squares[h + 1]) for h in pairs], 1)
    dt_w = jnp.concatenate([jnp.where(low, dt[:, h : h + 1], dt[:, h + 1 : h + 2]) for h in pairs], 1)
    fin_w = cum_w[Q - 1 : Q]
    enter_w = jnp.exp(cum_w) * aux[:, 4:5]
    leave_w = jnp.exp(fin_w - cum_w) * aux[:, 5:6]
    through_w = jnp.exp(fin_w) * aux[0:1, 6:7]
    return squares, dt_w, enter_w, leave_w, through_w


def ssd_fwd_kernel(c_ref, p_ref, aux_ref, seg_ref, par_ref, hp_ref, y_ref, sin_ref, rim, state, *, inner, nst, head):
    width = inner + 2 * nst
    state[...] = jnp.zeros_like(state)
    rim[...] = jnp.zeros_like(rim)
    par = par_ref[...]
    hp = hp_ref[...]
    core = c_ref[0]
    lax.fori_loop(0, CHUNKS, lambda t, _: ssd_fwd_chunk(t, core, p_ref, aux_ref, seg_ref, par, hp, y_ref, sin_ref, rim, state, inner, nst, head), None)


def place_of(t, core):
    return lax.rem(lax.div(t, 2) + core, 2), pl.ds(pl.multiple_of(lax.rem(t, 2) * Q, Q), Q)


def ssd_fwd_chunk(t, core, p_ref, aux_ref, seg_ref, par, hp, y_ref, sin_ref, rim, state, inner, nst, head):
    width = inner + 2 * nst
    side, rows = place_of(t, core)
    aux = aux_ref[pl.ds(pl.multiple_of(t * Q, Q), Q), :]
    ch = p_ref[side, 0, rows, :width]
    conv, _ = conv_of(ch, jnp.concatenate([rim[...], ch], 0), aux, par, width)
    rim[...] = ch[Q - 8 :]
    act = conv / (1.0 + jnp.exp(-conv))
    x_in, bm, cm = act[:, :inner], act[:, inner : inner + nst], act[:, inner + nst :]
    pre, dt, cum = rates(p_ref[side, 0, rows, width:], hp)
    low = iota((Q, 2 * head), 1) < head
    squares, dt_w, enter_w, leave_w, through_w = widen(cum, dt, aux, inner // head, low)
    xdt = x_in * dt_w
    scores = mm3(cm, bm, ((1,), (1,)))
    allowed = (iota((Q, Q), 0) >= iota((Q, Q), 1)) & (aux[:, 0:1] == seg_ref[t, 0:1, :])
    cum_t = cum.T
    s_old = state[...]
    sin_ref[t] = s_old
    result = enter_w * mm(cm, s_old) + par[6:7, :inner] * x_in
    for pair in range(inner // (2 * head)):
        cols = slice(2 * head * pair, 2 * head * (pair + 1))
        xp = xdt[:, cols].astype(BF16)
        none = jnp.zeros_like(xp)
        mixing = []
        for h in (2 * pair, 2 * pair + 1):
            decay = jnp.exp(jnp.where(allowed, squares[h] - cum_t[h : h + 1, :], NEG))
            mixing.append((scores * decay).astype(BF16))
        by_head = jnp.concatenate([jnp.where(low, xp, none), jnp.where(low, none, xp)], 0)
        y_ref[side, 0, rows, cols] = result[:, cols] + mm(jnp.concatenate(mixing, 1), by_head)
    state[...] = through_w * s_old + mm(bm, xdt * leave_w, ((0,), (0,)))


def ssd_bwd_kernel(c_ref, p_ref, aux_ref, seg_ref, par_ref, hp_ref, dy_ref, sin_ref, *refs, inner, nst, head):
    starts_given = len(refs) > 6
    starts = refs[1:4] if starts_given else (None,) * 3
    dp_ref, gconv_ref, ghead_ref, gskip_ref, rim, state = refs[-6:]
    core = c_ref[0]
    state[...] = jnp.zeros_like(state)
    rim[...] = jnp.zeros_like(rim)

    @pl.when(pl.program_id(0) == 0)
    def _():
        for ref, start in zip((gconv_ref, ghead_ref, gskip_ref), starts):
            ref[...] = start[...] if starts_given else jnp.zeros_like(ref)

    par = par_ref[...]
    hp = hp_ref[...]
    lax.fori_loop(
        0,
        CHUNKS,
        lambda t, _: ssd_bwd_chunk(
            CHUNKS - 1 - t, core, p_ref, aux_ref, seg_ref, par, hp, dy_ref, sin_ref, dp_ref, gconv_ref, ghead_ref, gskip_ref, rim, state, inner, nst, head
        ),
        None,
    )


def ssd_bwd_chunk(
    t, core, p_ref, aux_ref, seg_ref, par, hp, dy_ref, sin_ref, dp_ref, gconv_ref, ghead_ref, gskip_ref, rim, state, inner, nst, head
):
    width = inner + 2 * nst
    side, rows = place_of(t, core)
    aux = aux_ref[pl.ds(pl.multiple_of(t * Q, Q), Q), :]
    ch = p_ref[side, 0, rows, :width]
    prior = jnp.maximum(t - 1, 0)
    prev = p_ref[lax.rem(lax.div(prior, 2) + core, 2), 0, pl.ds(pl.multiple_of(lax.rem(prior, 2) * Q + Q - 8, 8), 8), :width]
    prev = prev * jnp.where(t == 0, 0.0, 1.0)
    conv, shifted = conv_of(ch, jnp.concatenate([prev, ch], 0), aux, par, width)
    sig = 1.0 / (1.0 + jnp.exp(-conv))
    act = conv * sig
    x_in, bm, cm = act[:, :inner], act[:, inner : inner + nst], act[:, inner + nst :]
    pre, dt, cum = rates(p_ref[side, 0, rows, width:], hp)
    low = iota((Q, 2 * head), 1) < head
    squares, dt_w, enter_w, leave_w, through_w = widen(cum, dt, aux, inner // head, low)
    xdt = x_in * dt_w
    scores = mm3(cm, bm, ((1,), (1,)))
    allowed = (iota((Q, Q), 0) >= iota((Q, Q), 1)) & (aux[:, 0:1] == seg_ref[t, 0:1, :])
    cum_t = cum.T
    bm = bm.astype(BF16)
    cm = cm.astype(BF16)
    dy = dy_ref[side, 0, rows, :]
    s_in = sin_ref[t]
    d_state = state[...]
    s_in_b = s_in.astype(BF16)
    d_state_b = d_state.astype(BF16)

    dye = (dy * enter_w).astype(BF16)
    inter = mm(cm, s_in_b) * enter_w
    from_state = mm(bm, d_state_b) * leave_w
    state[...] = mm(cm, dye, ((0,), (0,))) + through_w * d_state
    d_c = mm(dye, s_in_b, ((1,), (1,)))
    d_b = mm(xdt * leave_w, d_state_b, ((1,), (1,)))

    lane = iota((Q, Q), 1)
    sub = iota((8, Q), 0)
    d_scores = jnp.zeros((Q, Q), F32)
    row_sums = jnp.zeros((Q, Q), F32)
    col_sums = jnp.zeros((8, Q), F32)
    d_xdt = []
    for pair in range(inner // (2 * head)):
        cols = slice(2 * head * pair, 2 * head * (pair + 1))
        xp = xdt[:, cols]
        dyp = dy[:, cols]
        d_k2 = mm3(dyp, jnp.concatenate([jnp.where(low, xp, 0.0), jnp.where(low, 0.0, xp)], 0), ((1,), (1,)))
        kmats = []
        for k in range(2):
            h = 2 * pair + k
            decay = jnp.exp(jnp.where(allowed, squares[h] - cum_t[h : h + 1, :], NEG))
            d_k = d_k2[:, k * Q : (k + 1) * Q]
            kmat = scores * decay
            d_scores = d_scores + d_k * decay
            both = d_k * kmat
            row_sums = jnp.where(lane == h, jnp.sum(both, 1, keepdims=True), row_sums)
            col_sums = jnp.where(sub == h, jnp.sum(both, 0, keepdims=True), col_sums)
            kmats.append(kmat)
        dy_by_head = jnp.concatenate([jnp.where(low, dyp, 0.0), jnp.where(low, 0.0, dyp)], 0)
        d_xdt.append(mm3(jnp.concatenate(kmats, 0), dy_by_head, ((0,), (0,))))
    z = jnp.concatenate(d_xdt, 1) + from_state
    d_c = d_c + mm(d_scores, bm)
    d_b = d_b + mm(d_scores, cm, ((0,), (0,)))
    d_x = z * dt_w + par[6:7, :inner] * dy

    leaving = xdt * from_state
    ending = jnp.sum(s_in * d_state, 0, keepdims=True) * through_w + jnp.sum(leaving, 0, keepdims=True)
    folded = mm_fold(
        jnp.concatenate([x_in * z, dy * inter - leaving, jnp.broadcast_to(ending, (8, inner))], 0), gather_mat(inner, Q, head)
    )
    col_full = jnp.concatenate([col_sums, jnp.zeros((Q - 8, Q), F32)], 0).T
    d_cum = row_sums - col_full + folded[Q : 2 * Q]
    tri_up = (iota((Q, Q), 0) <= iota((Q, Q), 1)).astype(BF16)
    rev = mm_tri(tri_up, d_cum) + folded[2 * Q : 2 * Q + 1]
    d_dt = folded[:Q] - hp[1:2] * rev
    d_raw = d_dt / (1.0 + jnp.exp(-pre))
    live = (iota((1, Q), 1) < inner // head).astype(F32)
    d_raw = d_raw * live
    ghead_ref[0:1, :] += jnp.sum(d_raw, 0, keepdims=True)
    ghead_ref[1:2, :] += jnp.sum(rev * dt, 0, keepdims=True) * -hp[1:2]
    gskip_ref[0:1, :] += jnp.sum(dy * x_in, 0, keepdims=True)

    d_act = jnp.concatenate([d_x, d_b, d_c], 1)
    d_conv = d_act * (sig * (1.0 + conv * (1.0 - sig)))
    gconv_ref[4:5, :] += jnp.sum(d_conv, 0, keepdims=True)
    gconv_ref[3:4, :] += jnp.sum(d_conv * ch, 0, keepdims=True)
    d_ch = d_conv * par[3:4, :width]
    for s in range(1, 4):
        gconv_ref[3 - s : 4 - s, :] += jnp.sum(d_conv * shifted[s - 1], 0, keepdims=True)
        u = d_conv * aux[:, s : s + 1] * par[3 - s : 4 - s, :width]
        d_ch = d_ch + pltpu.roll(jnp.concatenate([u, rim[s - 1]], 0), Q + 8 - s, 0)[:Q]
        rim[s - 1] = u[:8]
    dp_ref[side, 0, rows, :width] = d_ch.astype(BF16)
    dp_ref[side, 0, rows, width:] = d_raw.astype(BF16)


def rows_spec(cols, first=0):
    return pl.BlockSpec((2, 1, CHUNKS * Q // 2, cols), lambda r, c: (0, r + first, 0, 0))


def common_specs(wide, width, first=0):
    return [
        rows_spec(wide, first),
        pl.BlockSpec((CHUNKS * Q, 128), lambda r, c: (r + first, 0)),
        pl.BlockSpec((CHUNKS, 8, Q), lambda r, c: (r + first, 0, 0)),
        pl.BlockSpec((8, width), lambda r, c: (0, 0)),
        pl.BlockSpec((8, 128), lambda r, c: (0, 0)),
    ]


def ssd_fwd(core, proj, aux, seg_rows, par, hp, *, inner, nst, head, interpret=False):
    seqs, half, wide = proj.shape[1:]
    rows = 2 * seqs * half
    width = inner + 2 * nst
    spec = pltpu.PrefetchScalarGridSpec(
        num_scalar_prefetch=1,
        grid=(seqs,),
        in_specs=common_specs(wide, width),
        out_specs=[rows_spec(inner), pl.BlockSpec((CHUNKS, nst, inner), lambda r, c: (r, 0, 0))],
        scratch_shapes=[pltpu.VMEM((8, width), F32), pltpu.VMEM((nst, inner), F32)],
    )
    y, s_in = pl.pallas_call(
        functools.partial(ssd_fwd_kernel, inner=inner, nst=nst, head=head),
        grid_spec=spec,
        out_shape=[
            jax.ShapeDtypeStruct((2, seqs, CHUNKS * Q // 2, inner), F32),
            jax.ShapeDtypeStruct((seqs * CHUNKS, nst, inner), F32),
        ],
        cost_estimate=pl.CostEstimate(flops=1, transcendentals=0, bytes_accessed=1),
        interpret=interpret,
        name="ssd_fwd",
    )(core, proj, aux, seg_rows, par, hp)
    return y, s_in


def ssd_bwd(core, proj, aux, seg_rows, par, hp, dy, s_in, first, count, so_far, *, inner, nst, head, interpret=False):
    seqs, half, wide = proj.shape[1:]
    rows = 2 * seqs * half
    width = inner + 2 * nst
    out_specs = [
        rows_spec(wide, first),
        pl.BlockSpec((8, width), lambda r, c: (0, 0)),
        pl.BlockSpec((8, 128), lambda r, c: (0, 0)),
        pl.BlockSpec((8, inner), lambda r, c: (0, 0)),
    ]
    in_specs = common_specs(wide, width, first) + [
        rows_spec(inner, first),
        pl.BlockSpec((CHUNKS, nst, inner), lambda r, c: (r + first, 0, 0)),
    ]
    operands = (core, proj, aux, seg_rows, par, hp, dy, s_in)
    aliases = {}
    if so_far is not None:
        aliases = {len(operands) + i: i for i in range(4)}
        in_specs += [pl.BlockSpec(memory_space=pl.ANY)] + out_specs[1:]
        operands += tuple(so_far)
    spec = pltpu.PrefetchScalarGridSpec(
        num_scalar_prefetch=1,
        grid=(count,),
        in_specs=in_specs,
        out_specs=out_specs,
        scratch_shapes=[pltpu.VMEM((3, 8, width), F32), pltpu.VMEM((nst, inner), F32)],
    )
    return pl.pallas_call(
        functools.partial(ssd_bwd_kernel, inner=inner, nst=nst, head=head),
        grid_spec=spec,
        out_shape=[
            jax.ShapeDtypeStruct((2, seqs, CHUNKS * Q // 2, wide), BF16),
            jax.ShapeDtypeStruct((8, width), F32),
            jax.ShapeDtypeStruct((8, 128), F32),
            jax.ShapeDtypeStruct((8, inner), F32),
        ],
        input_output_aliases=aliases,
        cost_estimate=pl.CostEstimate(flops=1, transcendentals=0, bytes_accessed=1),
        interpret=interpret,
        name="ssd_bwd",
    )(*operands)


def masks_of(seg):
    s_count, length = seg.shape
    cols = [seg.astype(F32)]
    for s in range(1, 4):
        back = jnp.concatenate([jnp.full((s_count, s), -1, seg.dtype), seg[:, :-s]], 1)
        cols.append((back == seg).astype(F32))
    by_chunk = seg.reshape(s_count, length // Q, Q)
    last = by_chunk[:, :, -1:]
    prev = jnp.concatenate([jnp.full((s_count, 1, 1), -1, seg.dtype), last[:, :-1]], 1)
    cols.append((by_chunk == prev).astype(F32).reshape(s_count, length))
    cols.append((by_chunk == last).astype(F32).reshape(s_count, length))
    cols.append(jnp.broadcast_to(prev == last, by_chunk.shape).astype(F32).reshape(s_count, length))
    aux = jnp.stack(cols, -1).reshape(s_count * length, len(cols))
    aux = jnp.pad(aux, ((0, 0), (0, 128 - len(cols))))
    rows = jnp.broadcast_to(seg.astype(F32).reshape(-1, 1, Q), (s_count * length // Q, 8, Q))
    return aux, rows


EPS = 1e-05
AXES = ("z", "y", "x", "c")


def pull(a, axis, d):
    return lax.ppermute(a, axis, [((i + d) % 4, i) for i in range(4)])


def swap(a):
    return lax.ppermute(a, "c", [(0, 1), (1, 0)])


def transpose_zy(a):
    return lax.ppermute(a, ("z", "y"), [(4 * y + z, 4 * z + y) for z in range(4) for y in range(4)])


def ring(a):
    return tuple(pull(a, "z", d) for d in (1, 2, 3))


def ring_ends(a):
    return pull(a, "z", 1), pull(a, "z", 3)


def ring_middle(one, three):
    half = one.shape[0] // 2
    return pull(one[:half], "z", 1), pull(three[half:], "z", 3)


def ring_back(q):
    return tuple(pull(q[d], "z", 4 - d) for d in (1, 2, 3))


def plane_all(a):
    return lax.all_gather(a, ("y", "x"), axis=0)


def line_all(a, axis, at):
    return jnp.roll(jnp.stack([a] + [pull(a, axis, d) for d in (1, 2, 3)]), at, 0)


def tie(*values):
    return lax.optimization_barrier(values)


def two_terms(a):
    top = lax.reduce_precision(a, 8, 7)
    return top.astype(BF16), (a - top).astype(BF16)


def after(value, *others):
    return lax.optimization_barrier((value,) + others)[0]


def cost(flops, bytes_accessed):
    return pl.CostEstimate(flops=1, transcendentals=0, bytes_accessed=1)


def whole(shape):
    return pl.BlockSpec(shape, lambda *_: (0,) * len(shape))


PER = 2


def near_spec(rows, cols):
    return pl.BlockSpec((PER, rows, cols), lambda h, r: (jnp.where(h == 0, r, 4 // PER - 1), 0, 0))


def far_spec(rows, cols):
    return pl.BlockSpec((PER, rows, cols), lambda h, r: (jnp.where(h == 0, 0, r), 0, 0))


def block_spec(cols, rows=256):
    return pl.BlockSpec((1, PER, rows, cols), lambda h, r: (h, r, 0, 0))


def flat_rows(ref):
    v = ref[0] if len(ref.shape) == 4 else ref[...]
    return v.reshape(v.shape[0] * v.shape[1], v.shape[2])


def put_rows(ref, v):
    if len(ref.shape) == 4:
        ref[0] = v.reshape(ref.shape[1:])
    else:
        ref[...] = v.reshape(ref.shape)


def half_cols(core, width):
    return pl.ds(pl.multiple_of(core * width, width), width), pl.ds(pl.multiple_of((1 - core) * width, width), width)


def enter_kernel(near_ref, far_ref, gain_ref, w_ref, normed_ref, proj_ref):
    def step(ref):
        p = flat_rows(ref).astype(F32)
        inverse = lax.rsqrt(jnp.mean(p * p, -1, keepdims=True) + EPS)
        normed = (p * inverse * gain_ref[...]).astype(BF16)
        put_rows(normed_ref, normed)
        put_rows(proj_ref, jnp.dot(normed, w_ref[...], preferred_element_type=F32))

    pl.when(pl.program_id(0) == 0)(lambda: step(near_ref))
    pl.when(pl.program_id(0) == 1)(lambda: step(far_ref))


def enter(near, far, gain, w):
    padded, model = near.shape[1:]
    rows, cols = 256, w.shape[1]
    return pl.pallas_call(
        enter_kernel,
        grid=(2, 4 // PER),
        out_shape=[jax.ShapeDtypeStruct((2, 4, rows, model), BF16), jax.ShapeDtypeStruct((2, 4, rows, cols), F32)],
        in_specs=[near_spec(padded, model), far_spec(padded, model), whole((1, model)), whole(w.shape)],
        out_specs=[block_spec(model), block_spec(cols)],
        cost_estimate=cost(16 * rows * model * cols, 8 * rows * (4 * model + 4 * cols)),
        name="enter",
    )(near, far, gain, w)


def gate_kernel(core_ref, normed_ref, near_ref, far_ref, wg_ref, wo_ref, wt_ref, y_ref, gain_ref, gate_ref, dm_ref, sums_ref):
    gate = jnp.dot(flat_rows(normed_ref), wg_ref[...], preferred_element_type=F32)
    here, there = half_cols(core_ref[0], wo_ref.shape[1])
    dims = (((1,), (1,)), ((), ()))

    def back(cot_ref):
        rows = gate.shape[0]
        a = cot_ref[:, :, here].reshape(rows, wo_ref.shape[1])
        b = cot_ref[:, :, there].reshape(rows, wo_ref.shape[1])
        put_rows(
            dm_ref,
            lax.dot_general(a, wo_ref[...], dims, preferred_element_type=F32)
            + lax.dot_general(b, wt_ref[...], dims, preferred_element_type=F32),
        )

    pl.when(pl.program_id(0) == 0)(lambda: back(near_ref))
    pl.when(pl.program_id(0) == 1)(lambda: back(far_ref))
    d_mixed = flat_rows(dm_ref)
    put_rows(gate_ref, gate)
    gated = flat_rows(y_ref) * gate / (1.0 + jnp.exp(-gate))
    ones = jnp.ones((8, gate.shape[1]), BF16)

    def total(v):
        top, low = halves(v)
        return (mm(ones, top, ((1,), (1,))) + mm(ones, low, ((1,), (1,))))[:1]

    both = jnp.concatenate([total(gated * gated), total(d_mixed * gain_ref[...] * gated)], 0)
    rows = sums_ref.shape[3]
    for q in range(PER):
        sums_ref[0, q] = both[:, q * rows : (q + 1) * rows]


def gate_stage(core, normed, near, far, w_g, w_o, w_t, y, gain):
    rows, model = normed.shape[2:]
    mine = w_g.shape[1]
    return pl.pallas_call(
        gate_kernel,
        grid=(2, 4 // PER),
        out_shape=[jax.ShapeDtypeStruct((2, 4, rows, mine), F32)] * 2 + [jax.ShapeDtypeStruct((2, 4, 2, rows), F32)],
        in_specs=[
            pl.BlockSpec(memory_space=pltpu.SMEM),
            block_spec(model),
            near_spec(rows, model),
            far_spec(rows, model),
            whole(w_g.shape),
            whole(w_o.shape),
            whole(w_t.shape),
            block_spec(mine),
            whole((1, mine)),
        ],
        out_specs=[block_spec(mine), block_spec(mine), block_spec(rows, 2)],
        cost_estimate=cost(32 * rows * model * mine, 8 * rows * (4 * model + 12 * mine)),
        name="gate_stage",
    )(core, normed, near, far, w_g, w_o, w_t, y, gain)


def turn_kernel(
    core_ref, normed_ref, near_ref, far_ref, wo_ref, wt_ref, y_ref, gate_ref, dm_ref, sums_ref, gain_ref,
    out_near_ref, out_far_ref, dy_ref, dgate_ref, keep_ref, send_ref, ggate_ref, ggain_ref, acc_o, acc_g, *, inner,
):
    h, r = pl.program_id(0), pl.program_id(1)
    rows = gate_ref.shape[2]
    gate, d_mixed, y, gain = flat_rows(gate_ref), flat_rows(dm_ref), flat_rows(y_ref), gain_ref[...]
    sums = jnp.concatenate(
        [jnp.concatenate([sums_ref[0, q], jnp.zeros((6, rows), F32)], 0).T for q in range(PER)], 0
    )
    scale = lax.rsqrt(sums[:, 0:1] / inner + EPS)
    lean = sums[:, 1:2] / inner * scale * scale
    sig = 1.0 / (1.0 + jnp.exp(-gate))
    act = gate * sig
    gated = y * act
    mixed = (gated * scale * gain).astype(BF16)
    d_gated = scale * (d_mixed * gain - gated * lean)
    put_rows(dy_ref, d_gated * act)
    d_gate = (d_gated * y * (sig * (1.0 + gate * (1.0 - sig)))).astype(BF16)
    put_rows(dgate_ref, d_gate)
    here, there = half_cols(core_ref[0], wo_ref.shape[1])

    def forward(out_ref, cot_ref):
        shape = out_ref.shape[:2] + (wo_ref.shape[1],)
        out_ref[:, :, here] = jnp.dot(mixed, wo_ref[...], preferred_element_type=F32).astype(BF16).reshape(shape)
        out_ref[:, :, there] = jnp.dot(mixed, wt_ref[...], preferred_element_type=F32).astype(BF16).reshape(shape)
        acc_o[...] += lax.dot_general(mixed, flat_rows(cot_ref), (((0,), (0,)), ((), ())), preferred_element_type=F32)

    @pl.when((h == 0) & (r == 0))
    def _():
        acc_o[...] = jnp.zeros_like(acc_o)
        acc_g[...] = jnp.zeros_like(acc_g)
        ggain_ref[...] = jnp.zeros_like(ggain_ref)

    ggain_ref[0:1, :] += jnp.sum(d_mixed * gated * scale, 0, keepdims=True)
    pl.when(h == 0)(lambda: forward(out_near_ref, near_ref))
    pl.when(h == 1)(lambda: forward(out_far_ref, far_ref))
    acc_g[...] += lax.dot_general(flat_rows(normed_ref), d_gate, (((0,), (0,)), ((), ())), preferred_element_type=F32)

    @pl.when((h == 1) & (r == pl.num_programs(1) - 1))
    def _():
        keep_ref[...] = acc_o[:, here].astype(BF16)
        send_ref[...] = acc_o[:, there].astype(BF16)
        ggate_ref[...] = acc_g[...].astype(BF16)


def turn_stage(core, normed, near, far, w_o, w_t, y, gate, d_mixed, sums, gain, inner):
    rows, model = normed.shape[2:]
    mine = w_o.shape[0]
    return pl.pallas_call(
        functools.partial(turn_kernel, inner=inner),
        grid=(2, 4 // PER),
        out_shape=[
            jax.ShapeDtypeStruct((4, rows, model), BF16),
            jax.ShapeDtypeStruct((4, rows, model), BF16),
            jax.ShapeDtypeStruct((2, 4, rows, mine), F32),
            jax.ShapeDtypeStruct((2, 4, rows, mine), BF16),
            jax.ShapeDtypeStruct(w_o.shape, BF16),
            jax.ShapeDtypeStruct(w_o.shape, BF16),
            jax.ShapeDtypeStruct((model, mine), BF16),
            jax.ShapeDtypeStruct((8, mine), F32),
        ],
        in_specs=[
            pl.BlockSpec(memory_space=pltpu.SMEM),
            block_spec(model),
            near_spec(rows, model),
            far_spec(rows, model),
            whole(w_o.shape),
            whole(w_o.shape),
            block_spec(mine),
            block_spec(mine),
            block_spec(mine),
            block_spec(rows, 2),
            whole((1, mine)),
        ],
        out_specs=[
            near_spec(rows, model),
            far_spec(rows, model),
            block_spec(mine),
            block_spec(mine),
            whole(w_o.shape),
            whole(w_o.shape),
            whole((model, mine)),
            whole((8, mine)),
        ],
        scratch_shapes=[pltpu.VMEM((mine, model), F32), pltpu.VMEM((model, mine), F32)],
        cost_estimate=cost(48 * rows * model * mine, 8 * rows * (6 * model + 18 * mine)),
        name="turn_stage",
    )(core, normed, near, far, w_o, w_t, y, gate, d_mixed, sums, gain)


def back_kernel(dp_ref, wa_ref, dg_ref, wg_ref, out_ref):
    t = lax.dot_general(dp_ref[0, 0], wa_ref[...], (((1,), (1,)), ((), ())), preferred_element_type=F32)
    t = t + lax.dot_general(dg_ref[0, 0], wg_ref[...], (((1,), (1,)), ((), ())), preferred_element_type=F32)
    out_ref[0] = t.astype(BF16)


def back_dot(d_proj, w_a, d_gate, w_g, side):
    rows, ka = d_proj.shape[2:]
    m, kg = w_g.shape
    return pl.pallas_call(
        back_kernel,
        grid=(4,),
        out_shape=jax.ShapeDtypeStruct((4, rows, m), BF16),
        in_specs=[
            pl.BlockSpec((1, 1, rows, ka), lambda r: (side, r, 0, 0)),
            whole((m, ka)),
            pl.BlockSpec((1, 1, rows, kg), lambda r: (side, r, 0, 0)),
            whole((m, kg)),
        ],
        out_specs=pl.BlockSpec((1, rows, m), lambda r: (r, 0, 0)),
        cost_estimate=cost(8 * rows * m * (ka + kg), 2 * (4 * rows + m) * (ka + kg) + 8 * rows * m),
        name="back_dot",
    )(d_proj, w_a, d_gate, w_g)


def unpack_kernel(core_ref, all_ref, wg_ref, mine_ref, send_ref):
    rows, width = all_ref.shape[1:]
    part, cols = rows // 2, wg_ref.shape[1]
    for k in range(16):
        wg_ref[k * rows : (k + 1) * rows, :] = all_ref[k, :, :cols]

    def move(ref, side):
        for x in (2 * side, 2 * side + 1):
            for y in range(4):
                at = (4 * (x % 2) + y) * part
                for k in range(2):
                    piece = all_ref[4 * y + x, k * part : (k + 1) * part, cols:]
                    ref[at : at + part, k * (width - cols) : (k + 1) * (width - cols)] = piece

    for core in range(2):

        @pl.when(core_ref[0] == core)
        def _():
            move(mine_ref, core)
            move(send_ref, 1 - core)


def unpack(core, gathered, cols):
    _, rows, width = gathered.shape
    half = jax.ShapeDtypeStruct((4 * rows, 2 * (width - cols)), BF16)
    return pl.pallas_call(
        unpack_kernel,
        in_specs=[pl.BlockSpec(memory_space=pltpu.SMEM), whole(gathered.shape)],
        out_specs=[whole((16 * rows, cols)), whole(half.shape), whole(half.shape)],
        grid=(1,),
        out_shape=[jax.ShapeDtypeStruct((16 * rows, cols), BF16), half, half],
        cost_estimate=cost(0, 0),
        name="unpack",
    )(core, gathered)


def pack_kernel(core_ref, gate_ref, keep_ref, got_ref, out_ref):
    rows, width = out_ref.shape[1:]
    part, cols = rows // 2, gate_ref.shape[1]
    for k in range(16):
        out_ref[k, :, :cols] = gate_ref[k * rows : (k + 1) * rows, :]

    def move(ref, side):
        for x in (2 * side, 2 * side + 1):
            for y in range(4):
                at = (4 * (x % 2) + y) * part
                for k in range(2):
                    piece = ref[at : at + part, k * (width - cols) : (k + 1) * (width - cols)]
                    out_ref[4 * y + x, k * part : (k + 1) * part, cols:] = piece

    for core in range(2):

        @pl.when(core_ref[0] == core)
        def _():
            move(keep_ref, core)
            move(got_ref, 1 - core)


def pack(core, g_gate, keep, got):
    model, cols = g_gate.shape
    rows = model // 16
    shape = (16, rows, cols + keep.shape[1] // 2)
    return pl.pallas_call(
        pack_kernel,
        in_specs=[pl.BlockSpec(memory_space=pltpu.SMEM), whole(g_gate.shape), whole(keep.shape), whole(got.shape)],
        out_specs=whole(shape),
        grid=(1,),
        out_shape=jax.ShapeDtypeStruct(shape, BF16),
        cost_estimate=cost(0, 0),
        name="pack",
    )(core, g_gate, keep, got)


def assemble_kernel(at_ref, near_ref, far_ref, win_ref, gwin_ref, gwo_ref, norm_ref, extra_ref, *, mine, nst, my_heads):
    z, core = at_ref[0], at_ref[1]
    rows, wide = win_ref.shape
    inner = 8 * mine
    part = gwo_ref.shape[0] // 4
    width = mine + 2 * nst + 128
    bc = jnp.zeros((rows, 2 * nst), F32)
    extra = jnp.zeros((near_ref.shape[1] - rows, near_ref.shape[2]), F32)
    raw = jnp.zeros((rows, 128), F32)
    lane = iota((rows, 128), 1)
    for zz in range(4):
        r = lax.rem(zz - z + 4, 4)
        for cc in range(2):
            j = 2 * zz + cc
            both = jnp.where(core == cc, near_ref[r].astype(F32), far_ref[r].astype(F32))
            extra = extra + both[rows:]
            both = both[:rows]
            a, b = both[:, :width], both[:, width:]
            gwin_ref[:, j * mine : (j + 1) * mine] = b[:, :mine]
            gwin_ref[:, inner + j * mine : inner + (j + 1) * mine] = a[:, :mine]
            bc = bc + a[:, mine : mine + 2 * nst]
            piece = a[:, mine + 2 * nst :]
            piece = jnp.where(lane < my_heads, piece, 0.0)
            raw = raw + (pltpu.roll(piece, j * my_heads, 1) if j else piece)
            for k in range(2):
                cols = (2 * cc + k) * (b.shape[1] - mine)
                gwo_ref[zz * part : (zz + 1) * part, cols : cols + b.shape[1] - mine] = b[k * part : (k + 1) * part, mine:]
    gwin_ref[:, 2 * inner : 2 * inner + 2 * nst] = bc
    gwin_ref[:, 2 * inner + 2 * nst :] = raw[:, : wide - 2 * inner - 2 * nst]
    extra_ref[...] = extra
    norm_ref[...] = jnp.sum(gwin_ref[...] * win_ref[...].astype(F32), 1, keepdims=True)


def assemble(z, core, near, far, w_in, w_out, mine, nst, my_heads):
    at = jnp.concatenate([z.astype(jnp.int32).reshape(1), core])
    arrays = (near, far, w_in)
    rows = w_in.shape[0]
    extra = (near.shape[1] - rows, near.shape[2])
    return pl.pallas_call(
        functools.partial(assemble_kernel, mine=mine, nst=nst, my_heads=my_heads),
        in_specs=[pl.BlockSpec(memory_space=pltpu.SMEM)] + [whole(a.shape) for a in arrays],
        out_specs=[whole(w_in.shape), whole(w_out.shape), whole((rows, 1)), whole(extra)],
        grid=(1,),
        out_shape=[
            jax.ShapeDtypeStruct(w_in.shape, F32),
            jax.ShapeDtypeStruct(w_out.shape, F32),
            jax.ShapeDtypeStruct((rows, 1), F32),
            jax.ShapeDtypeStruct(extra, F32),
        ],
        cost_estimate=cost(0, 0),
        name="assemble",
    )(at, *arrays)


def dot(a, b, dims):
    return lax.dot_general(a, b, (dims, ((), ())), preferred_element_type=F32)


def local(inputs, segments, norm_gain, w_in, conv_w, conv_b, dt_bias, a_log, d_skip, out_gain, w_out, cotangent):
    z, y, x, c = (lax.axis_index(name) for name in AXES)
    member = 2 * z + c
    length, model = inputs.shape[1:]
    inner = 16 * out_gain.shape[0]
    heads = 16 * d_skip.shape[0]
    xwidth = 16 * conv_b.shape[0]
    nst = (xwidth - inner) // 2
    head = inner // heads
    mine = inner // 8
    my_heads = heads // 8
    core = c.astype(jnp.int32).reshape(1)
    rows_in = w_in.shape[0]

    def lanes(a):
        return jnp.pad(a, ((0, 0), (0, -a.shape[1] % 128))).reshape(-1, 128)

    tiny = jnp.concatenate([dt_bias, a_log, d_skip])[None]
    small = jnp.concatenate([lanes(conv_w), lanes(conv_b[None]), lanes(out_gain[None]), lanes(norm_gain[None]), lanes(tiny)], 0)
    small_line = line_all(jnp.pad(small, ((0, -small.shape[0] % 16), (0, 0))), "x", x)
    small = line_all(small_line, "y", y)

    x_mine = inputs[0]
    one, three = ring_ends(x_mine)
    middle = ring_middle(one, three)
    seg_mine = segments.reshape(-1, 128)
    seg_all = jnp.stack((seg_mine,) + ring(seg_mine)).reshape(4, -1)
    aux, seg_rows = masks_of(seg_all)

    small = small.reshape(16, -1, 128).astype(F32)
    k, kn, hn = conv_b.shape[0], out_gain.shape[0], d_skip.shape[0]
    lk, lg = -(-k // 128), -(-kn // 128)
    conv_wf = small[:, : 4 * lk].reshape(16, 4, lk * 128)[:, :, :k].transpose(1, 0, 2).reshape(4, xwidth)
    conv_bf = small[:, 4 * lk : 5 * lk].reshape(16, lk * 128)[:, :k].reshape(1, xwidth)
    gain_f = small[:, 5 * lk : 5 * lk + lg].reshape(16, lg * 128)[:, :kn].reshape(-1)
    norm_f = small[:, 5 * lk + lg, :rows_in].reshape(-1)
    dtb_f, alog_f, skip_f = (small[:, 5 * lk + lg + 1, i * hn : (i + 1) * hn].reshape(-1) for i in range(3))

    def own(a, count):
        return lax.dynamic_slice_in_dim(a, member * count, count, a.ndim - 1)

    conv_all = jnp.concatenate([conv_wf, conv_bf], 0)
    conv_mine = jnp.concatenate([own(conv_all[:, :inner], mine), conv_all[:, inner:]], 1)
    skip_mine = jnp.repeat(own(skip_f, my_heads), head)
    par = jnp.concatenate(
        [conv_mine, jnp.zeros((1, mine + 2 * nst), F32), jnp.pad(skip_mine, (0, 2 * nst))[None], jnp.zeros((1, mine + 2 * nst), F32)], 0
    )
    rates_mine = jnp.stack([own(dtb_f, my_heads), jnp.exp(own(alog_f, my_heads))])
    hp = jnp.pad(rates_mine, ((0, 6), (0, 128 - my_heads)))
    gain_mine = own(gain_f, mine)[None]

    w_x = lax.dynamic_slice_in_dim(w_in, inner + member * mine, mine, 1)
    w_dt = jnp.pad(
        lax.dynamic_slice_in_dim(w_in[:, inner + xwidth :], member * my_heads, my_heads, 1), ((0, 0), (0, 128 - my_heads))
    )
    w_bc = jnp.concatenate([w_in[:, inner + mine * 8 : inner + xwidth], w_dt], 1)
    all_a = plane_all(jnp.concatenate([w_x, w_bc], 1))
    w_a = all_a.reshape(model, -1)
    w_g = lax.dynamic_slice_in_dim(w_in, member * mine, mine, 1)
    part = w_out.shape[0] // 4
    half = model // 2
    wo_piece = lax.dynamic_slice(w_out, (z * part, c * half), (part, half))
    wo_piece = transpose_zy(jnp.concatenate([wo_piece[:, : half // 2], wo_piece[:, half // 2 :]], 0))
    block_b = jnp.concatenate([w_g, wo_piece], 1)
    middle, block_b, norm_row, par, hp, gain_mine, aux, seg_rows = tie(
        middle, block_b, norm_f[None], par, hp, gain_mine, aux, seg_rows
    )
    all_b = plane_all(block_b)
    x_near = jnp.stack([x_mine, one, jnp.concatenate(middle, 0), three])
    x_far = swap(x_near)
    cot_ring = ring(after(cotangent[0], x_near))

    sizes_k = dict(inner=mine, nst=nst, head=head)
    normed, proj = enter(x_near, x_far, norm_row, w_a)
    mixed_ssd, s_in = ssd_fwd(core, proj, aux, seg_rows, par, hp, **sizes_k)
    mixed_ssd, cot_ring = tie(mixed_ssd, cot_ring)
    cot_near = jnp.stack((cotangent[0],) + cot_ring)
    cot_far = swap(cot_near)
    all_b = after(all_b, cot_near)
    w_g, w_o, w_t = unpack(core, all_b, mine)
    w_t = swap(w_t)
    gate, d_mixed, sums = gate_stage(core, normed, cot_near, cot_far, w_g, w_o, w_t, mixed_ssd, gain_mine)
    sums = sums + jnp.flip(swap(sums), 0)
    sums = sums + sum(jnp.roll(pull(sums, "z", d), d, 1) for d in (1, 2, 3))
    out_near, out_far, d_y, d_gate, wo_keep, wo_send, g_gate, g_gain = turn_stage(
        core, normed, cot_near, cot_far, w_o, w_t, mixed_ssd, gate, d_mixed, sums, gain_mine, inner
    )

    def core_sum(near, far):
        return (near.astype(F32) + swap(far).astype(F32)).astype(BF16)

    backward = functools.partial(ssd_bwd, core, proj, aux, seg_rows, par, hp, d_y, s_in, **sizes_k)
    so_far, wo_got = tie(backward(0, 1, None), swap(wo_send))
    g_b = pack(core, g_gate, wo_keep, wo_got)
    all_b = lax.all_to_all(g_b, ("y", "x"), 0, 0)
    so_far = backward(1, 1, after(so_far, g_b))
    so_far, out_both = tie(so_far, core_sum(out_near, out_far))
    out_ring = ring_back(out_both)
    d_proj, g_conv, g_head, g_skip = backward(2, 2, so_far)
    d_far = back_dot(d_proj, w_a, d_gate, w_g, 1)
    d_near = back_dot(after(d_proj, d_far), w_a, d_gate, w_g, 0)
    d_proj, d_far, d_near, all_b, out_ring = tie(d_proj, d_far, d_near, all_b, out_ring)
    flat = 8 * length
    g_a = dot(normed.reshape(flat, model), d_proj.reshape(flat, -1), ((0,), (0,))).astype(BF16)
    sum_b = jnp.sum(all_b.astype(F32), 0).astype(BF16)

    g_conv_full = lax.dynamic_update_slice(jnp.zeros((5, xwidth), F32), g_conv[:5, :mine], (0, member * mine))
    g_conv_full = lax.dynamic_update_slice(g_conv_full, g_conv[:5, mine:], (0, inner))
    g_heads = jnp.stack([g_head[0, :my_heads], g_head[1, :my_heads], g_skip[0].reshape(my_heads, head).sum(1)])
    g_heads = lax.dynamic_update_slice(jnp.zeros((3, heads), F32), g_heads, (0, member * my_heads))
    g_gain_full = lax.dynamic_update_slice(jnp.zeros((inner,), F32), g_gain[0], (member * mine,))
    vec = jnp.concatenate(
        [
            g_conv_full.reshape(5, 16, -1).transpose(1, 0, 2).reshape(16, -1),
            g_heads.reshape(3, 16, -1).transpose(1, 0, 2).reshape(16, -1),
            g_gain_full.reshape(16, -1),
        ],
        1,
    )
    cols = g_a.shape[1]
    vec = jnp.pad(vec, ((0, 0), (0, model - vec.shape[1]))).reshape(16, model // cols, cols)
    vec_rows = jnp.pad(jnp.concatenate(two_terms(vec), 1), ((0, 0), (0, 8 - 2 * (model // cols)), (0, 0)))
    g_rows = jnp.concatenate([g_a.reshape(16, rows_in, cols), vec_rows], 1)
    g_rows, d_both = tie(g_rows, core_sum(d_near, d_far))
    all_sums = lax.all_to_all(g_rows, ("y", "x"), 0, 0)
    d_ring = ring_back(d_both)
    wo_sum = transpose_zy(sum_b[:, mine:])
    output = (x_mine.astype(F32) + sum(p.astype(F32) for p in (out_both[0],) + out_ring)).astype(BF16)

    all_sums, d_ring, wo_sum = tie(all_sums, d_ring, wo_sum)
    vec = jnp.sum(all_sums[:, rows_in:].astype(F32), 0)
    vec = (vec[: model // cols] + vec[model // cols : 2 * (model // cols)]).reshape(1, model)
    last = jnp.concatenate([jnp.sum(all_sums[:, :rows_in].astype(F32), 0).astype(BF16), sum_b[:, :mine], wo_sum], 1)
    last = jnp.concatenate([last, *two_terms(vec), jnp.zeros((14, model), BF16)], 0)
    near = jnp.stack((last,) + ring(last))
    w_in_grad, w_out_grad, norm_sum, vec_sum = assemble(z, core, near, swap(near), w_in, w_out, mine, nst, my_heads)
    vec = vec_sum[0] + vec_sum[1]
    norm_gain_grad = norm_sum[:, 0] / norm_gain.astype(F32)
    d_normed = sum(p.astype(F32) for p in (d_both[0],) + d_ring)

    x_f = x_mine.astype(F32)
    inverse = lax.rsqrt(jnp.mean(x_f * x_f, -1, keepdims=True) + EPS)
    scaled = x_f * inverse
    d_hat = d_normed * norm_f[None]
    d_x = inverse * (d_hat - scaled * jnp.mean(d_hat * scaled, -1, keepdims=True))
    input_grad = (cotangent[0].astype(F32) + d_x).astype(BF16)

    conv_w_grad = vec[: 4 * k].reshape(4, k)
    conv_b_grad = vec[4 * k : 5 * k]
    h0 = 5 * k
    dt_bias_grad, a_log_grad, d_skip_grad = (vec[h0 + i * hn : h0 + (i + 1) * hn] for i in range(3))
    out_gain_grad = vec[h0 + 3 * hn : h0 + 3 * hn + out_gain.shape[0]]

    return (
        output[None],
        input_grad[None],
        norm_gain_grad,
        w_in_grad,
        conv_w_grad,
        conv_b_grad,
        dt_bias_grad,
        a_log_grad,
        d_skip_grad,
        out_gain_grad,
        w_out_grad,
    )


def solution(mesh):
    cube = Mesh(mesh.devices.reshape(4, 4, 4, 2), AXES)
    rows, shard = P(("z", "y", "x"), "c", None), ("y", "x")
    return jax.shard_map(
        local,
        mesh=cube,
        in_specs=(
            rows,
            P(("z", "y", "x"), None),
            P(shard),
            P(shard, None),
            P(None, shard),
            P(shard),
            P(shard),
            P(shard),
            P(shard),
            P(shard),
            P(shard, None),
            rows,
        ),
        out_specs=(
            rows,
            rows,
            P(shard),
            P(shard, None),
            P(None, shard),
            P(shard),
            P(shard),
            P(shard),
            P(shard),
            P(shard),
            P(shard, None),
        ),
        check_vma=False,
    )
```

```python
import functools
import jax
import jax.numpy as jnp
from jax import lax
from jax.experimental import pallas as pl
from jax.experimental.pallas import tpu as pltpu
from jax.sharding import Mesh, PartitionSpec as P

F32 = jnp.float32
BF16 = jnp.bfloat16
Q = 128
CHUNKS = 4
NEG = -1e30


def mm(a, b, dims=((1,), (0,))):
    return lax.dot_general(a.astype(BF16), b.astype(BF16), (dims, ((), ())), preferred_element_type=F32)


def halves(a):
    top = a.astype(BF16)
    return top, (a - top.astype(F32)).astype(BF16)


def mm3(a, b, dims=((1,), (0,))):
    a_top, a_low = halves(a)
    b_top, b_low = halves(b)
    return mm(a_top, b_top, dims) + (mm(a_low, b_top, dims) + mm(a_top, b_low, dims))


def mm_fold(a, b):
    top, low = halves(a)
    return mm(top, b) + mm(low, b)


def mm_tri(tri, b):
    return mm(jnp.concatenate([tri, tri], 1), jnp.concatenate(halves(b), 0))


def iota(shape, axis):
    return lax.broadcasted_iota(jnp.int32, shape, axis)


def gather_mat(width, cols, head):
    return (iota((width, cols), 0) // head == iota((width, cols), 1)).astype(BF16)


def conv_of(ch, ext, aux, par, width):
    conv = ch * par[3:4, :width] + par[4:5, :width]
    shifted = []
    for s in range(1, 4):
        sh = pltpu.roll(ext, s, 0)[8:] * aux[:, s : s + 1]
        shifted.append(sh)
        conv = conv + par[3 - s : 4 - s, :width] * sh
    return conv, shifted


def softplus(v):
    return jnp.maximum(v, 0.0) + jnp.log1p(jnp.exp(-jnp.abs(v)))


def rates(raw, hp):
    pre = raw + hp[0:1]
    dt = softplus(pre)
    tri = (iota((Q, Q), 0) >= iota((Q, Q), 1)).astype(BF16)
    return pre, dt, mm_tri(tri, -hp[1:2] * dt)


def widen(cum, dt, aux, heads, low):
    squares = [jnp.broadcast_to(cum[:, h : h + 1], (Q, Q)) for h in range(heads)]
    pairs = range(0, heads, 2)
    cum_w = jnp.concatenate([jnp.where(low, squares[h], squares[h + 1]) for h in pairs], 1)
    dt_w = jnp.concatenate([jnp.where(low, dt[:, h : h + 1], dt[:, h + 1 : h + 2]) for h in pairs], 1)
    fin_w = cum_w[Q - 1 : Q]
    enter_w = jnp.exp(cum_w) * aux[:, 4:5]
    leave_w = jnp.exp(fin_w - cum_w) * aux[:, 5:6]
    through_w = jnp.exp(fin_w) * aux[0:1, 6:7]
    return squares, dt_w, enter_w, leave_w, through_w


def ssd_fwd_kernel(c_ref, p_ref, aux_ref, seg_ref, par_ref, hp_ref, y_ref, sin_ref, rim, state, *, inner, nst, head):
    width = inner + 2 * nst
    state[...] = jnp.zeros_like(state)
    rim[...] = jnp.zeros_like(rim)
    par = par_ref[...]
    hp = hp_ref[...]
    core = c_ref[0]
    lax.fori_loop(0, CHUNKS, lambda t, _: ssd_fwd_chunk(t, core, p_ref, aux_ref, seg_ref, par, hp, y_ref, sin_ref, rim, state, inner, nst, head), None)


def place_of(t, core):
    return lax.rem(lax.div(t, 2) + core, 2), pl.ds(pl.multiple_of(lax.rem(t, 2) * Q, Q), Q)


def ssd_fwd_chunk(t, core, p_ref, aux_ref, seg_ref, par, hp, y_ref, sin_ref, rim, state, inner, nst, head):
    width = inner + 2 * nst
    side, rows = place_of(t, core)
    aux = aux_ref[pl.ds(pl.multiple_of(t * Q, Q), Q), :]
    ch = p_ref[side, 0, rows, :width]
    conv, _ = conv_of(ch, jnp.concatenate([rim[...], ch], 0), aux, par, width)
    rim[...] = ch[Q - 8 :]
    act = conv / (1.0 + jnp.exp(-conv))
    x_in, bm, cm = act[:, :inner], act[:, inner : inner + nst], act[:, inner + nst :]
    pre, dt, cum = rates(p_ref[side, 0, rows, width:], hp)
    low = iota((Q, 2 * head), 1) < head
    squares, dt_w, enter_w, leave_w, through_w = widen(cum, dt, aux, inner // head, low)
    xdt = x_in * dt_w
    scores = mm3(cm, bm, ((1,), (1,)))
    allowed = (iota((Q, Q), 0) >= iota((Q, Q), 1)) & (aux[:, 0:1] == seg_ref[t, 0:1, :])
    cum_t = cum.T
    s_old = state[...]
    sin_ref[t] = s_old
    result = enter_w * mm(cm, s_old) + par[6:7, :inner] * x_in
    for pair in range(inner // (2 * head)):
        cols = slice(2 * head * pair, 2 * head * (pair + 1))
        xp = xdt[:, cols].astype(BF16)
        none = jnp.zeros_like(xp)
        mixing = []
        for h in (2 * pair, 2 * pair + 1):
            decay = jnp.exp(jnp.where(allowed, squares[h] - cum_t[h : h + 1, :], NEG))
            mixing.append((scores * decay).astype(BF16))
        by_head = jnp.concatenate([jnp.where(low, xp, none), jnp.where(low, none, xp)], 0)
        y_ref[side, 0, rows, cols] = result[:, cols] + mm(jnp.concatenate(mixing, 1), by_head)
    state[...] = through_w * s_old + mm(bm, xdt * leave_w, ((0,), (0,)))


def ssd_bwd_kernel(c_ref, p_ref, aux_ref, seg_ref, par_ref, hp_ref, dy_ref, sin_ref, *refs, inner, nst, head):
    starts_given = len(refs) > 6
    starts = refs[1:4] if starts_given else (None,) * 3
    dp_ref, gconv_ref, ghead_ref, gskip_ref, rim, state = refs[-6:]
    core = c_ref[0]
    state[...] = jnp.zeros_like(state)
    rim[...] = jnp.zeros_like(rim)

    @pl.when(pl.program_id(0) == 0)
    def _():
        for ref, start in zip((gconv_ref, ghead_ref, gskip_ref), starts):
            ref[...] = start[...] if starts_given else jnp.zeros_like(ref)

    par = par_ref[...]
    hp = hp_ref[...]
    lax.fori_loop(
        0,
        CHUNKS,
        lambda t, _: ssd_bwd_chunk(
            CHUNKS - 1 - t, core, p_ref, aux_ref, seg_ref, par, hp, dy_ref, sin_ref, dp_ref, gconv_ref, ghead_ref, gskip_ref, rim, state, inner, nst, head
        ),
        None,
    )


def ssd_bwd_chunk(
    t, core, p_ref, aux_ref, seg_ref, par, hp, dy_ref, sin_ref, dp_ref, gconv_ref, ghead_ref, gskip_ref, rim, state, inner, nst, head
):
    width = inner + 2 * nst
    side, rows = place_of(t, core)
    aux = aux_ref[pl.ds(pl.multiple_of(t * Q, Q), Q), :]
    ch = p_ref[side, 0, rows, :width]
    prior = jnp.maximum(t - 1, 0)
    prev = p_ref[lax.rem(lax.div(prior, 2) + core, 2), 0, pl.ds(pl.multiple_of(lax.rem(prior, 2) * Q + Q - 8, 8), 8), :width]
    prev = prev * jnp.where(t == 0, 0.0, 1.0)
    conv, shifted = conv_of(ch, jnp.concatenate([prev, ch], 0), aux, par, width)
    sig = 1.0 / (1.0 + jnp.exp(-conv))
    act = conv * sig
    x_in, bm, cm = act[:, :inner], act[:, inner : inner + nst], act[:, inner + nst :]
    pre, dt, cum = rates(p_ref[side, 0, rows, width:], hp)
    low = iota((Q, 2 * head), 1) < head
    squares, dt_w, enter_w, leave_w, through_w = widen(cum, dt, aux, inner // head, low)
    xdt = x_in * dt_w
    scores = mm3(cm, bm, ((1,), (1,)))
    allowed = (iota((Q, Q), 0) >= iota((Q, Q), 1)) & (aux[:, 0:1] == seg_ref[t, 0:1, :])
    cum_t = cum.T
    bm = bm.astype(BF16)
    cm = cm.astype(BF16)
    dy = dy_ref[side, 0, rows, :]
    s_in = sin_ref[t]
    d_state = state[...]
    s_in_b = s_in.astype(BF16)
    d_state_b = d_state.astype(BF16)

    dye = (dy * enter_w).astype(BF16)
    inter = mm(cm, s_in_b) * enter_w
    from_state = mm(bm, d_state_b) * leave_w
    state[...] = mm(cm, dye, ((0,), (0,))) + through_w * d_state
    d_c = mm(dye, s_in_b, ((1,), (1,)))
    d_b = mm(xdt * leave_w, d_state_b, ((1,), (1,)))

    lane = iota((Q, Q), 1)
    sub = iota((8, Q), 0)
    d_scores = jnp.zeros((Q, Q), F32)
    row_sums = jnp.zeros((Q, Q), F32)
    col_sums = jnp.zeros((8, Q), F32)
    d_xdt = []
    for pair in range(inner // (2 * head)):
        cols = slice(2 * head * pair, 2 * head * (pair + 1))
        xp = xdt[:, cols]
        dyp = dy[:, cols]
        d_k2 = mm3(dyp, jnp.concatenate([jnp.where(low, xp, 0.0), jnp.where(low, 0.0, xp)], 0), ((1,), (1,)))
        kmats = []
        for k in range(2):
            h = 2 * pair + k
            decay = jnp.exp(jnp.where(allowed, squares[h] - cum_t[h : h + 1, :], NEG))
            d_k = d_k2[:, k * Q : (k + 1) * Q]
            kmat = scores * decay
            d_scores = d_scores + d_k * decay
            both = d_k * kmat
            row_sums = jnp.where(lane == h, jnp.sum(both, 1, keepdims=True), row_sums)
            col_sums = jnp.where(sub == h, jnp.sum(both, 0, keepdims=True), col_sums)
            kmats.append(kmat)
        dy_by_head = jnp.concatenate([jnp.where(low, dyp, 0.0), jnp.where(low, 0.0, dyp)], 0)
        d_xdt.append(mm3(jnp.concatenate(kmats, 0), dy_by_head, ((0,), (0,))))
    z = jnp.concatenate(d_xdt, 1) + from_state
    d_c = d_c + mm(d_scores, bm)
    d_b = d_b + mm(d_scores, cm, ((0,), (0,)))
    d_x = z * dt_w + par[6:7, :inner] * dy

    leaving = xdt * from_state
    ending = jnp.sum(s_in * d_state, 0, keepdims=True) * through_w + jnp.sum(leaving, 0, keepdims=True)
    folded = mm_fold(
        jnp.concatenate([x_in * z, dy * inter - leaving, jnp.broadcast_to(ending, (8, inner))], 0), gather_mat(inner, Q, head)
    )
    col_full = jnp.concatenate([col_sums, jnp.zeros((Q - 8, Q), F32)], 0).T
    d_cum = row_sums - col_full + folded[Q : 2 * Q]
    tri_up = (iota((Q, Q), 0) <= iota((Q, Q), 1)).astype(BF16)
    rev = mm_tri(tri_up, d_cum) + folded[2 * Q : 2 * Q + 1]
    d_dt = folded[:Q] - hp[1:2] * rev
    d_raw = d_dt / (1.0 + jnp.exp(-pre))
    live = (iota((1, Q), 1) < inner // head).astype(F32)
    d_raw = d_raw * live
    ghead_ref[0:1, :] += jnp.sum(d_raw, 0, keepdims=True)
    ghead_ref[1:2, :] += jnp.sum(rev * dt, 0, keepdims=True) * -hp[1:2]
    gskip_ref[0:1, :] += jnp.sum(dy * x_in, 0, keepdims=True)

    d_act = jnp.concatenate([d_x, d_b, d_c], 1)
    d_conv = d_act * (sig * (1.0 + conv * (1.0 - sig)))
    gconv_ref[4:5, :] += jnp.sum(d_conv, 0, keepdims=True)
    gconv_ref[3:4, :] += jnp.sum(d_conv * ch, 0, keepdims=True)
    d_ch = d_conv * par[3:4, :width]
    for s in range(1, 4):
        gconv_ref[3 - s : 4 - s, :] += jnp.sum(d_conv * shifted[s - 1], 0, keepdims=True)
        u = d_conv * aux[:, s : s + 1] * par[3 - s : 4 - s, :width]
        d_ch = d_ch + pltpu.roll(jnp.concatenate([u, rim[s - 1]], 0), Q + 8 - s, 0)[:Q]
        rim[s - 1] = u[:8]
    dp_ref[side, 0, rows, :width] = d_ch.astype(BF16)
    dp_ref[side, 0, rows, width:] = d_raw.astype(BF16)


def rows_spec(cols, first=0):
    return pl.BlockSpec((2, 1, CHUNKS * Q // 2, cols), lambda r, c: (0, r + first, 0, 0))


def common_specs(wide, width, first=0):
    return [
        rows_spec(wide, first),
        pl.BlockSpec((CHUNKS * Q, 128), lambda r, c: (r + first, 0)),
        pl.BlockSpec((CHUNKS, 8, Q), lambda r, c: (r + first, 0, 0)),
        pl.BlockSpec((8, width), lambda r, c: (0, 0)),
        pl.BlockSpec((8, 128), lambda r, c: (0, 0)),
    ]


def ssd_fwd(core, proj, aux, seg_rows, par, hp, *, inner, nst, head, interpret=False):
    seqs, half, wide = proj.shape[1:]
    rows = 2 * seqs * half
    width = inner + 2 * nst
    spec = pltpu.PrefetchScalarGridSpec(
        num_scalar_prefetch=1,
        grid=(seqs,),
        in_specs=common_specs(wide, width),
        out_specs=[rows_spec(inner), pl.BlockSpec((CHUNKS, nst, inner), lambda r, c: (r, 0, 0))],
        scratch_shapes=[pltpu.VMEM((8, width), F32), pltpu.VMEM((nst, inner), F32)],
    )
    y, s_in = pl.pallas_call(
        functools.partial(ssd_fwd_kernel, inner=inner, nst=nst, head=head),
        grid_spec=spec,
        out_shape=[
            jax.ShapeDtypeStruct((2, seqs, CHUNKS * Q // 2, inner), F32),
            jax.ShapeDtypeStruct((seqs * CHUNKS, nst, inner), F32),
        ],
        cost_estimate=pl.CostEstimate(flops=1, transcendentals=0, bytes_accessed=1),
        interpret=interpret,
        name="ssd_fwd",
    )(core, proj, aux, seg_rows, par, hp)
    return y, s_in


def ssd_bwd(core, proj, aux, seg_rows, par, hp, dy, s_in, first, count, so_far, *, inner, nst, head, interpret=False):
    seqs, half, wide = proj.shape[1:]
    rows = 2 * seqs * half
    width = inner + 2 * nst
    out_specs = [
        rows_spec(wide, first),
        pl.BlockSpec((8, width), lambda r, c: (0, 0)),
        pl.BlockSpec((8, 128), lambda r, c: (0, 0)),
        pl.BlockSpec((8, inner), lambda r, c: (0, 0)),
    ]
    in_specs = common_specs(wide, width, first) + [
        rows_spec(inner, first),
        pl.BlockSpec((CHUNKS, nst, inner), lambda r, c: (r + first, 0, 0)),
    ]
    operands = (core, proj, aux, seg_rows, par, hp, dy, s_in)
    aliases = {}
    if so_far is not None:
        aliases = {len(operands) + i: i for i in range(4)}
        in_specs += [pl.BlockSpec(memory_space=pl.ANY)] + out_specs[1:]
        operands += tuple(so_far)
    spec = pltpu.PrefetchScalarGridSpec(
        num_scalar_prefetch=1,
        grid=(count,),
        in_specs=in_specs,
        out_specs=out_specs,
        scratch_shapes=[pltpu.VMEM((3, 8, width), F32), pltpu.VMEM((nst, inner), F32)],
    )
    return pl.pallas_call(
        functools.partial(ssd_bwd_kernel, inner=inner, nst=nst, head=head),
        grid_spec=spec,
        out_shape=[
            jax.ShapeDtypeStruct((2, seqs, CHUNKS * Q // 2, wide), BF16),
            jax.ShapeDtypeStruct((8, width), F32),
            jax.ShapeDtypeStruct((8, 128), F32),
            jax.ShapeDtypeStruct((8, inner), F32),
        ],
        input_output_aliases=aliases,
        cost_estimate=pl.CostEstimate(flops=1, transcendentals=0, bytes_accessed=1),
        interpret=interpret,
        name="ssd_bwd",
    )(*operands)


def masks_of(seg):
    s_count, length = seg.shape
    cols = [seg.astype(F32)]
    for s in range(1, 4):
        back = jnp.concatenate([jnp.full((s_count, s), -1, seg.dtype), seg[:, :-s]], 1)
        cols.append((back == seg).astype(F32))
    by_chunk = seg.reshape(s_count, length // Q, Q)
    last = by_chunk[:, :, -1:]
    prev = jnp.concatenate([jnp.full((s_count, 1, 1), -1, seg.dtype), last[:, :-1]], 1)
    cols.append((by_chunk == prev).astype(F32).reshape(s_count, length))
    cols.append((by_chunk == last).astype(F32).reshape(s_count, length))
    cols.append(jnp.broadcast_to(prev == last, by_chunk.shape).astype(F32).reshape(s_count, length))
    aux = jnp.stack(cols, -1).reshape(s_count * length, len(cols))
    aux = jnp.pad(aux, ((0, 0), (0, 128 - len(cols))))
    rows = jnp.broadcast_to(seg.astype(F32).reshape(-1, 1, Q), (s_count * length // Q, 8, Q))
    return aux, rows


EPS = 1e-05
AXES = ("z", "y", "x", "c")


def pull(a, axis, d):
    return lax.ppermute(a, axis, [((i + d) % 4, i) for i in range(4)])


def swap(a):
    return lax.ppermute(a, "c", [(0, 1), (1, 0)])


def transpose_zy(a):
    return lax.ppermute(a, ("z", "y"), [(4 * y + z, 4 * z + y) for z in range(4) for y in range(4)])


def ring(a):
    return tuple(pull(a, "z", d) for d in (1, 2, 3))


def ring_ends(a):
    return pull(a, "z", 1), pull(a, "z", 3)


def ring_middle(one, three):
    half = one.shape[0] // 2
    return pull(one[:half], "z", 1), pull(three[half:], "z", 3)


def ring_back(q):
    return tuple(pull(q[d], "z", 4 - d) for d in (1, 2, 3))


def plane_all(a):
    return lax.all_gather(a, ("y", "x"), axis=0)


def plane_all_small(a):
    return lax.all_to_all(jnp.broadcast_to(a[None], (16,) + a.shape), ("y", "x"), 0, 0)


def tie(*values):
    return lax.optimization_barrier(values)


def two_terms(a):
    top = lax.reduce_precision(a, 8, 7)
    return top.astype(BF16), (a - top).astype(BF16)


def after(value, *others):
    return lax.optimization_barrier((value,) + others)[0]


def cost(flops, bytes_accessed):
    return pl.CostEstimate(flops=1, transcendentals=0, bytes_accessed=1)


def whole(shape):
    return pl.BlockSpec(shape, lambda *_: (0,) * len(shape))


PER = 2


def near_spec(rows, cols):
    return pl.BlockSpec((PER, rows, cols), lambda h, r: (jnp.where(h == 0, r, 4 // PER - 1), 0, 0))


def far_spec(rows, cols):
    return pl.BlockSpec((PER, rows, cols), lambda h, r: (jnp.where(h == 0, 0, r), 0, 0))


def block_spec(cols, rows=256):
    return pl.BlockSpec((1, PER, rows, cols), lambda h, r: (h, r, 0, 0))


def flat_rows(ref):
    v = ref[0] if len(ref.shape) == 4 else ref[...]
    return v.reshape(v.shape[0] * v.shape[1], v.shape[2])


def put_rows(ref, v):
    if len(ref.shape) == 4:
        ref[0] = v.reshape(ref.shape[1:])
    else:
        ref[...] = v.reshape(ref.shape)


def half_cols(core, width):
    return pl.ds(pl.multiple_of(core * width, width), width), pl.ds(pl.multiple_of((1 - core) * width, width), width)


def enter_kernel(near_ref, far_ref, gain_ref, w_ref, normed_ref, proj_ref):
    def step(ref):
        p = flat_rows(ref).astype(F32)
        inverse = lax.rsqrt(jnp.mean(p * p, -1, keepdims=True) + EPS)
        normed = (p * inverse * gain_ref[...]).astype(BF16)
        put_rows(normed_ref, normed)
        put_rows(proj_ref, jnp.dot(normed, w_ref[...], preferred_element_type=F32))

    pl.when(pl.program_id(0) == 0)(lambda: step(near_ref))
    pl.when(pl.program_id(0) == 1)(lambda: step(far_ref))


def enter(near, far, gain, w):
    padded, model = near.shape[1:]
    rows, cols = 256, w.shape[1]
    return pl.pallas_call(
        enter_kernel,
        grid=(2, 4 // PER),
        out_shape=[jax.ShapeDtypeStruct((2, 4, rows, model), BF16), jax.ShapeDtypeStruct((2, 4, rows, cols), F32)],
        in_specs=[near_spec(padded, model), far_spec(padded, model), whole((1, model)), whole(w.shape)],
        out_specs=[block_spec(model), block_spec(cols)],
        cost_estimate=cost(16 * rows * model * cols, 8 * rows * (4 * model + 4 * cols)),
        name="enter",
    )(near, far, gain, w)


def gate_kernel(core_ref, normed_ref, near_ref, far_ref, wg_ref, wo_ref, wt_ref, y_ref, gain_ref, gate_ref, dm_ref, sums_ref):
    gate = jnp.dot(flat_rows(normed_ref), wg_ref[...], preferred_element_type=F32)
    here, there = half_cols(core_ref[0], wo_ref.shape[1])
    dims = (((1,), (1,)), ((), ()))

    def back(cot_ref):
        rows = gate.shape[0]
        a = cot_ref[:, :, here].reshape(rows, wo_ref.shape[1])
        b = cot_ref[:, :, there].reshape(rows, wo_ref.shape[1])
        put_rows(
            dm_ref,
            lax.dot_general(a, wo_ref[...], dims, preferred_element_type=F32)
            + lax.dot_general(b, wt_ref[...], dims, preferred_element_type=F32),
        )

    pl.when(pl.program_id(0) == 0)(lambda: back(near_ref))
    pl.when(pl.program_id(0) == 1)(lambda: back(far_ref))
    d_mixed = flat_rows(dm_ref)
    put_rows(gate_ref, gate)
    gated = flat_rows(y_ref) * gate / (1.0 + jnp.exp(-gate))
    ones = jnp.ones((8, gate.shape[1]), BF16)

    def total(v):
        top, low = halves(v)
        return (mm(ones, top, ((1,), (1,))) + mm(ones, low, ((1,), (1,))))[:1]

    both = jnp.concatenate([total(gated * gated), total(d_mixed * gain_ref[...] * gated)], 0)
    rows = sums_ref.shape[3]
    for q in range(PER):
        sums_ref[0, q] = both[:, q * rows : (q + 1) * rows]


def gate_stage(core, normed, near, far, w_g, w_o, w_t, y, gain):
    rows, model = normed.shape[2:]
    mine = w_g.shape[1]
    return pl.pallas_call(
        gate_kernel,
        grid=(2, 4 // PER),
        out_shape=[jax.ShapeDtypeStruct((2, 4, rows, mine), F32)] * 2 + [jax.ShapeDtypeStruct((2, 4, 2, rows), F32)],
        in_specs=[
            pl.BlockSpec(memory_space=pltpu.SMEM),
            block_spec(model),
            near_spec(rows, model),
            far_spec(rows, model),
            whole(w_g.shape),
            whole(w_o.shape),
            whole(w_t.shape),
            block_spec(mine),
            whole((1, mine)),
        ],
        out_specs=[block_spec(mine), block_spec(mine), block_spec(rows, 2)],
        cost_estimate=cost(32 * rows * model * mine, 8 * rows * (4 * model + 12 * mine)),
        name="gate_stage",
    )(core, normed, near, far, w_g, w_o, w_t, y, gain)


def turn_kernel(
    core_ref, normed_ref, near_ref, far_ref, wo_ref, wt_ref, y_ref, gate_ref, dm_ref, sums_ref, gain_ref,
    out_near_ref, out_far_ref, dy_ref, dgate_ref, keep_ref, send_ref, ggate_ref, ggain_ref, acc_o, acc_g, *, inner,
):
    h, r = pl.program_id(0), pl.program_id(1)
    rows = gate_ref.shape[2]
    gate, d_mixed, y, gain = flat_rows(gate_ref), flat_rows(dm_ref), flat_rows(y_ref), gain_ref[...]
    sums = jnp.concatenate(
        [jnp.concatenate([sums_ref[0, q], jnp.zeros((6, rows), F32)], 0).T for q in range(PER)], 0
    )
    scale = lax.rsqrt(sums[:, 0:1] / inner + EPS)
    lean = sums[:, 1:2] / inner * scale * scale
    sig = 1.0 / (1.0 + jnp.exp(-gate))
    act = gate * sig
    gated = y * act
    mixed = (gated * scale * gain).astype(BF16)
    d_gated = scale * (d_mixed * gain - gated * lean)
    put_rows(dy_ref, d_gated * act)
    d_gate = (d_gated * y * (sig * (1.0 + gate * (1.0 - sig)))).astype(BF16)
    put_rows(dgate_ref, d_gate)
    here, there = half_cols(core_ref[0], wo_ref.shape[1])

    def forward(out_ref, cot_ref):
        shape = out_ref.shape[:2] + (wo_ref.shape[1],)
        out_ref[:, :, here] = jnp.dot(mixed, wo_ref[...], preferred_element_type=F32).astype(BF16).reshape(shape)
        out_ref[:, :, there] = jnp.dot(mixed, wt_ref[...], preferred_element_type=F32).astype(BF16).reshape(shape)
        acc_o[...] += lax.dot_general(mixed, flat_rows(cot_ref), (((0,), (0,)), ((), ())), preferred_element_type=F32)

    @pl.when((h == 0) & (r == 0))
    def _():
        acc_o[...] = jnp.zeros_like(acc_o)
        acc_g[...] = jnp.zeros_like(acc_g)
        ggain_ref[...] = jnp.zeros_like(ggain_ref)

    ggain_ref[0:1, :] += jnp.sum(d_mixed * gated * scale, 0, keepdims=True)
    pl.when(h == 0)(lambda: forward(out_near_ref, near_ref))
    pl.when(h == 1)(lambda: forward(out_far_ref, far_ref))
    acc_g[...] += lax.dot_general(flat_rows(normed_ref), d_gate, (((0,), (0,)), ((), ())), preferred_element_type=F32)

    @pl.when((h == 1) & (r == pl.num_programs(1) - 1))
    def _():
        keep_ref[...] = acc_o[:, here].astype(BF16)
        send_ref[...] = acc_o[:, there].astype(BF16)
        ggate_ref[...] = acc_g[...].astype(BF16)


def turn_stage(core, normed, near, far, w_o, w_t, y, gate, d_mixed, sums, gain, inner):
    rows, model = normed.shape[2:]
    mine = w_o.shape[0]
    return pl.pallas_call(
        functools.partial(turn_kernel, inner=inner),
        grid=(2, 4 // PER),
        out_shape=[
            jax.ShapeDtypeStruct((4, rows, model), BF16),
            jax.ShapeDtypeStruct((4, rows, model), BF16),
            jax.ShapeDtypeStruct((2, 4, rows, mine), F32),
            jax.ShapeDtypeStruct((2, 4, rows, mine), BF16),
            jax.ShapeDtypeStruct(w_o.shape, BF16),
            jax.ShapeDtypeStruct(w_o.shape, BF16),
            jax.ShapeDtypeStruct((model, mine), BF16),
            jax.ShapeDtypeStruct((8, mine), F32),
        ],
        in_specs=[
            pl.BlockSpec(memory_space=pltpu.SMEM),
            block_spec(model),
            near_spec(rows, model),
            far_spec(rows, model),
            whole(w_o.shape),
            whole(w_o.shape),
            block_spec(mine),
            block_spec(mine),
            block_spec(mine),
            block_spec(rows, 2),
            whole((1, mine)),
        ],
        out_specs=[
            near_spec(rows, model),
            far_spec(rows, model),
            block_spec(mine),
            block_spec(mine),
            whole(w_o.shape),
            whole(w_o.shape),
            whole((model, mine)),
            whole((8, mine)),
        ],
        scratch_shapes=[pltpu.VMEM((mine, model), F32), pltpu.VMEM((model, mine), F32)],
        cost_estimate=cost(48 * rows * model * mine, 8 * rows * (6 * model + 18 * mine)),
        name="turn_stage",
    )(core, normed, near, far, w_o, w_t, y, gate, d_mixed, sums, gain)


def back_kernel(dp_ref, wa_ref, dg_ref, wg_ref, near_ref, far_ref):
    t = lax.dot_general(flat_rows(dp_ref), wa_ref[...], (((1,), (1,)), ((), ())), preferred_element_type=F32)
    t = t + lax.dot_general(flat_rows(dg_ref), wg_ref[...], (((1,), (1,)), ((), ())), preferred_element_type=F32)
    pl.when(pl.program_id(0) == 0)(lambda: put_rows(near_ref, t.astype(BF16)))
    pl.when(pl.program_id(0) == 1)(lambda: put_rows(far_ref, t.astype(BF16)))


def back_dot(d_proj, w_a, d_gate, w_g):
    rows, ka = d_proj.shape[2:]
    m, kg = w_g.shape
    return pl.pallas_call(
        back_kernel,
        grid=(2, 4 // PER),
        out_shape=[jax.ShapeDtypeStruct((4, rows, m), BF16)] * 2,
        in_specs=[block_spec(ka), whole((m, ka)), block_spec(kg), whole((m, kg))],
        out_specs=[near_spec(rows, m), far_spec(rows, m)],
        cost_estimate=cost(0, 0),
        name="back_dot",
    )(d_proj, w_a, d_gate, w_g)


def unpack_kernel(core_ref, all_ref, wg_ref, mine_ref, send_ref):
    rows, width = all_ref.shape[1:]
    part, cols = rows // 2, wg_ref.shape[1]
    for k in range(16):
        wg_ref[k * rows : (k + 1) * rows, :] = all_ref[k, :, :cols]

    def move(ref, side):
        for x in (2 * side, 2 * side + 1):
            for y in range(4):
                at = (4 * (x % 2) + y) * part
                for k in range(2):
                    piece = all_ref[4 * y + x, k * part : (k + 1) * part, cols:]
                    ref[at : at + part, k * (width - cols) : (k + 1) * (width - cols)] = piece

    for core in range(2):

        @pl.when(core_ref[0] == core)
        def _():
            move(mine_ref, core)
            move(send_ref, 1 - core)


def unpack(core, gathered, cols):
    _, rows, width = gathered.shape
    half = jax.ShapeDtypeStruct((4 * rows, 2 * (width - cols)), BF16)
    return pl.pallas_call(
        unpack_kernel,
        in_specs=[pl.BlockSpec(memory_space=pltpu.SMEM), whole(gathered.shape)],
        out_specs=[whole((16 * rows, cols)), whole(half.shape), whole(half.shape)],
        grid=(1,),
        out_shape=[jax.ShapeDtypeStruct((16 * rows, cols), BF16), half, half],
        cost_estimate=cost(0, 0),
        name="unpack",
    )(core, gathered)


def pack_kernel(core_ref, gate_ref, keep_ref, got_ref, out_ref):
    rows, width = out_ref.shape[1:]
    part, cols = rows // 2, gate_ref.shape[1]
    for k in range(16):
        out_ref[k, :, :cols] = gate_ref[k * rows : (k + 1) * rows, :]

    def move(ref, side):
        for x in (2 * side, 2 * side + 1):
            for y in range(4):
                at = (4 * (x % 2) + y) * part
                for k in range(2):
                    piece = ref[at : at + part, k * (width - cols) : (k + 1) * (width - cols)]
                    out_ref[4 * y + x, k * part : (k + 1) * part, cols:] = piece

    for core in range(2):

        @pl.when(core_ref[0] == core)
        def _():
            move(keep_ref, core)
            move(got_ref, 1 - core)


def pack(core, g_gate, keep, got):
    model, cols = g_gate.shape
    rows = model // 16
    shape = (16, rows, cols + keep.shape[1] // 2)
    return pl.pallas_call(
        pack_kernel,
        in_specs=[pl.BlockSpec(memory_space=pltpu.SMEM), whole(g_gate.shape), whole(keep.shape), whole(got.shape)],
        out_specs=whole(shape),
        grid=(1,),
        out_shape=jax.ShapeDtypeStruct(shape, BF16),
        cost_estimate=cost(0, 0),
        name="pack",
    )(core, g_gate, keep, got)


def assemble_kernel(
    at_ref, near_ref, far_ref, win_ref, gain_ref, gwin_ref, gwo_ref, norm_ref, convw_ref, convb_ref, dtb_ref, alog_ref,
    skip_ref, outg_ref, conv_ref, wide_ref, *, mine, nst, my_heads,
):
    z, core, shard = at_ref[0], at_ref[1], at_ref[2]
    rows, wide = win_ref.shape
    inner = 8 * mine
    part = gwo_ref.shape[0] // 4
    width = mine + 2 * nst + 128
    bc = jnp.zeros((rows, 2 * nst), F32)
    conv_bc = jnp.zeros((8, 2 * nst), F32)
    heads = jnp.zeros((8, 128), F32)
    width_c = mine + 2 * nst
    raw = jnp.zeros((rows, 128), F32)
    lane = iota((rows, 128), 1)
    for zz in range(4):
        r = lax.rem(zz - z + 4, 4)
        for cc in range(2):
            j = 2 * zz + cc
            both = jnp.where(core == cc, near_ref[r].astype(F32), far_ref[r].astype(F32))
            v = both[rows : rows + 8] + both[rows + 8 : rows + 16]
            conv_ref[:, j * mine : (j + 1) * mine] = v[:, :mine]
            conv_bc = conv_bc + v[:, mine:width_c]
            h = jnp.where(iota((8, 128), 1) < my_heads, v[:, width_c : width_c + 128], 0.0)
            heads = heads + (pltpu.roll(h, j * my_heads, 1) if j else h)
            wide_ref[0:1, j * mine : (j + 1) * mine] = v[0:1, width_c + 128 : width_c + 128 + mine]
            wide_ref[1:2, j * mine : (j + 1) * mine] = v[0:1, width_c + 128 + mine :]
            both = both[:rows]
            a, b = both[:, :width], both[:, width:]
            gwin_ref[:, j * mine : (j + 1) * mine] = b[:, :mine]
            gwin_ref[:, inner + j * mine : inner + (j + 1) * mine] = a[:, :mine]
            bc = bc + a[:, mine : mine + 2 * nst]
            piece = a[:, mine + 2 * nst :]
            piece = jnp.where(lane < my_heads, piece, 0.0)
            raw = raw + (pltpu.roll(piece, j * my_heads, 1) if j else piece)
            for k in range(2):
                cols = (2 * cc + k) * (b.shape[1] - mine)
                gwo_ref[zz * part : (zz + 1) * part, cols : cols + b.shape[1] - mine] = b[k * part : (k + 1) * part, mine:]
    gwin_ref[:, 2 * inner : 2 * inner + 2 * nst] = bc
    gwin_ref[:, 2 * inner + 2 * nst :] = raw[:, : wide - 2 * inner - 2 * nst]
    conv_ref[:, inner:] = conv_bc
    k, kn, hn = convb_ref.shape[1], outg_ref.shape[1], dtb_ref.shape[1]

    def own(v, count):
        total = v.shape[1]
        return pltpu.roll(v, lax.rem(total - shard * count, total), 1)[:, :count]

    conv = own(conv_ref[...], k)
    convw_ref[...] = conv[:4]
    convb_ref[...] = conv[4:5]
    wide_own = own(wide_ref[...], kn)
    outg_ref[...] = wide_own[1:2]
    per = kn // hn
    skips = [jnp.sum(wide_own[0:1, i * per : (i + 1) * per], 1, keepdims=True) for i in range(hn)]
    skip_ref[...] = jnp.concatenate(skips, 1)
    heads = pltpu.roll(heads, lax.rem(128 - shard * hn, 128), 1)
    dtb_ref[...] = heads[0:1, :hn]
    alog_ref[...] = heads[1:2, :hn]
    norm = jnp.sum(gwin_ref[...] * win_ref[...].astype(F32), 1, keepdims=True)
    norm_ref[...] = jnp.broadcast_to(norm, (rows, 128)).T[0:1, :] / gain_ref[...].astype(F32)


def assemble(z, core, shard, near, far, w_in, norm_gain, w_out, k, kn, hn, mine, nst, my_heads):
    at = jnp.stack([z, core[0], shard]).astype(jnp.int32)
    arrays = (near, far, w_in, norm_gain[None])
    shapes = [w_in.shape, w_out.shape, (1, w_in.shape[0]), (4, k), (1, k), (1, hn), (1, hn), (1, hn), (1, kn)]
    return pl.pallas_call(
        functools.partial(assemble_kernel, mine=mine, nst=nst, my_heads=my_heads),
        in_specs=[pl.BlockSpec(memory_space=pltpu.SMEM)] + [whole(a.shape) for a in arrays],
        out_specs=[whole(a) for a in shapes],
        grid=(1,),
        out_shape=[jax.ShapeDtypeStruct(a, F32) for a in shapes],
        scratch_shapes=[pltpu.VMEM((8, 8 * mine + 2 * nst), F32), pltpu.VMEM((2, 8 * mine), F32)],
        cost_estimate=cost(0, 0),
        name="assemble",
    )(at, *arrays)


def dot(a, b, dims):
    return lax.dot_general(a, b, (dims, ((), ())), preferred_element_type=F32)


def local(inputs, segments, norm_gain, w_in, conv_w, conv_b, dt_bias, a_log, d_skip, out_gain, w_out, cotangent):
    z, y, x, c = (lax.axis_index(name) for name in AXES)
    member = 2 * z + c
    length, model = inputs.shape[1:]
    inner = 16 * out_gain.shape[0]
    heads = 16 * d_skip.shape[0]
    xwidth = 16 * conv_b.shape[0]
    nst = (xwidth - inner) // 2
    head = inner // heads
    mine = inner // 8
    my_heads = heads // 8
    core = c.astype(jnp.int32).reshape(1)
    rows_in = w_in.shape[0]

    w_x = lax.dynamic_slice_in_dim(w_in, inner + member * mine, mine, 1)
    w_dt = jnp.pad(
        lax.dynamic_slice_in_dim(w_in[:, inner + xwidth :], member * my_heads, my_heads, 1), ((0, 0), (0, 128 - my_heads))
    )
    w_bc = jnp.concatenate([w_in[:, inner + mine * 8 : inner + xwidth], w_dt], 1)
    block_a = jnp.concatenate([w_x, w_bc], 1)
    all_a = plane_all(block_a)
    w_a = all_a.reshape(model, -1)

    def lanes(a):
        return jnp.pad(a, ((0, 0), (0, -a.shape[1] % 128))).reshape(-1, 128)

    tiny = jnp.concatenate([dt_bias, a_log, d_skip])[None]
    small = jnp.concatenate([lanes(conv_w), lanes(conv_b[None]), lanes(out_gain[None]), lanes(norm_gain[None]), lanes(tiny)], 0)
    small = after(jnp.pad(small, ((0, -small.shape[0] % 16), (0, 0))), block_a)

    x_mine = inputs[0]
    one, three = ring_ends(x_mine)
    middle = ring_middle(one, three)
    seg_mine = after(segments.reshape(-1, 128), block_a)
    seg_all = jnp.stack((seg_mine,) + ring(seg_mine)).reshape(4, -1)
    aux, seg_rows = masks_of(seg_all)

    small = plane_all_small(small).astype(F32)
    k, kn, hn = conv_b.shape[0], out_gain.shape[0], d_skip.shape[0]
    lk, lg = -(-k // 128), -(-kn // 128)
    conv_wf = small[:, : 4 * lk].reshape(16, 4, lk * 128)[:, :, :k].transpose(1, 0, 2).reshape(4, xwidth)
    conv_bf = small[:, 4 * lk : 5 * lk].reshape(16, lk * 128)[:, :k].reshape(1, xwidth)
    gain_f = small[:, 5 * lk : 5 * lk + lg].reshape(16, lg * 128)[:, :kn].reshape(-1)
    norm_f = small[:, 5 * lk + lg, :rows_in].reshape(-1)
    dtb_f, alog_f, skip_f = (small[:, 5 * lk + lg + 1, i * hn : (i + 1) * hn].reshape(-1) for i in range(3))

    def own(a, count):
        return lax.dynamic_slice_in_dim(a, member * count, count, a.ndim - 1)

    conv_all = jnp.concatenate([conv_wf, conv_bf], 0)
    conv_mine = jnp.concatenate([own(conv_all[:, :inner], mine), conv_all[:, inner:]], 1)
    skip_mine = jnp.repeat(own(skip_f, my_heads), head)
    par = jnp.concatenate(
        [conv_mine, jnp.zeros((1, mine + 2 * nst), F32), jnp.pad(skip_mine, (0, 2 * nst))[None], jnp.zeros((1, mine + 2 * nst), F32)], 0
    )
    rates_mine = jnp.stack([own(dtb_f, my_heads), jnp.exp(own(alog_f, my_heads))])
    hp = jnp.pad(rates_mine, ((0, 6), (0, 128 - my_heads)))
    gain_mine = own(gain_f, mine)[None]

    w_g = lax.dynamic_slice_in_dim(w_in, member * mine, mine, 1)
    part = w_out.shape[0] // 4
    half = model // 2
    wo_piece = lax.dynamic_slice(w_out, (z * part, c * half), (part, half))
    wo_piece = transpose_zy(jnp.concatenate([wo_piece[:, : half // 2], wo_piece[:, half // 2 :]], 0))
    block_b = jnp.concatenate([w_g, wo_piece], 1)
    middle, block_b, norm_row, par, hp, gain_mine, aux, seg_rows = tie(
        middle, block_b, norm_f[None], par, hp, gain_mine, aux, seg_rows
    )
    all_b = plane_all(block_b)
    x_near = jnp.stack([x_mine, one, jnp.concatenate(middle, 0), three])
    x_far = swap(x_near)
    cot_ring = ring(after(cotangent[0], x_near))

    sizes_k = dict(inner=mine, nst=nst, head=head)
    normed, proj = enter(x_near, x_far, norm_row, w_a)
    mixed_ssd, s_in = ssd_fwd(core, proj, aux, seg_rows, par, hp, **sizes_k)
    mixed_ssd, cot_ring = tie(mixed_ssd, cot_ring)
    cot_near = jnp.stack((cotangent[0],) + cot_ring)
    cot_far = swap(cot_near)
    all_b = after(all_b, cot_near)
    w_g, w_o, w_t = unpack(core, all_b, mine)
    w_t = swap(w_t)
    gate, d_mixed, sums = gate_stage(core, normed, cot_near, cot_far, w_g, w_o, w_t, mixed_ssd, gain_mine)
    sums = sums + jnp.flip(swap(sums), 0)
    sums = sums + sum(jnp.roll(pull(sums, "z", d), d, 1) for d in (1, 2, 3))
    out_near, out_far, d_y, d_gate, wo_keep, wo_send, g_gate, g_gain = turn_stage(
        core, normed, cot_near, cot_far, w_o, w_t, mixed_ssd, gate, d_mixed, sums, gain_mine, inner
    )

    def core_sum(near, far):
        return (near.astype(F32) + swap(far).astype(F32)).astype(BF16)

    backward = functools.partial(ssd_bwd, core, proj, aux, seg_rows, par, hp, d_y, s_in, **sizes_k)
    so_far, wo_got = tie(backward(0, 1, None), swap(wo_send))
    g_b = pack(core, g_gate, wo_keep, wo_got)
    all_b = lax.all_to_all(g_b, ("y", "x"), 0, 0)
    so_far, out_both = tie(after(so_far, g_b), core_sum(out_near, out_far))
    out_ring = ring_back(out_both)
    d_proj, g_conv, g_head, g_skip = backward(1, 3, so_far)
    raw = jnp.pad(jnp.concatenate([g_conv, g_head, g_skip, g_gain], 1), ((0, 16), (0, 0)))
    d_proj, raw = tie(d_proj, raw)
    raw = jnp.sum(lax.all_gather(raw, ("y", "x"), axis=0), 0)[:8]
    d_near, d_far = back_dot(d_proj, w_a, d_gate, w_g)
    d_proj, d_far, d_near, all_b, out_ring = tie(d_proj, d_far, d_near, all_b, out_ring)
    flat = 8 * length
    g_a = dot(normed.reshape(flat, model), d_proj.reshape(flat, -1), ((0,), (0,))).astype(BF16)
    sum_b = jnp.sum(all_b.astype(F32), 0).astype(BF16)

    g_a, d_both = tie(g_a, core_sum(d_near, d_far))
    all_sums = lax.all_to_all(g_a.reshape(16, rows_in, -1), ("y", "x"), 0, 0)
    d_ring = ring_back(d_both)
    wo_sum = transpose_zy(sum_b[:, mine:])
    output = (x_mine.astype(F32) + sum(p.astype(F32) for p in (out_both[0],) + out_ring)).astype(BF16)

    all_sums, wo_sum, raw, d_ring = tie(all_sums, wo_sum, raw, d_ring)
    last = jnp.concatenate([jnp.sum(all_sums.astype(F32), 0).astype(BF16), sum_b[:, :mine], wo_sum], 1)
    last = jnp.concatenate([last, *two_terms(raw)], 0)
    last_ring = ring(last)
    d_normed = sum(p.astype(F32) for p in (d_both[0],) + d_ring)
    x_f = x_mine.astype(F32)
    inverse = lax.rsqrt(jnp.mean(x_f * x_f, -1, keepdims=True) + EPS)
    scaled = x_f * inverse
    d_hat = d_normed * norm_f[None]
    d_x = inverse * (d_hat - scaled * jnp.mean(d_hat * scaled, -1, keepdims=True))
    input_grad = (cotangent[0].astype(F32) + d_x).astype(BF16)

    last_ring, input_grad = tie(last_ring, input_grad)
    near = jnp.stack((last,) + last_ring)
    shard = 4 * y + x
    w_in_grad, w_out_grad, *others = assemble(
        z, core, shard, near, swap(near), w_in, norm_gain, w_out, k, kn, hn, mine, nst, my_heads
    )
    norm_gain_grad, conv_w_grad = others[0][0], others[1]
    conv_b_grad, dt_bias_grad, a_log_grad, d_skip_grad, out_gain_grad = (o[0] for o in others[2:])
    return (
        output[None],
        input_grad[None],
        norm_gain_grad,
        w_in_grad,
        conv_w_grad,
        conv_b_grad,
        dt_bias_grad,
        a_log_grad,
        d_skip_grad,
        out_gain_grad,
        w_out_grad,
    )


def solution(mesh):
    cube = Mesh(mesh.devices.reshape(4, 4, 4, 2), AXES)
    rows, shard = P(("z", "y", "x"), "c", None), ("y", "x")
    return jax.shard_map(
        local,
        mesh=cube,
        in_specs=(
            rows,
            P(("z", "y", "x"), None),
            P(shard),
            P(shard, None),
            P(None, shard),
            P(shard),
            P(shard),
            P(shard),
            P(shard),
            P(shard),
            P(shard, None),
            rows,
        ),
        out_specs=(
            rows,
            rows,
            P(shard),
            P(shard, None),
            P(None, shard),
            P(shard),
            P(shard),
            P(shard),
            P(shard),
            P(shard),
            P(shard, None),
        ),
        check_vma=False,
    )
```

```python
import functools
import jax
import jax.numpy as jnp
from jax import lax
from jax.experimental import pallas as pl
from jax.experimental.pallas import tpu as pltpu
from jax.sharding import Mesh, PartitionSpec as P

F32 = jnp.float32
BF16 = jnp.bfloat16
Q = 128
CHUNKS = 4
NEG = -1e30


def mm(a, b, dims=((1,), (0,))):
    return lax.dot_general(a.astype(BF16), b.astype(BF16), (dims, ((), ())), preferred_element_type=F32)


def halves(a):
    top = a.astype(BF16)
    return top, (a - top.astype(F32)).astype(BF16)


def mm3(a, b, dims=((1,), (0,))):
    a_top, a_low = halves(a)
    b_top, b_low = halves(b)
    return mm(a_top, b_top, dims) + (mm(a_low, b_top, dims) + mm(a_top, b_low, dims))


def mm_fold(a, b):
    top, low = halves(a)
    return mm(top, b) + mm(low, b)


def mm_tri(tri, b):
    return mm(jnp.concatenate([tri, tri], 1), jnp.concatenate(halves(b), 0))


def iota(shape, axis):
    return lax.broadcasted_iota(jnp.int32, shape, axis)


def gather_mat(width, cols, head):
    return (iota((width, cols), 0) // head == iota((width, cols), 1)).astype(BF16)


def conv_of(ch, ext, aux, par, width):
    conv = ch * par[3:4, :width] + par[4:5, :width]
    shifted = []
    for s in range(1, 4):
        sh = pltpu.roll(ext, s, 0)[8:] * aux[:, s : s + 1]
        shifted.append(sh)
        conv = conv + par[3 - s : 4 - s, :width] * sh
    return conv, shifted


def softplus(v):
    return jnp.maximum(v, 0.0) + jnp.log1p(jnp.exp(-jnp.abs(v)))


def rates(raw, hp):
    pre = raw + hp[0:1]
    dt = softplus(pre)
    tri = (iota((Q, Q), 0) >= iota((Q, Q), 1)).astype(BF16)
    return pre, dt, mm_tri(tri, -hp[1:2] * dt)


def widen(cum, dt, aux, heads, low):
    squares = [jnp.broadcast_to(cum[:, h : h + 1], (Q, Q)) for h in range(heads)]
    pairs = range(0, heads, 2)
    cum_w = jnp.concatenate([jnp.where(low, squares[h], squares[h + 1]) for h in pairs], 1)
    dt_w = jnp.concatenate([jnp.where(low, dt[:, h : h + 1], dt[:, h + 1 : h + 2]) for h in pairs], 1)
    fin_w = cum_w[Q - 1 : Q]
    enter_w = jnp.exp(cum_w) * aux[:, 4:5]
    leave_w = jnp.exp(fin_w - cum_w) * aux[:, 5:6]
    through_w = jnp.exp(fin_w) * aux[0:1, 6:7]
    return squares, dt_w, enter_w, leave_w, through_w


def ssd_fwd_kernel(c_ref, p_ref, aux_ref, seg_ref, par_ref, hp_ref, y_ref, sin_ref, rim, state, *, inner, nst, head):
    width = inner + 2 * nst
    state[...] = jnp.zeros_like(state)
    rim[...] = jnp.zeros_like(rim)
    par = par_ref[...]
    hp = hp_ref[...]
    core = c_ref[0]
    lax.fori_loop(0, CHUNKS, lambda t, _: ssd_fwd_chunk(t, core, p_ref, aux_ref, seg_ref, par, hp, y_ref, sin_ref, rim, state, inner, nst, head), None)


def place_of(t, core):
    return lax.rem(lax.div(t, 2) + core, 2), pl.ds(pl.multiple_of(lax.rem(t, 2) * Q, Q), Q)


def ssd_fwd_chunk(t, core, p_ref, aux_ref, seg_ref, par, hp, y_ref, sin_ref, rim, state, inner, nst, head):
    width = inner + 2 * nst
    side, rows = place_of(t, core)
    aux = aux_ref[pl.ds(pl.multiple_of(t * Q, Q), Q), :]
    ch = p_ref[side, 0, rows, :width]
    conv, _ = conv_of(ch, jnp.concatenate([rim[...], ch], 0), aux, par, width)
    rim[...] = ch[Q - 8 :]
    act = conv / (1.0 + jnp.exp(-conv))
    x_in, bm, cm = act[:, :inner], act[:, inner : inner + nst], act[:, inner + nst :]
    pre, dt, cum = rates(p_ref[side, 0, rows, width:], hp)
    low = iota((Q, 2 * head), 1) < head
    squares, dt_w, enter_w, leave_w, through_w = widen(cum, dt, aux, inner // head, low)
    xdt = x_in * dt_w
    scores = mm3(cm, bm, ((1,), (1,)))
    allowed = (iota((Q, Q), 0) >= iota((Q, Q), 1)) & (aux[:, 0:1] == seg_ref[t, 0:1, :])
    cum_t = cum.T
    s_old = state[...]
    sin_ref[t] = s_old
    result = enter_w * mm(cm, s_old) + par[6:7, :inner] * x_in
    for pair in range(inner // (2 * head)):
        cols = slice(2 * head * pair, 2 * head * (pair + 1))
        xp = xdt[:, cols].astype(BF16)
        none = jnp.zeros_like(xp)
        mixing = []
        for h in (2 * pair, 2 * pair + 1):
            decay = jnp.exp(jnp.where(allowed, squares[h] - cum_t[h : h + 1, :], NEG))
            mixing.append((scores * decay).astype(BF16))
        by_head = jnp.concatenate([jnp.where(low, xp, none), jnp.where(low, none, xp)], 0)
        y_ref[side, 0, rows, cols] = result[:, cols] + mm(jnp.concatenate(mixing, 1), by_head)
    state[...] = through_w * s_old + mm(bm, xdt * leave_w, ((0,), (0,)))


def ssd_bwd_kernel(c_ref, p_ref, aux_ref, seg_ref, par_ref, hp_ref, dy_ref, sin_ref, *refs, inner, nst, head):
    starts_given = len(refs) > 6
    starts = refs[1:4] if starts_given else (None,) * 3
    dp_ref, gconv_ref, ghead_ref, gskip_ref, rim, state = refs[-6:]
    core = c_ref[0]
    state[...] = jnp.zeros_like(state)
    rim[...] = jnp.zeros_like(rim)

    @pl.when(pl.program_id(0) == 0)
    def _():
        for ref, start in zip((gconv_ref, ghead_ref, gskip_ref), starts):
            ref[...] = start[...] if starts_given else jnp.zeros_like(ref)

    par = par_ref[...]
    hp = hp_ref[...]
    lax.fori_loop(
        0,
        CHUNKS,
        lambda t, _: ssd_bwd_chunk(
            CHUNKS - 1 - t, core, p_ref, aux_ref, seg_ref, par, hp, dy_ref, sin_ref, dp_ref, gconv_ref, ghead_ref, gskip_ref, rim, state, inner, nst, head
        ),
        None,
    )


def ssd_bwd_chunk(
    t, core, p_ref, aux_ref, seg_ref, par, hp, dy_ref, sin_ref, dp_ref, gconv_ref, ghead_ref, gskip_ref, rim, state, inner, nst, head
):
    width = inner + 2 * nst
    side, rows = place_of(t, core)
    aux = aux_ref[pl.ds(pl.multiple_of(t * Q, Q), Q), :]
    ch = p_ref[side, 0, rows, :width]
    prior = jnp.maximum(t - 1, 0)
    prev = p_ref[lax.rem(lax.div(prior, 2) + core, 2), 0, pl.ds(pl.multiple_of(lax.rem(prior, 2) * Q + Q - 8, 8), 8), :width]
    prev = prev * jnp.where(t == 0, 0.0, 1.0)
    conv, shifted = conv_of(ch, jnp.concatenate([prev, ch], 0), aux, par, width)
    sig = 1.0 / (1.0 + jnp.exp(-conv))
    act = conv * sig
    x_in, bm, cm = act[:, :inner], act[:, inner : inner + nst], act[:, inner + nst :]
    pre, dt, cum = rates(p_ref[side, 0, rows, width:], hp)
    low = iota((Q, 2 * head), 1) < head
    squares, dt_w, enter_w, leave_w, through_w = widen(cum, dt, aux, inner // head, low)
    xdt = x_in * dt_w
    scores = mm3(cm, bm, ((1,), (1,)))
    allowed = (iota((Q, Q), 0) >= iota((Q, Q), 1)) & (aux[:, 0:1] == seg_ref[t, 0:1, :])
    cum_t = cum.T
    bm = bm.astype(BF16)
    cm = cm.astype(BF16)
    dy = dy_ref[side, 0, rows, :]
    s_in = sin_ref[t]
    d_state = state[...]
    s_in_b = s_in.astype(BF16)
    d_state_b = d_state.astype(BF16)

    dye = (dy * enter_w).astype(BF16)
    inter = mm(cm, s_in_b) * enter_w
    from_state = mm(bm, d_state_b) * leave_w
    state[...] = mm(cm, dye, ((0,), (0,))) + through_w * d_state
    d_c = mm(dye, s_in_b, ((1,), (1,)))
    d_b = mm(xdt * leave_w, d_state_b, ((1,), (1,)))

    lane = iota((Q, Q), 1)
    sub = iota((8, Q), 0)
    d_scores = jnp.zeros((Q, Q), F32)
    row_sums = jnp.zeros((Q, Q), F32)
    col_sums = jnp.zeros((8, Q), F32)
    d_xdt = []
    for pair in range(inner // (2 * head)):
        cols = slice(2 * head * pair, 2 * head * (pair + 1))
        xp = xdt[:, cols]
        dyp = dy[:, cols]
        d_k2 = mm3(dyp, jnp.concatenate([jnp.where(low, xp, 0.0), jnp.where(low, 0.0, xp)], 0), ((1,), (1,)))
        kmats = []
        for k in range(2):
            h = 2 * pair + k
            decay = jnp.exp(jnp.where(allowed, squares[h] - cum_t[h : h + 1, :], NEG))
            d_k = d_k2[:, k * Q : (k + 1) * Q]
            kmat = scores * decay
            d_scores = d_scores + d_k * decay
            both = d_k * kmat
            row_sums = jnp.where(lane == h, jnp.sum(both, 1, keepdims=True), row_sums)
            col_sums = jnp.where(sub == h, jnp.sum(both, 0, keepdims=True), col_sums)
            kmats.append(kmat)
        dy_by_head = jnp.concatenate([jnp.where(low, dyp, 0.0), jnp.where(low, 0.0, dyp)], 0)
        d_xdt.append(mm3(jnp.concatenate(kmats, 0), dy_by_head, ((0,), (0,))))
    z = jnp.concatenate(d_xdt, 1) + from_state
    d_c = d_c + mm(d_scores, bm)
    d_b = d_b + mm(d_scores, cm, ((0,), (0,)))
    d_x = z * dt_w + par[6:7, :inner] * dy

    leaving = xdt * from_state
    ending = jnp.sum(s_in * d_state, 0, keepdims=True) * through_w + jnp.sum(leaving, 0, keepdims=True)
    folded = mm_fold(
        jnp.concatenate([x_in * z, dy * inter - leaving, jnp.broadcast_to(ending, (8, inner))], 0), gather_mat(inner, Q, head)
    )
    col_full = jnp.concatenate([col_sums, jnp.zeros((Q - 8, Q), F32)], 0).T
    d_cum = row_sums - col_full + folded[Q : 2 * Q]
    tri_up = (iota((Q, Q), 0) <= iota((Q, Q), 1)).astype(BF16)
    rev = mm_tri(tri_up, d_cum) + folded[2 * Q : 2 * Q + 1]
    d_dt = folded[:Q] - hp[1:2] * rev
    d_raw = d_dt / (1.0 + jnp.exp(-pre))
    live = (iota((1, Q), 1) < inner // head).astype(F32)
    d_raw = d_raw * live
    ghead_ref[0:1, :] += jnp.sum(d_raw, 0, keepdims=True)
    ghead_ref[1:2, :] += jnp.sum(rev * dt, 0, keepdims=True) * -hp[1:2]
    gskip_ref[0:1, :] += jnp.sum(dy * x_in, 0, keepdims=True)

    d_act = jnp.concatenate([d_x, d_b, d_c], 1)
    d_conv = d_act * (sig * (1.0 + conv * (1.0 - sig)))
    gconv_ref[4:5, :] += jnp.sum(d_conv, 0, keepdims=True)
    gconv_ref[3:4, :] += jnp.sum(d_conv * ch, 0, keepdims=True)
    d_ch = d_conv * par[3:4, :width]
    for s in range(1, 4):
        gconv_ref[3 - s : 4 - s, :] += jnp.sum(d_conv * shifted[s - 1], 0, keepdims=True)
        u = d_conv * aux[:, s : s + 1] * par[3 - s : 4 - s, :width]
        d_ch = d_ch + pltpu.roll(jnp.concatenate([u, rim[s - 1]], 0), Q + 8 - s, 0)[:Q]
        rim[s - 1] = u[:8]
    dp_ref[side, 0, rows, :width] = d_ch.astype(BF16)
    dp_ref[side, 0, rows, width:] = d_raw.astype(BF16)


def rows_spec(cols, first=0):
    return pl.BlockSpec((2, 1, CHUNKS * Q // 2, cols), lambda r, c: (0, r + first, 0, 0))


def common_specs(wide, width, first=0):
    return [
        rows_spec(wide, first),
        pl.BlockSpec((CHUNKS * Q, 128), lambda r, c: (r + first, 0)),
        pl.BlockSpec((CHUNKS, 8, Q), lambda r, c: (r + first, 0, 0)),
        pl.BlockSpec((8, width), lambda r, c: (0, 0)),
        pl.BlockSpec((8, 128), lambda r, c: (0, 0)),
    ]


def ssd_fwd(core, proj, aux, seg_rows, par, hp, *, inner, nst, head, interpret=False):
    seqs, half, wide = proj.shape[1:]
    rows = 2 * seqs * half
    width = inner + 2 * nst
    spec = pltpu.PrefetchScalarGridSpec(
        num_scalar_prefetch=1,
        grid=(seqs,),
        in_specs=common_specs(wide, width),
        out_specs=[rows_spec(inner), pl.BlockSpec((CHUNKS, nst, inner), lambda r, c: (r, 0, 0))],
        scratch_shapes=[pltpu.VMEM((8, width), F32), pltpu.VMEM((nst, inner), F32)],
    )
    y, s_in = pl.pallas_call(
        functools.partial(ssd_fwd_kernel, inner=inner, nst=nst, head=head),
        grid_spec=spec,
        out_shape=[
            jax.ShapeDtypeStruct((2, seqs, CHUNKS * Q // 2, inner), F32),
            jax.ShapeDtypeStruct((seqs * CHUNKS, nst, inner), F32),
        ],
        cost_estimate=pl.CostEstimate(flops=1, transcendentals=0, bytes_accessed=1),
        interpret=interpret,
        name="ssd_fwd",
        compiler_params=pltpu.CompilerParams(vmem_limit_bytes=14 << 20),
    )(core, proj, aux, seg_rows, par, hp)
    return y, s_in


def ssd_bwd(core, proj, aux, seg_rows, par, hp, dy, s_in, first, count, so_far, *, inner, nst, head, interpret=False):
    seqs, half, wide = proj.shape[1:]
    rows = 2 * seqs * half
    width = inner + 2 * nst
    out_specs = [
        rows_spec(wide, first),
        pl.BlockSpec((8, width), lambda r, c: (0, 0)),
        pl.BlockSpec((8, 128), lambda r, c: (0, 0)),
        pl.BlockSpec((8, inner), lambda r, c: (0, 0)),
    ]
    in_specs = common_specs(wide, width, first) + [
        rows_spec(inner, first),
        pl.BlockSpec((CHUNKS, nst, inner), lambda r, c: (r + first, 0, 0)),
    ]
    operands = (core, proj, aux, seg_rows, par, hp, dy, s_in)
    aliases = {}
    if so_far is not None:
        aliases = {len(operands) + i: i for i in range(4)}
        in_specs += [pl.BlockSpec(memory_space=pl.ANY)] + out_specs[1:]
        operands += tuple(so_far)
    spec = pltpu.PrefetchScalarGridSpec(
        num_scalar_prefetch=1,
        grid=(count,),
        in_specs=in_specs,
        out_specs=out_specs,
        scratch_shapes=[pltpu.VMEM((3, 8, width), F32), pltpu.VMEM((nst, inner), F32)],
    )
    return pl.pallas_call(
        functools.partial(ssd_bwd_kernel, inner=inner, nst=nst, head=head),
        grid_spec=spec,
        out_shape=[
            jax.ShapeDtypeStruct((2, seqs, CHUNKS * Q // 2, wide), BF16),
            jax.ShapeDtypeStruct((8, width), F32),
            jax.ShapeDtypeStruct((8, 128), F32),
            jax.ShapeDtypeStruct((8, inner), F32),
        ],
        input_output_aliases=aliases,
        cost_estimate=pl.CostEstimate(flops=1, transcendentals=0, bytes_accessed=1),
        interpret=interpret,
        name="ssd_bwd",
    )(*operands)


def masks_of(seg):
    s_count, length = seg.shape
    cols = [seg.astype(F32)]
    for s in range(1, 4):
        back = jnp.concatenate([jnp.full((s_count, s), -1, seg.dtype), seg[:, :-s]], 1)
        cols.append((back == seg).astype(F32))
    by_chunk = seg.reshape(s_count, length // Q, Q)
    last = by_chunk[:, :, -1:]
    prev = jnp.concatenate([jnp.full((s_count, 1, 1), -1, seg.dtype), last[:, :-1]], 1)
    cols.append((by_chunk == prev).astype(F32).reshape(s_count, length))
    cols.append((by_chunk == last).astype(F32).reshape(s_count, length))
    cols.append(jnp.broadcast_to(prev == last, by_chunk.shape).astype(F32).reshape(s_count, length))
    aux = jnp.stack(cols, -1).reshape(s_count * length, len(cols))
    aux = jnp.pad(aux, ((0, 0), (0, 128 - len(cols))))
    rows = jnp.broadcast_to(seg.astype(F32).reshape(-1, 1, Q), (s_count * length // Q, 8, Q))
    return aux, rows


EPS = 1e-05
AXES = ("z", "y", "x", "c")


def pull(a, axis, d):
    return lax.ppermute(a, axis, [((i + d) % 4, i) for i in range(4)])


def swap(a):
    return lax.ppermute(a, "c", [(0, 1), (1, 0)])


def transpose_zy(a):
    return lax.ppermute(a, ("z", "y"), [(4 * y + z, 4 * z + y) for z in range(4) for y in range(4)])


def ring(a):
    return tuple(pull(a, "z", d) for d in (1, 2, 3))


def ring_ends(a):
    return pull(a, "z", 1), pull(a, "z", 3)


def ring_middle(one, three):
    half = one.shape[0] // 2
    return pull(one[:half], "z", 1), pull(three[half:], "z", 3)


def ring_back(q):
    return tuple(pull(q[d], "z", 4 - d) for d in (1, 2, 3))


def plane_all(a):
    return lax.all_gather(a, ("y", "x"), axis=0)


def plane_all_small(a):
    return lax.all_to_all(jnp.broadcast_to(a[None], (16,) + a.shape), ("y", "x"), 0, 0)


def tie(*values):
    return lax.optimization_barrier(values)


def two_terms(a):
    top = lax.reduce_precision(a, 8, 7)
    return top.astype(BF16), (a - top).astype(BF16)


def after(value, *others):
    return lax.optimization_barrier((value,) + others)[0]


def cost(flops, bytes_accessed):
    return pl.CostEstimate(flops=1, transcendentals=0, bytes_accessed=1)


def whole(shape):
    return pl.BlockSpec(shape, lambda *_: (0,) * len(shape))


PER = 2


def near_spec(rows, cols):
    return pl.BlockSpec((PER, rows, cols), lambda h, r: (jnp.where(h == 0, r, 4 // PER - 1), 0, 0))


def far_spec(rows, cols):
    return pl.BlockSpec((PER, rows, cols), lambda h, r: (jnp.where(h == 0, 0, r), 0, 0))


def block_spec(cols, rows=256):
    return pl.BlockSpec((1, PER, rows, cols), lambda h, r: (h, r, 0, 0))


def flat_rows(ref):
    v = ref[0] if len(ref.shape) == 4 else ref[...]
    return v.reshape(v.shape[0] * v.shape[1], v.shape[2])


def put_rows(ref, v):
    if len(ref.shape) == 4:
        ref[0] = v.reshape(ref.shape[1:])
    else:
        ref[...] = v.reshape(ref.shape)


def half_cols(core, width):
    return pl.ds(pl.multiple_of(core * width, width), width), pl.ds(pl.multiple_of((1 - core) * width, width), width)


def enter_kernel(near_ref, far_ref, gain_ref, w_ref, normed_ref, proj_ref):
    def step(ref):
        p = flat_rows(ref).astype(F32)
        inverse = lax.rsqrt(jnp.mean(p * p, -1, keepdims=True) + EPS)
        normed = (p * inverse * gain_ref[...]).astype(BF16)
        put_rows(normed_ref, normed)
        put_rows(proj_ref, jnp.dot(normed, w_ref[...], preferred_element_type=F32))

    pl.when(pl.program_id(0) == 0)(lambda: step(near_ref))
    pl.when(pl.program_id(0) == 1)(lambda: step(far_ref))


def enter(near, far, gain, w):
    padded, model = near.shape[1:]
    rows, cols = 256, w.shape[1]
    return pl.pallas_call(
        enter_kernel,
        grid=(2, 4 // PER),
        out_shape=[jax.ShapeDtypeStruct((2, 4, rows, model), BF16), jax.ShapeDtypeStruct((2, 4, rows, cols), F32)],
        in_specs=[near_spec(padded, model), far_spec(padded, model), whole((1, model)), whole(w.shape)],
        out_specs=[block_spec(model), block_spec(cols)],
        cost_estimate=cost(16 * rows * model * cols, 8 * rows * (4 * model + 4 * cols)),
        name="enter",
        compiler_params=pltpu.CompilerParams(vmem_limit_bytes=24 << 20),
    )(near, far, gain, w)


def gate_kernel(core_ref, normed_ref, near_ref, far_ref, wg_ref, wo_ref, wt_ref, y_ref, gain_ref, gate_ref, dm_ref, sums_ref):
    gate = jnp.dot(flat_rows(normed_ref), wg_ref[...], preferred_element_type=F32)
    here, there = half_cols(core_ref[0], wo_ref.shape[1])
    dims = (((1,), (1,)), ((), ()))

    def back(cot_ref):
        rows = gate.shape[0]
        a = cot_ref[:, :, here].reshape(rows, wo_ref.shape[1])
        b = cot_ref[:, :, there].reshape(rows, wo_ref.shape[1])
        put_rows(
            dm_ref,
            lax.dot_general(a, wo_ref[...], dims, preferred_element_type=F32)
            + lax.dot_general(b, wt_ref[...], dims, preferred_element_type=F32),
        )

    pl.when(pl.program_id(0) == 0)(lambda: back(near_ref))
    pl.when(pl.program_id(0) == 1)(lambda: back(far_ref))
    d_mixed = flat_rows(dm_ref)
    put_rows(gate_ref, gate)
    gated = flat_rows(y_ref) * gate / (1.0 + jnp.exp(-gate))
    ones = jnp.ones((8, gate.shape[1]), BF16)

    def total(v):
        top, low = halves(v)
        return (mm(ones, top, ((1,), (1,))) + mm(ones, low, ((1,), (1,))))[:1]

    both = jnp.concatenate([total(gated * gated), total(d_mixed * gain_ref[...] * gated)], 0)
    rows = sums_ref.shape[3]
    for q in range(PER):
        sums_ref[0, q] = both[:, q * rows : (q + 1) * rows]


def gate_stage(core, normed, near, far, w_g, w_o, w_t, y, gain):
    rows, model = normed.shape[2:]
    mine = w_g.shape[1]
    return pl.pallas_call(
        gate_kernel,
        grid=(2, 4 // PER),
        out_shape=[jax.ShapeDtypeStruct((2, 4, rows, mine), F32)] * 2 + [jax.ShapeDtypeStruct((2, 4, 2, rows), F32)],
        in_specs=[
            pl.BlockSpec(memory_space=pltpu.SMEM),
            block_spec(model),
            near_spec(rows, model),
            far_spec(rows, model),
            whole(w_g.shape),
            whole(w_o.shape),
            whole(w_t.shape),
            block_spec(mine),
            whole((1, mine)),
        ],
        out_specs=[block_spec(mine), block_spec(mine), block_spec(rows, 2)],
        cost_estimate=cost(32 * rows * model * mine, 8 * rows * (4 * model + 12 * mine)),
        name="gate_stage",
    )(core, normed, near, far, w_g, w_o, w_t, y, gain)


def turn_kernel(
    core_ref, normed_ref, near_ref, far_ref, wo_ref, wt_ref, y_ref, gate_ref, dm_ref, sums_ref, gain_ref,
    out_near_ref, out_far_ref, dy_ref, dgate_ref, keep_ref, send_ref, ggate_ref, ggain_ref, acc_o, acc_g, *, inner,
):
    h, r = pl.program_id(0), pl.program_id(1)
    rows = gate_ref.shape[2]
    gate, d_mixed, y, gain = flat_rows(gate_ref), flat_rows(dm_ref), flat_rows(y_ref), gain_ref[...]
    sums = jnp.concatenate(
        [jnp.concatenate([sums_ref[0, q], jnp.zeros((6, rows), F32)], 0).T for q in range(PER)], 0
    )
    scale = lax.rsqrt(sums[:, 0:1] / inner + EPS)
    lean = sums[:, 1:2] / inner * scale * scale
    sig = 1.0 / (1.0 + jnp.exp(-gate))
    act = gate * sig
    gated = y * act
    mixed = (gated * scale * gain).astype(BF16)
    d_gated = scale * (d_mixed * gain - gated * lean)
    put_rows(dy_ref, d_gated * act)
    d_gate = (d_gated * y * (sig * (1.0 + gate * (1.0 - sig)))).astype(BF16)
    put_rows(dgate_ref, d_gate)
    here, there = half_cols(core_ref[0], wo_ref.shape[1])

    def forward(out_ref, cot_ref):
        shape = out_ref.shape[:2] + (wo_ref.shape[1],)
        out_ref[:, :, here] = jnp.dot(mixed, wo_ref[...], preferred_element_type=F32).astype(BF16).reshape(shape)
        out_ref[:, :, there] = jnp.dot(mixed, wt_ref[...], preferred_element_type=F32).astype(BF16).reshape(shape)
        acc_o[...] += lax.dot_general(mixed, flat_rows(cot_ref), (((0,), (0,)), ((), ())), preferred_element_type=F32)

    @pl.when((h == 0) & (r == 0))
    def _():
        acc_o[...] = jnp.zeros_like(acc_o)
        acc_g[...] = jnp.zeros_like(acc_g)
        ggain_ref[...] = jnp.zeros_like(ggain_ref)

    ggain_ref[0:1, :] += jnp.sum(d_mixed * gated * scale, 0, keepdims=True)
    pl.when(h == 0)(lambda: forward(out_near_ref, near_ref))
    pl.when(h == 1)(lambda: forward(out_far_ref, far_ref))
    acc_g[...] += lax.dot_general(flat_rows(normed_ref), d_gate, (((0,), (0,)), ((), ())), preferred_element_type=F32)

    @pl.when((h == 1) & (r == pl.num_programs(1) - 1))
    def _():
        keep_ref[...] = acc_o[:, here].astype(BF16)
        send_ref[...] = acc_o[:, there].astype(BF16)
        ggate_ref[:, :, : acc_g.shape[1]] = acc_g[...].astype(BF16).reshape(16, -1, acc_g.shape[1])


def turn_stage(core, normed, near, far, w_o, w_t, y, gate, d_mixed, sums, gain, inner):
    rows, model = normed.shape[2:]
    mine = w_o.shape[0]
    blocks = (16, model // 16, 2 * mine)
    return pl.pallas_call(
        functools.partial(turn_kernel, inner=inner),
        grid=(2, 4 // PER),
        out_shape=[
            jax.ShapeDtypeStruct((4, rows, model), BF16),
            jax.ShapeDtypeStruct((4, rows, model), BF16),
            jax.ShapeDtypeStruct((2, 4, rows, mine), F32),
            jax.ShapeDtypeStruct((2, 4, rows, mine), BF16),
            jax.ShapeDtypeStruct(w_o.shape, BF16),
            jax.ShapeDtypeStruct(w_o.shape, BF16),
            jax.ShapeDtypeStruct(blocks, BF16),
            jax.ShapeDtypeStruct((8, mine), F32),
        ],
        in_specs=[
            pl.BlockSpec(memory_space=pltpu.SMEM),
            block_spec(model),
            near_spec(rows, model),
            far_spec(rows, model),
            whole(w_o.shape),
            whole(w_o.shape),
            block_spec(mine),
            block_spec(mine),
            block_spec(mine),
            block_spec(rows, 2),
            whole((1, mine)),
        ],
        out_specs=[
            near_spec(rows, model),
            far_spec(rows, model),
            block_spec(mine),
            block_spec(mine),
            whole(w_o.shape),
            whole(w_o.shape),
            whole(blocks),
            whole((8, mine)),
        ],
        scratch_shapes=[pltpu.VMEM((mine, model), F32), pltpu.VMEM((model, mine), F32)],
        cost_estimate=cost(48 * rows * model * mine, 8 * rows * (6 * model + 18 * mine)),
        name="turn_stage",
    )(core, normed, near, far, w_o, w_t, y, gate, d_mixed, sums, gain)


def back_kernel(dp_ref, wa_ref, dg_ref, wg_ref, near_ref, far_ref):
    t = lax.dot_general(flat_rows(dp_ref), wa_ref[...], (((1,), (1,)), ((), ())), preferred_element_type=F32)
    t = t + lax.dot_general(flat_rows(dg_ref), wg_ref[...], (((1,), (1,)), ((), ())), preferred_element_type=F32)
    pl.when(pl.program_id(0) == 0)(lambda: put_rows(near_ref, t.astype(BF16)))
    pl.when(pl.program_id(0) == 1)(lambda: put_rows(far_ref, t.astype(BF16)))


def back_dot(d_proj, w_a, d_gate, w_g):
    rows, ka = d_proj.shape[2:]
    m, kg = w_g.shape
    return pl.pallas_call(
        back_kernel,
        grid=(2, 4 // PER),
        out_shape=[jax.ShapeDtypeStruct((4, rows, m), BF16)] * 2,
        in_specs=[block_spec(ka), whole((m, ka)), block_spec(kg), whole((m, kg))],
        out_specs=[near_spec(rows, m), far_spec(rows, m)],
        cost_estimate=cost(0, 0),
        name="back_dot",
    )(d_proj, w_a, d_gate, w_g)


def unpack_kernel(core_ref, all_ref, wg_ref, mine_ref, send_ref):
    rows, width = all_ref.shape[1:]
    part, cols = rows // 2, wg_ref.shape[1]
    for k in range(16):
        wg_ref[k * rows : (k + 1) * rows, :] = all_ref[k, :, :cols]

    def move(ref, side):
        for x in (2 * side, 2 * side + 1):
            for y in range(4):
                at = (4 * (x % 2) + y) * part
                for k in range(2):
                    piece = all_ref[4 * y + x, k * part : (k + 1) * part, cols:]
                    ref[at : at + part, k * (width - cols) : (k + 1) * (width - cols)] = piece

    for core in range(2):

        @pl.when(core_ref[0] == core)
        def _():
            move(mine_ref, core)
            move(send_ref, 1 - core)


def unpack(core, gathered, cols):
    _, rows, width = gathered.shape
    half = jax.ShapeDtypeStruct((4 * rows, 2 * (width - cols)), BF16)
    return pl.pallas_call(
        unpack_kernel,
        in_specs=[pl.BlockSpec(memory_space=pltpu.SMEM), whole(gathered.shape)],
        out_specs=[whole((16 * rows, cols)), whole(half.shape), whole(half.shape)],
        grid=(1,),
        out_shape=[jax.ShapeDtypeStruct((16 * rows, cols), BF16), half, half],
        cost_estimate=cost(0, 0),
        name="unpack",
    )(core, gathered)


def pack_kernel(core_ref, gate_ref, keep_ref, got_ref, out_ref):
    del gate_ref
    rows, width = out_ref.shape[1:]
    part = rows // 2

    def move(ref, side):
        for x in (2 * side, 2 * side + 1):
            for y in range(4):
                at = (4 * (x % 2) + y) * part
                for k in range(2):
                    out_ref[4 * y + x, k * part : (k + 1) * part, :] = ref[at : at + part, k * width : (k + 1) * width]

    for core in range(2):

        @pl.when(core_ref[0] == core)
        def _():
            move(keep_ref, core)
            move(got_ref, 1 - core)


def pack(core, g_gate, keep, got):
    _, rows, width = g_gate.shape
    return pl.pallas_call(
        pack_kernel,
        in_specs=[
            pl.BlockSpec(memory_space=pltpu.SMEM),
            pl.BlockSpec(memory_space=pl.ANY),
            whole(keep.shape),
            whole(got.shape),
        ],
        out_specs=pl.BlockSpec((16, rows, width // 2), lambda *_: (0, 0, 1)),
        grid=(1,),
        out_shape=jax.ShapeDtypeStruct(g_gate.shape, BF16),
        input_output_aliases={1: 0},
        cost_estimate=cost(0, 0),
        name="pack",
    )(core, g_gate, keep, got)


def assemble_kernel(
    at_ref, near_ref, far_ref, win_ref, gain_ref, gwin_ref, gwo_ref, norm_ref, convw_ref, convb_ref, dtb_ref, alog_ref,
    skip_ref, outg_ref, conv_ref, wide_ref, *, mine, nst, my_heads,
):
    z, core, shard = at_ref[0], at_ref[1], at_ref[2]
    rows, wide = win_ref.shape
    inner = 8 * mine
    part = gwo_ref.shape[0] // 4
    width = mine + 2 * nst + 128
    bc = jnp.zeros((rows, 2 * nst), F32)
    conv_bc = jnp.zeros((8, 2 * nst), F32)
    heads = jnp.zeros((8, 128), F32)
    width_c = mine + 2 * nst
    raw = jnp.zeros((rows, 128), F32)
    lane = iota((rows, 128), 1)
    for zz in range(4):
        r = lax.rem(zz - z + 4, 4)
        for cc in range(2):
            j = 2 * zz + cc
            both = jnp.where(core == cc, near_ref[r].astype(F32), far_ref[r].astype(F32))
            v = both[rows : rows + 8] + both[rows + 8 : rows + 16]
            conv_ref[:, j * mine : (j + 1) * mine] = v[:, :mine]
            conv_bc = conv_bc + v[:, mine:width_c]
            h = jnp.where(iota((8, 128), 1) < my_heads, v[:, width_c : width_c + 128], 0.0)
            heads = heads + (pltpu.roll(h, j * my_heads, 1) if j else h)
            wide_ref[0:1, j * mine : (j + 1) * mine] = v[0:1, width_c + 128 : width_c + 128 + mine]
            wide_ref[1:2, j * mine : (j + 1) * mine] = v[0:1, width_c + 128 + mine :]
            both = both[:rows]
            a, b = both[:, :width], both[:, width:]
            gwin_ref[:, j * mine : (j + 1) * mine] = b[:, :mine]
            gwin_ref[:, inner + j * mine : inner + (j + 1) * mine] = a[:, :mine]
            bc = bc + a[:, mine : mine + 2 * nst]
            piece = a[:, mine + 2 * nst :]
            piece = jnp.where(lane < my_heads, piece, 0.0)
            raw = raw + (pltpu.roll(piece, j * my_heads, 1) if j else piece)
            for k in range(2):
                cols = (2 * cc + k) * (b.shape[1] - mine)
                gwo_ref[zz * part : (zz + 1) * part, cols : cols + b.shape[1] - mine] = b[k * part : (k + 1) * part, mine:]
    gwin_ref[:, 2 * inner : 2 * inner + 2 * nst] = bc
    gwin_ref[:, 2 * inner + 2 * nst :] = raw[:, : wide - 2 * inner - 2 * nst]
    conv_ref[:, inner:] = conv_bc
    k, kn, hn = convb_ref.shape[1], outg_ref.shape[1], dtb_ref.shape[1]

    def own(v, count):
        total = v.shape[1]
        return pltpu.roll(v, lax.rem(total - shard * count, total), 1)[:, :count]

    conv = own(conv_ref[...], k)
    convw_ref[...] = conv[:4]
    convb_ref[...] = conv[4:5]
    wide_own = own(wide_ref[...], kn)
    outg_ref[...] = wide_own[1:2]
    per = kn // hn
    skips = [jnp.sum(wide_own[0:1, i * per : (i + 1) * per], 1, keepdims=True) for i in range(hn)]
    skip_ref[...] = jnp.concatenate(skips, 1)
    heads = pltpu.roll(heads, lax.rem(128 - shard * hn, 128), 1)
    dtb_ref[...] = heads[0:1, :hn]
    alog_ref[...] = heads[1:2, :hn]
    norm = jnp.sum(gwin_ref[...] * win_ref[...].astype(F32), 1, keepdims=True)
    norm_ref[...] = jnp.broadcast_to(norm, (rows, 128)).T[0:1, :] / gain_ref[...].astype(F32)


def assemble(z, core, shard, near, far, w_in, norm_gain, w_out, k, kn, hn, mine, nst, my_heads):
    at = jnp.stack([z, core[0], shard]).astype(jnp.int32)
    arrays = (near, far, w_in, norm_gain[None])
    shapes = [w_in.shape, w_out.shape, (1, w_in.shape[0]), (4, k), (1, k), (1, hn), (1, hn), (1, hn), (1, kn)]
    return pl.pallas_call(
        functools.partial(assemble_kernel, mine=mine, nst=nst, my_heads=my_heads),
        in_specs=[pl.BlockSpec(memory_space=pltpu.SMEM)] + [whole(a.shape) for a in arrays],
        out_specs=[whole(a) for a in shapes],
        grid=(1,),
        out_shape=[jax.ShapeDtypeStruct(a, F32) for a in shapes],
        scratch_shapes=[pltpu.VMEM((8, 8 * mine + 2 * nst), F32), pltpu.VMEM((2, 8 * mine), F32)],
        cost_estimate=cost(0, 0),
        name="assemble",
    )(at, *arrays)


def dot(a, b, dims):
    return lax.dot_general(a, b, (dims, ((), ())), preferred_element_type=F32)


def local(inputs, segments, norm_gain, w_in, conv_w, conv_b, dt_bias, a_log, d_skip, out_gain, w_out, cotangent):
    z, y, x, c = (lax.axis_index(name) for name in AXES)
    member = 2 * z + c
    length, model = inputs.shape[1:]
    inner = 16 * out_gain.shape[0]
    heads = 16 * d_skip.shape[0]
    xwidth = 16 * conv_b.shape[0]
    nst = (xwidth - inner) // 2
    head = inner // heads
    mine = inner // 8
    my_heads = heads // 8
    core = c.astype(jnp.int32).reshape(1)
    rows_in = w_in.shape[0]

    w_x = lax.dynamic_slice_in_dim(w_in, inner + member * mine, mine, 1)
    w_dt = jnp.pad(
        lax.dynamic_slice_in_dim(w_in[:, inner + xwidth :], member * my_heads, my_heads, 1), ((0, 0), (0, 128 - my_heads))
    )
    w_bc = jnp.concatenate([w_in[:, inner + mine * 8 : inner + xwidth], w_dt], 1)
    block_a = jnp.concatenate([w_x, w_bc], 1)
    all_a = plane_all(block_a)
    w_a = all_a.reshape(model, -1)

    def lanes(a):
        return jnp.pad(a, ((0, 0), (0, -a.shape[1] % 128))).reshape(-1, 128)

    tiny = jnp.concatenate([dt_bias, a_log, d_skip])[None]
    small = jnp.concatenate([lanes(conv_w), lanes(conv_b[None]), lanes(out_gain[None]), lanes(norm_gain[None]), lanes(tiny)], 0)
    small = after(jnp.pad(small, ((0, -small.shape[0] % 16), (0, 0))), block_a)

    x_mine = inputs[0]
    one, three = ring_ends(x_mine)
    middle = ring_middle(one, three)
    seg_mine = after(segments.reshape(-1, 128), block_a)
    seg_all = jnp.stack((seg_mine,) + ring(seg_mine)).reshape(4, -1)
    aux, seg_rows = masks_of(seg_all)

    small = plane_all_small(small).astype(F32)
    k, kn, hn = conv_b.shape[0], out_gain.shape[0], d_skip.shape[0]
    lk, lg = -(-k // 128), -(-kn // 128)
    conv_wf = small[:, : 4 * lk].reshape(16, 4, lk * 128)[:, :, :k].transpose(1, 0, 2).reshape(4, xwidth)
    conv_bf = small[:, 4 * lk : 5 * lk].reshape(16, lk * 128)[:, :k].reshape(1, xwidth)
    gain_f = small[:, 5 * lk : 5 * lk + lg].reshape(16, lg * 128)[:, :kn].reshape(-1)
    norm_f = small[:, 5 * lk + lg, :rows_in].reshape(-1)
    dtb_f, alog_f, skip_f = (small[:, 5 * lk + lg + 1, i * hn : (i + 1) * hn].reshape(-1) for i in range(3))

    def own(a, count):
        return lax.dynamic_slice_in_dim(a, member * count, count, a.ndim - 1)

    conv_all = jnp.concatenate([conv_wf, conv_bf], 0)
    conv_mine = jnp.concatenate([own(conv_all[:, :inner], mine), conv_all[:, inner:]], 1)
    skip_mine = jnp.repeat(own(skip_f, my_heads), head)
    par = jnp.concatenate(
        [conv_mine, jnp.zeros((1, mine + 2 * nst), F32), jnp.pad(skip_mine, (0, 2 * nst))[None], jnp.zeros((1, mine + 2 * nst), F32)], 0
    )
    rates_mine = jnp.stack([own(dtb_f, my_heads), jnp.exp(own(alog_f, my_heads))])
    hp = jnp.pad(rates_mine, ((0, 6), (0, 128 - my_heads)))
    gain_mine = own(gain_f, mine)[None]

    w_g = lax.dynamic_slice_in_dim(w_in, member * mine, mine, 1)
    part = w_out.shape[0] // 4
    half = model // 2
    wo_piece = lax.dynamic_slice(w_out, (z * part, c * half), (part, half))
    wo_piece = transpose_zy(jnp.concatenate([wo_piece[:, : half // 2], wo_piece[:, half // 2 :]], 0))
    block_b = jnp.concatenate([w_g, wo_piece], 1)
    middle, block_b, norm_row, par, hp, gain_mine, aux, seg_rows = tie(
        middle, block_b, norm_f[None], par, hp, gain_mine, aux, seg_rows
    )
    all_b = plane_all(block_b)
    x_near = jnp.stack([x_mine, one, jnp.concatenate(middle, 0), three])
    x_far = swap(x_near)
    cot_ring = ring(after(cotangent[0], x_near))

    sizes_k = dict(inner=mine, nst=nst, head=head)
    normed, proj = enter(x_near, x_far, norm_row, w_a)
    mixed_ssd, s_in = ssd_fwd(core, proj, aux, seg_rows, par, hp, **sizes_k)
    mixed_ssd, cot_ring = tie(mixed_ssd, cot_ring)
    cot_near = jnp.stack((cotangent[0],) + cot_ring)
    cot_far = swap(cot_near)
    all_b = after(all_b, cot_near)
    w_g, w_o, w_t = unpack(core, all_b, mine)
    w_t = swap(w_t)
    gate, d_mixed, sums = gate_stage(core, normed, cot_near, cot_far, w_g, w_o, w_t, mixed_ssd, gain_mine)
    sums = sums + jnp.flip(swap(sums), 0)
    sums = sums + sum(jnp.roll(pull(sums, "z", d), d, 1) for d in (1, 2, 3))
    out_near, out_far, d_y, d_gate, wo_keep, wo_send, g_gate, g_gain = turn_stage(
        core, normed, cot_near, cot_far, w_o, w_t, mixed_ssd, gate, d_mixed, sums, gain_mine, inner
    )

    def core_sum(near, far):
        far = swap(far)
        return [(near[i].astype(F32) + far[i].astype(F32)).astype(BF16) for i in range(4)]

    def core_sum_whole(near, far):
        return (near.astype(F32) + swap(far).astype(F32)).astype(BF16)

    backward = functools.partial(ssd_bwd, core, proj, aux, seg_rows, par, hp, d_y, s_in, **sizes_k)
    so_far, wo_got = tie(backward(0, 1, None), swap(wo_send))
    g_b = pack(core, g_gate, wo_keep, wo_got)
    all_b = lax.all_to_all(g_b, ("y", "x"), 0, 0)
    so_far, out_both = tie(after(so_far, g_b), core_sum(out_near, out_far))
    out_ring = ring_back(out_both)
    d_proj, g_conv, g_head, g_skip = backward(1, 3, so_far)
    raw = jnp.pad(jnp.concatenate([g_conv, g_head, g_skip, g_gain], 1), ((0, 16), (0, 0)))
    d_proj, raw = tie(d_proj, raw)
    raw = jnp.sum(lax.all_gather(raw, ("y", "x"), axis=0), 0)[:8]
    d_near, d_far = back_dot(d_proj, w_a, d_gate, w_g)
    d_proj, d_far, d_near, all_b, out_ring = tie(d_proj, d_far, d_near, all_b, out_ring)
    flat = 8 * length
    g_a = dot(normed.reshape(flat, model), d_proj.reshape(flat, -1), ((0,), (0,))).astype(BF16)
    sum_b = jnp.sum(all_b.astype(F32), 0).astype(BF16)

    g_a, d_both = tie(g_a, core_sum_whole(d_near, d_far))
    all_sums = lax.all_to_all(g_a.reshape(16, rows_in, -1), ("y", "x"), 0, 0)
    d_ring = ring_back(d_both)
    wo_sum = transpose_zy(sum_b[:, mine:])
    output = (x_mine.astype(F32) + sum(p.astype(F32) for p in (out_both[0],) + out_ring)).astype(BF16)

    all_sums, wo_sum, raw, d_ring = tie(all_sums, wo_sum, raw, d_ring)
    last = jnp.concatenate([jnp.sum(all_sums.astype(F32), 0).astype(BF16), sum_b[:, :mine], wo_sum], 1)
    last = jnp.concatenate([last, *two_terms(raw)], 0)
    last_ring = ring(last)
    d_normed = sum(p.astype(F32) for p in (d_both[0],) + d_ring)
    x_f = x_mine.astype(F32)
    inverse = lax.rsqrt(jnp.mean(x_f * x_f, -1, keepdims=True) + EPS)
    scaled = x_f * inverse
    d_hat = d_normed * norm_f[None]
    d_x = inverse * (d_hat - scaled * jnp.mean(d_hat * scaled, -1, keepdims=True))
    input_grad = (cotangent[0].astype(F32) + d_x).astype(BF16)

    last_ring, input_grad = tie(last_ring, input_grad)
    near = jnp.stack((last,) + last_ring)
    shard = 4 * y + x
    w_in_grad, w_out_grad, *others = assemble(
        z, core, shard, near, swap(near), w_in, norm_gain, w_out, k, kn, hn, mine, nst, my_heads
    )
    norm_gain_grad, conv_w_grad = others[0][0], others[1]
    conv_b_grad, dt_bias_grad, a_log_grad, d_skip_grad, out_gain_grad = (o[0] for o in others[2:])
    return (
        output[None],
        input_grad[None],
        norm_gain_grad,
        w_in_grad,
        conv_w_grad,
        conv_b_grad,
        dt_bias_grad,
        a_log_grad,
        d_skip_grad,
        out_gain_grad,
        w_out_grad,
    )


def solution(mesh):
    cube = Mesh(mesh.devices.reshape(4, 4, 4, 2), AXES)
    rows, shard = P(("z", "y", "x"), "c", None), ("y", "x")
    return jax.shard_map(
        local,
        mesh=cube,
        in_specs=(
            rows,
            P(("z", "y", "x"), None),
            P(shard),
            P(shard, None),
            P(None, shard),
            P(shard),
            P(shard),
            P(shard),
            P(shard),
            P(shard),
            P(shard, None),
            rows,
        ),
        out_specs=(
            rows,
            rows,
            P(shard),
            P(shard, None),
            P(None, shard),
            P(shard),
            P(shard),
            P(shard),
            P(shard),
            P(shard),
            P(shard, None),
        ),
        check_vma=False,
    )
```

```python
import functools
import jax
import jax.numpy as jnp
from jax import lax
from jax.experimental import pallas as pl
from jax.experimental.pallas import tpu as pltpu
from jax.sharding import Mesh, PartitionSpec as P

F32 = jnp.float32
BF16 = jnp.bfloat16
Q = 128
CHUNKS = 4
NEG = -1e30


def mm(a, b, dims=((1,), (0,))):
    return lax.dot_general(a.astype(BF16), b.astype(BF16), (dims, ((), ())), preferred_element_type=F32)


def halves(a):
    top = a.astype(BF16)
    return top, (a - top.astype(F32)).astype(BF16)


def mm3(a, b, dims=((1,), (0,))):
    a_top, a_low = halves(a)
    b_top, b_low = halves(b)
    return mm(a_top, b_top, dims) + (mm(a_low, b_top, dims) + mm(a_top, b_low, dims))


def mm_fold(a, b):
    top, low = halves(a)
    return mm(top, b) + mm(low, b)


def mm_tri(tri, b):
    return mm(jnp.concatenate([tri, tri], 1), jnp.concatenate(halves(b), 0))


def iota(shape, axis):
    return lax.broadcasted_iota(jnp.int32, shape, axis)


def gather_mat(width, cols, head):
    return (iota((width, cols), 0) // head == iota((width, cols), 1)).astype(BF16)


def conv_of(ch, ext, aux, par, width):
    conv = ch * par[3:4, :width] + par[4:5, :width]
    shifted = []
    for s in range(1, 4):
        sh = pltpu.roll(ext, s, 0)[8:] * aux[:, s : s + 1]
        shifted.append(sh)
        conv = conv + par[3 - s : 4 - s, :width] * sh
    return conv, shifted


def softplus(v):
    return jnp.maximum(v, 0.0) + jnp.log1p(jnp.exp(-jnp.abs(v)))


def rates(raw, hp):
    pre = raw + hp[0:1]
    dt = softplus(pre)
    tri = (iota((Q, Q), 0) >= iota((Q, Q), 1)).astype(BF16)
    return pre, dt, mm_tri(tri, -hp[1:2] * dt)


def widen(cum, dt, aux, heads, low):
    squares = [jnp.broadcast_to(cum[:, h : h + 1], (Q, Q)) for h in range(heads)]
    pairs = range(0, heads, 2)
    cum_w = jnp.concatenate([jnp.where(low, squares[h], squares[h + 1]) for h in pairs], 1)
    dt_w = jnp.concatenate([jnp.where(low, dt[:, h : h + 1], dt[:, h + 1 : h + 2]) for h in pairs], 1)
    fin_w = cum_w[Q - 1 : Q]
    enter_w = jnp.exp(cum_w) * aux[:, 4:5]
    leave_w = jnp.exp(fin_w - cum_w) * aux[:, 5:6]
    through_w = jnp.exp(fin_w) * aux[0:1, 6:7]
    return squares, dt_w, enter_w, leave_w, through_w


def ssd_fwd_kernel(c_ref, p_ref, aux_ref, seg_ref, par_ref, hp_ref, y_ref, sin_ref, rim, state, *, inner, nst, head):
    width = inner + 2 * nst
    state[...] = jnp.zeros_like(state)
    rim[...] = jnp.zeros_like(rim)
    par = par_ref[...]
    hp = hp_ref[...]
    core = c_ref[0]
    lax.fori_loop(0, CHUNKS, lambda t, _: ssd_fwd_chunk(t, core, p_ref, aux_ref, seg_ref, par, hp, y_ref, sin_ref, rim, state, inner, nst, head), None)


def place_of(t, core):
    return lax.rem(lax.div(t, 2) + core, 2), pl.ds(pl.multiple_of(lax.rem(t, 2) * Q, Q), Q)


def ssd_fwd_chunk(t, core, p_ref, aux_ref, seg_ref, par, hp, y_ref, sin_ref, rim, state, inner, nst, head):
    width = inner + 2 * nst
    side, rows = place_of(t, core)
    aux = aux_ref[pl.ds(pl.multiple_of(t * Q, Q), Q), :]
    ch = p_ref[side, 0, rows, :width]
    conv, _ = conv_of(ch, jnp.concatenate([rim[...], ch], 0), aux, par, width)
    rim[...] = ch[Q - 8 :]
    act = conv / (1.0 + jnp.exp(-conv))
    x_in, bm, cm = act[:, :inner], act[:, inner : inner + nst], act[:, inner + nst :]
    pre, dt, cum = rates(p_ref[side, 0, rows, width:], hp)
    low = iota((Q, 2 * head), 1) < head
    squares, dt_w, enter_w, leave_w, through_w = widen(cum, dt, aux, inner // head, low)
    xdt = x_in * dt_w
    scores = mm3(cm, bm, ((1,), (1,)))
    allowed = (iota((Q, Q), 0) >= iota((Q, Q), 1)) & (aux[:, 0:1] == seg_ref[t, 0:1, :])
    cum_t = cum.T
    s_old = state[...]
    sin_ref[t] = s_old
    result = enter_w * mm(cm, s_old) + par[6:7, :inner] * x_in
    for pair in range(inner // (2 * head)):
        cols = slice(2 * head * pair, 2 * head * (pair + 1))
        xp = xdt[:, cols].astype(BF16)
        none = jnp.zeros_like(xp)
        mixing = []
        for h in (2 * pair, 2 * pair + 1):
            decay = jnp.exp(jnp.where(allowed, squares[h] - cum_t[h : h + 1, :], NEG))
            mixing.append((scores * decay).astype(BF16))
        by_head = jnp.concatenate([jnp.where(low, xp, none), jnp.where(low, none, xp)], 0)
        y_ref[side, 0, rows, cols] = result[:, cols] + mm(jnp.concatenate(mixing, 1), by_head)
    state[...] = through_w * s_old + mm(bm, xdt * leave_w, ((0,), (0,)))


def ssd_bwd_kernel(c_ref, p_ref, aux_ref, seg_ref, par_ref, hp_ref, dy_ref, sin_ref, *refs, inner, nst, head):
    starts_given = len(refs) > 6
    starts = refs[1:4] if starts_given else (None,) * 3
    dp_ref, gconv_ref, ghead_ref, gskip_ref, rim, state = refs[-6:]
    core = c_ref[0]
    state[...] = jnp.zeros_like(state)
    rim[...] = jnp.zeros_like(rim)

    @pl.when(pl.program_id(0) == 0)
    def _():
        for ref, start in zip((gconv_ref, ghead_ref, gskip_ref), starts):
            ref[...] = start[...] if starts_given else jnp.zeros_like(ref)

    par = par_ref[...]
    hp = hp_ref[...]
    lax.fori_loop(
        0,
        CHUNKS,
        lambda t, _: ssd_bwd_chunk(
            CHUNKS - 1 - t, core, p_ref, aux_ref, seg_ref, par, hp, dy_ref, sin_ref, dp_ref, gconv_ref, ghead_ref, gskip_ref, rim, state, inner, nst, head
        ),
        None,
    )


def ssd_bwd_chunk(
    t, core, p_ref, aux_ref, seg_ref, par, hp, dy_ref, sin_ref, dp_ref, gconv_ref, ghead_ref, gskip_ref, rim, state, inner, nst, head
):
    width = inner + 2 * nst
    side, rows = place_of(t, core)
    aux = aux_ref[pl.ds(pl.multiple_of(t * Q, Q), Q), :]
    ch = p_ref[side, 0, rows, :width]
    prior = jnp.maximum(t - 1, 0)
    prev = p_ref[lax.rem(lax.div(prior, 2) + core, 2), 0, pl.ds(pl.multiple_of(lax.rem(prior, 2) * Q + Q - 8, 8), 8), :width]
    prev = prev * jnp.where(t == 0, 0.0, 1.0)
    conv, shifted = conv_of(ch, jnp.concatenate([prev, ch], 0), aux, par, width)
    sig = 1.0 / (1.0 + jnp.exp(-conv))
    act = conv * sig
    x_in, bm, cm = act[:, :inner], act[:, inner : inner + nst], act[:, inner + nst :]
    pre, dt, cum = rates(p_ref[side, 0, rows, width:], hp)
    low = iota((Q, 2 * head), 1) < head
    squares, dt_w, enter_w, leave_w, through_w = widen(cum, dt, aux, inner // head, low)
    xdt = x_in * dt_w
    scores = mm3(cm, bm, ((1,), (1,)))
    allowed = (iota((Q, Q), 0) >= iota((Q, Q), 1)) & (aux[:, 0:1] == seg_ref[t, 0:1, :])
    cum_t = cum.T
    bm = bm.astype(BF16)
    cm = cm.astype(BF16)
    dy = dy_ref[side, 0, rows, :]
    s_in = sin_ref[t]
    d_state = state[...]
    s_in_b = s_in.astype(BF16)
    d_state_b = d_state.astype(BF16)

    dye = (dy * enter_w).astype(BF16)
    inter = mm(cm, s_in_b) * enter_w
    from_state = mm(bm, d_state_b) * leave_w
    state[...] = mm(cm, dye, ((0,), (0,))) + through_w * d_state
    d_c = mm(dye, s_in_b, ((1,), (1,)))
    d_b = mm(xdt * leave_w, d_state_b, ((1,), (1,)))

    lane = iota((Q, Q), 1)
    sub = iota((8, Q), 0)
    d_scores = jnp.zeros((Q, Q), F32)
    row_sums = jnp.zeros((Q, Q), F32)
    col_sums = jnp.zeros((8, Q), F32)
    d_xdt = []
    for pair in range(inner // (2 * head)):
        cols = slice(2 * head * pair, 2 * head * (pair + 1))
        xp = xdt[:, cols]
        dyp = dy[:, cols]
        d_k2 = mm3(dyp, jnp.concatenate([jnp.where(low, xp, 0.0), jnp.where(low, 0.0, xp)], 0), ((1,), (1,)))
        kmats = []
        for k in range(2):
            h = 2 * pair + k
            decay = jnp.exp(jnp.where(allowed, squares[h] - cum_t[h : h + 1, :], NEG))
            d_k = d_k2[:, k * Q : (k + 1) * Q]
            kmat = scores * decay
            d_scores = d_scores + d_k * decay
            both = d_k * kmat
            row_sums = jnp.where(lane == h, jnp.sum(both, 1, keepdims=True), row_sums)
            col_sums = jnp.where(sub == h, jnp.sum(both, 0, keepdims=True), col_sums)
            kmats.append(kmat)
        dy_by_head = jnp.concatenate([jnp.where(low, dyp, 0.0), jnp.where(low, 0.0, dyp)], 0)
        d_xdt.append(mm3(jnp.concatenate(kmats, 0), dy_by_head, ((0,), (0,))))
    z = jnp.concatenate(d_xdt, 1) + from_state
    d_c = d_c + mm(d_scores, bm)
    d_b = d_b + mm(d_scores, cm, ((0,), (0,)))
    d_x = z * dt_w + par[6:7, :inner] * dy

    leaving = xdt * from_state
    ending = jnp.sum(s_in * d_state, 0, keepdims=True) * through_w + jnp.sum(leaving, 0, keepdims=True)
    folded = mm_fold(
        jnp.concatenate([x_in * z, dy * inter - leaving, jnp.broadcast_to(ending, (8, inner))], 0), gather_mat(inner, Q, head)
    )
    col_full = jnp.concatenate([col_sums, jnp.zeros((Q - 8, Q), F32)], 0).T
    d_cum = row_sums - col_full + folded[Q : 2 * Q]
    tri_up = (iota((Q, Q), 0) <= iota((Q, Q), 1)).astype(BF16)
    rev = mm_tri(tri_up, d_cum) + folded[2 * Q : 2 * Q + 1]
    d_dt = folded[:Q] - hp[1:2] * rev
    d_raw = d_dt / (1.0 + jnp.exp(-pre))
    live = (iota((1, Q), 1) < inner // head).astype(F32)
    d_raw = d_raw * live
    ghead_ref[0:1, :] += jnp.sum(d_raw, 0, keepdims=True)
    ghead_ref[1:2, :] += jnp.sum(rev * dt, 0, keepdims=True) * -hp[1:2]
    gskip_ref[0:1, :] += jnp.sum(dy * x_in, 0, keepdims=True)

    d_act = jnp.concatenate([d_x, d_b, d_c], 1)
    d_conv = d_act * (sig * (1.0 + conv * (1.0 - sig)))
    gconv_ref[4:5, :] += jnp.sum(d_conv, 0, keepdims=True)
    gconv_ref[3:4, :] += jnp.sum(d_conv * ch, 0, keepdims=True)
    d_ch = d_conv * par[3:4, :width]
    for s in range(1, 4):
        gconv_ref[3 - s : 4 - s, :] += jnp.sum(d_conv * shifted[s - 1], 0, keepdims=True)
        u = d_conv * aux[:, s : s + 1] * par[3 - s : 4 - s, :width]
        d_ch = d_ch + pltpu.roll(jnp.concatenate([u, rim[s - 1]], 0), Q + 8 - s, 0)[:Q]
        rim[s - 1] = u[:8]
    dp_ref[side, 0, rows, :width] = d_ch.astype(BF16)
    dp_ref[side, 0, rows, width:] = d_raw.astype(BF16)


def rows_spec(cols, first=0):
    return pl.BlockSpec((2, 1, CHUNKS * Q // 2, cols), lambda r, c: (0, r + first, 0, 0))


def common_specs(wide, width, first=0):
    return [
        rows_spec(wide, first),
        pl.BlockSpec((CHUNKS * Q, 128), lambda r, c: (r + first, 0)),
        pl.BlockSpec((CHUNKS, 8, Q), lambda r, c: (r + first, 0, 0)),
        pl.BlockSpec((8, width), lambda r, c: (0, 0)),
        pl.BlockSpec((8, 128), lambda r, c: (0, 0)),
    ]


def ssd_fwd(core, proj, aux, seg_rows, par, hp, *, inner, nst, head, interpret=False):
    seqs, half, wide = proj.shape[1:]
    rows = 2 * seqs * half
    width = inner + 2 * nst
    spec = pltpu.PrefetchScalarGridSpec(
        num_scalar_prefetch=1,
        grid=(seqs,),
        in_specs=common_specs(wide, width),
        out_specs=[rows_spec(inner), pl.BlockSpec((CHUNKS, nst, inner), lambda r, c: (r, 0, 0))],
        scratch_shapes=[pltpu.VMEM((8, width), F32), pltpu.VMEM((nst, inner), F32)],
    )
    y, s_in = pl.pallas_call(
        functools.partial(ssd_fwd_kernel, inner=inner, nst=nst, head=head),
        grid_spec=spec,
        out_shape=[
            jax.ShapeDtypeStruct((2, seqs, CHUNKS * Q // 2, inner), F32),
            jax.ShapeDtypeStruct((seqs * CHUNKS, nst, inner), F32),
        ],
        cost_estimate=pl.CostEstimate(flops=1, transcendentals=0, bytes_accessed=1),
        interpret=interpret,
        name="ssd_fwd",
        compiler_params=pltpu.CompilerParams(vmem_limit_bytes=14 << 20),
    )(core, proj, aux, seg_rows, par, hp)
    return y, s_in


def ssd_bwd(core, proj, aux, seg_rows, par, hp, dy, s_in, first, count, so_far, *, inner, nst, head, interpret=False):
    seqs, half, wide = proj.shape[1:]
    rows = 2 * seqs * half
    width = inner + 2 * nst
    out_specs = [
        rows_spec(wide, first),
        pl.BlockSpec((8, width), lambda r, c: (0, 0)),
        pl.BlockSpec((8, 128), lambda r, c: (0, 0)),
        pl.BlockSpec((8, inner), lambda r, c: (0, 0)),
    ]
    in_specs = common_specs(wide, width, first) + [
        rows_spec(inner, first),
        pl.BlockSpec((CHUNKS, nst, inner), lambda r, c: (r + first, 0, 0)),
    ]
    operands = (core, proj, aux, seg_rows, par, hp, dy, s_in)
    aliases = {}
    if so_far is not None:
        aliases = {len(operands) + i: i for i in range(4)}
        in_specs += [pl.BlockSpec(memory_space=pl.ANY)] + out_specs[1:]
        operands += tuple(so_far)
    spec = pltpu.PrefetchScalarGridSpec(
        num_scalar_prefetch=1,
        grid=(count,),
        in_specs=in_specs,
        out_specs=out_specs,
        scratch_shapes=[pltpu.VMEM((3, 8, width), F32), pltpu.VMEM((nst, inner), F32)],
    )
    return pl.pallas_call(
        functools.partial(ssd_bwd_kernel, inner=inner, nst=nst, head=head),
        grid_spec=spec,
        out_shape=[
            jax.ShapeDtypeStruct((2, seqs, CHUNKS * Q // 2, wide), BF16),
            jax.ShapeDtypeStruct((8, width), F32),
            jax.ShapeDtypeStruct((8, 128), F32),
            jax.ShapeDtypeStruct((8, inner), F32),
        ],
        input_output_aliases=aliases,
        cost_estimate=pl.CostEstimate(flops=1, transcendentals=0, bytes_accessed=1),
        interpret=interpret,
        name="ssd_bwd",
    )(*operands)


def masks_of(seg):
    s_count, length = seg.shape
    cols = [seg.astype(F32)]
    for s in range(1, 4):
        back = jnp.concatenate([jnp.full((s_count, s), -1, seg.dtype), seg[:, :-s]], 1)
        cols.append((back == seg).astype(F32))
    by_chunk = seg.reshape(s_count, length // Q, Q)
    last = by_chunk[:, :, -1:]
    prev = jnp.concatenate([jnp.full((s_count, 1, 1), -1, seg.dtype), last[:, :-1]], 1)
    cols.append((by_chunk == prev).astype(F32).reshape(s_count, length))
    cols.append((by_chunk == last).astype(F32).reshape(s_count, length))
    cols.append(jnp.broadcast_to(prev == last, by_chunk.shape).astype(F32).reshape(s_count, length))
    aux = jnp.stack(cols, -1).reshape(s_count * length, len(cols))
    aux = jnp.pad(aux, ((0, 0), (0, 128 - len(cols))))
    rows = jnp.broadcast_to(seg.astype(F32).reshape(-1, 1, Q), (s_count * length // Q, 8, Q))
    return aux, rows


EPS = 1e-05
AXES = ("z", "y", "x", "c")


def pull(a, axis, d):
    return lax.ppermute(a, axis, [((i + d) % 4, i) for i in range(4)])


def swap(a):
    return lax.ppermute(a, "c", [(0, 1), (1, 0)])


def transpose_zy(a):
    return lax.ppermute(a, ("z", "y"), [(4 * y + z, 4 * z + y) for z in range(4) for y in range(4)])


def ring(a):
    return tuple(pull(a, "z", d) for d in (1, 2, 3))


def ring_ends(a):
    return pull(a, "z", 1), pull(a, "z", 3)


def ring_middle(one, three):
    half = one.shape[0] // 2
    return pull(one[:half], "z", 1), pull(three[half:], "z", 3)


def ring_back(q):
    return tuple(pull(q[d], "z", 4 - d) for d in (1, 2, 3))


def plane_all(a):
    return lax.all_gather(a, ("y", "x"), axis=0)


def plane_all_small(a):
    return lax.all_to_all(jnp.broadcast_to(a[None], (16,) + a.shape), ("y", "x"), 0, 0)


def tie(*values):
    return lax.optimization_barrier(values)


def two_terms(a):
    top = lax.reduce_precision(a, 8, 7)
    return top.astype(BF16), (a - top).astype(BF16)


def after(value, *others):
    return lax.optimization_barrier((value,) + others)[0]


def cost(flops, bytes_accessed):
    return pl.CostEstimate(flops=1, transcendentals=0, bytes_accessed=1)


def whole(shape):
    return pl.BlockSpec(shape, lambda *_: (0,) * len(shape))


PER = 2


def near_spec(rows, cols):
    return pl.BlockSpec((PER, rows, cols), lambda h, r: (jnp.where(h == 0, r, 4 // PER - 1), 0, 0))


def far_spec(rows, cols):
    return pl.BlockSpec((PER, rows, cols), lambda h, r: (jnp.where(h == 0, 0, r), 0, 0))


def block_spec(cols, rows=256):
    return pl.BlockSpec((1, PER, rows, cols), lambda h, r: (h, r, 0, 0))


def flat_rows(ref):
    v = ref[0] if len(ref.shape) == 4 else ref[...]
    return v.reshape(v.shape[0] * v.shape[1], v.shape[2])


def put_rows(ref, v):
    if len(ref.shape) == 4:
        ref[0] = v.reshape(ref.shape[1:])
    else:
        ref[...] = v.reshape(ref.shape)


def half_cols(core, width):
    return pl.ds(pl.multiple_of(core * width, width), width), pl.ds(pl.multiple_of((1 - core) * width, width), width)


def enter_kernel(near_ref, far_ref, gain_ref, w_ref, normed_ref, proj_ref):
    def step(ref):
        p = flat_rows(ref).astype(F32)
        inverse = lax.rsqrt(jnp.mean(p * p, -1, keepdims=True) + EPS)
        normed = (p * inverse * gain_ref[...]).astype(BF16)
        put_rows(normed_ref, normed)
        put_rows(proj_ref, jnp.dot(normed, w_ref[...], preferred_element_type=F32))

    pl.when(pl.program_id(0) == 0)(lambda: step(near_ref))
    pl.when(pl.program_id(0) == 1)(lambda: step(far_ref))


def enter(near, far, gain, w):
    padded, model = near.shape[1:]
    rows, cols = 256, w.shape[1]
    return pl.pallas_call(
        enter_kernel,
        grid=(2, 4 // PER),
        out_shape=[jax.ShapeDtypeStruct((2, 4, rows, model), BF16), jax.ShapeDtypeStruct((2, 4, rows, cols), F32)],
        in_specs=[near_spec(padded, model), far_spec(padded, model), whole((1, model)), whole(w.shape)],
        out_specs=[block_spec(model), block_spec(cols)],
        cost_estimate=cost(16 * rows * model * cols, 8 * rows * (4 * model + 4 * cols)),
        name="enter",
        compiler_params=pltpu.CompilerParams(vmem_limit_bytes=24 << 20),
    )(near, far, gain, w)


def gate_kernel(core_ref, normed_ref, near_ref, far_ref, wg_ref, wo_ref, wt_ref, y_ref, gain_ref, gate_ref, dm_ref, sums_ref):
    gate = jnp.dot(flat_rows(normed_ref), wg_ref[...], preferred_element_type=F32)
    here, there = half_cols(core_ref[0], wo_ref.shape[1])
    dims = (((1,), (1,)), ((), ()))

    def back(cot_ref):
        rows = gate.shape[0]
        a = cot_ref[:, :, here].reshape(rows, wo_ref.shape[1])
        b = cot_ref[:, :, there].reshape(rows, wo_ref.shape[1])
        put_rows(
            dm_ref,
            lax.dot_general(a, wo_ref[...], dims, preferred_element_type=F32)
            + lax.dot_general(b, wt_ref[...], dims, preferred_element_type=F32),
        )

    pl.when(pl.program_id(0) == 0)(lambda: back(near_ref))
    pl.when(pl.program_id(0) == 1)(lambda: back(far_ref))
    d_mixed = flat_rows(dm_ref)
    put_rows(gate_ref, gate)
    gated = flat_rows(y_ref) * gate / (1.0 + jnp.exp(-gate))
    ones = jnp.ones((8, gate.shape[1]), BF16)

    def total(v):
        top, low = halves(v)
        return (mm(ones, top, ((1,), (1,))) + mm(ones, low, ((1,), (1,))))[:1]

    both = jnp.concatenate([total(gated * gated), total(d_mixed * gain_ref[...] * gated)], 0)
    rows = sums_ref.shape[3]
    for q in range(PER):
        sums_ref[0, q] = both[:, q * rows : (q + 1) * rows]


def gate_stage(core, normed, near, far, w_g, w_o, w_t, y, gain):
    rows, model = normed.shape[2:]
    mine = w_g.shape[1]
    return pl.pallas_call(
        gate_kernel,
        grid=(2, 4 // PER),
        out_shape=[jax.ShapeDtypeStruct((2, 4, rows, mine), F32)] * 2 + [jax.ShapeDtypeStruct((2, 4, 2, rows), F32)],
        in_specs=[
            pl.BlockSpec(memory_space=pltpu.SMEM),
            block_spec(model),
            near_spec(rows, model),
            far_spec(rows, model),
            whole(w_g.shape),
            whole(w_o.shape),
            whole(w_t.shape),
            block_spec(mine),
            whole((1, mine)),
        ],
        out_specs=[block_spec(mine), block_spec(mine), block_spec(rows, 2)],
        cost_estimate=cost(32 * rows * model * mine, 8 * rows * (4 * model + 12 * mine)),
        name="gate_stage",
    )(core, normed, near, far, w_g, w_o, w_t, y, gain)


def turn_kernel(
    core_ref, normed_ref, near_ref, far_ref, wo_ref, wt_ref, y_ref, gate_ref, dm_ref, sums_ref, gain_ref,
    out_near_ref, out_far_ref, dy_ref, dgate_ref, keep_ref, send_ref, ggate_ref, ggain_ref, acc_o, acc_g, *, inner,
):
    h, r = pl.program_id(0), pl.program_id(1)
    rows = gate_ref.shape[2]
    gate, d_mixed, y, gain = flat_rows(gate_ref), flat_rows(dm_ref), flat_rows(y_ref), gain_ref[...]
    sums = jnp.concatenate(
        [jnp.concatenate([sums_ref[0, q], jnp.zeros((6, rows), F32)], 0).T for q in range(PER)], 0
    )
    scale = lax.rsqrt(sums[:, 0:1] / inner + EPS)
    lean = sums[:, 1:2] / inner * scale * scale
    sig = 1.0 / (1.0 + jnp.exp(-gate))
    act = gate * sig
    gated = y * act
    mixed = (gated * scale * gain).astype(BF16)
    d_gated = scale * (d_mixed * gain - gated * lean)
    put_rows(dy_ref, d_gated * act)
    d_gate = (d_gated * y * (sig * (1.0 + gate * (1.0 - sig)))).astype(BF16)
    put_rows(dgate_ref, d_gate)
    here, there = half_cols(core_ref[0], wo_ref.shape[1])

    def forward(out_ref, cot_ref):
        shape = out_ref.shape[:2] + (wo_ref.shape[1],)
        out_ref[:, :, here] = jnp.dot(mixed, wo_ref[...], preferred_element_type=F32).astype(BF16).reshape(shape)
        out_ref[:, :, there] = jnp.dot(mixed, wt_ref[...], preferred_element_type=F32).astype(BF16).reshape(shape)
        acc_o[...] += lax.dot_general(mixed, flat_rows(cot_ref), (((0,), (0,)), ((), ())), preferred_element_type=F32)

    @pl.when((h == 0) & (r == 0))
    def _():
        acc_o[...] = jnp.zeros_like(acc_o)
        acc_g[...] = jnp.zeros_like(acc_g)
        ggain_ref[...] = jnp.zeros_like(ggain_ref)

    ggain_ref[0:1, :] += jnp.sum(d_mixed * gated * scale, 0, keepdims=True)
    pl.when(h == 0)(lambda: forward(out_near_ref, near_ref))
    pl.when(h == 1)(lambda: forward(out_far_ref, far_ref))
    acc_g[...] += lax.dot_general(flat_rows(normed_ref), d_gate, (((0,), (0,)), ((), ())), preferred_element_type=F32)

    @pl.when((h == 1) & (r == pl.num_programs(1) - 1))
    def _():
        keep_ref[...] = acc_o[:, here].astype(BF16)
        send_ref[...] = acc_o[:, there].astype(BF16)
        ggate_ref[:, :, : acc_g.shape[1]] = acc_g[...].astype(BF16).reshape(16, -1, acc_g.shape[1])


def turn_stage(core, normed, near, far, w_o, w_t, y, gate, d_mixed, sums, gain, inner):
    rows, model = normed.shape[2:]
    mine = w_o.shape[0]
    blocks = (16, model // 16, 2 * mine)
    return pl.pallas_call(
        functools.partial(turn_kernel, inner=inner),
        grid=(2, 4 // PER),
        out_shape=[
            jax.ShapeDtypeStruct((4, rows, model), BF16),
            jax.ShapeDtypeStruct((4, rows, model), BF16),
            jax.ShapeDtypeStruct((2, 4, rows, mine), F32),
            jax.ShapeDtypeStruct((2, 4, rows, mine), BF16),
            jax.ShapeDtypeStruct(w_o.shape, BF16),
            jax.ShapeDtypeStruct(w_o.shape, BF16),
            jax.ShapeDtypeStruct(blocks, BF16),
            jax.ShapeDtypeStruct((8, mine), F32),
        ],
        in_specs=[
            pl.BlockSpec(memory_space=pltpu.SMEM),
            block_spec(model),
            near_spec(rows, model),
            far_spec(rows, model),
            whole(w_o.shape),
            whole(w_o.shape),
            block_spec(mine),
            block_spec(mine),
            block_spec(mine),
            block_spec(rows, 2),
            whole((1, mine)),
        ],
        out_specs=[
            near_spec(rows, model),
            far_spec(rows, model),
            block_spec(mine),
            block_spec(mine),
            whole(w_o.shape),
            whole(w_o.shape),
            whole(blocks),
            whole((8, mine)),
        ],
        scratch_shapes=[pltpu.VMEM((mine, model), F32), pltpu.VMEM((model, mine), F32)],
        cost_estimate=cost(48 * rows * model * mine, 8 * rows * (6 * model + 18 * mine)),
        name="turn_stage",
    )(core, normed, near, far, w_o, w_t, y, gate, d_mixed, sums, gain)


def back_kernel(dp_ref, wa_ref, dg_ref, wg_ref, near_ref, far_ref):
    t = lax.dot_general(flat_rows(dp_ref), wa_ref[...], (((1,), (1,)), ((), ())), preferred_element_type=F32)
    t = t + lax.dot_general(flat_rows(dg_ref), wg_ref[...], (((1,), (1,)), ((), ())), preferred_element_type=F32)
    pl.when(pl.program_id(0) == 0)(lambda: put_rows(near_ref, t.astype(BF16)))
    pl.when(pl.program_id(0) == 1)(lambda: put_rows(far_ref, t.astype(BF16)))


def back_dot(d_proj, w_a, d_gate, w_g):
    rows, ka = d_proj.shape[2:]
    m, kg = w_g.shape
    return pl.pallas_call(
        back_kernel,
        grid=(2, 4 // PER),
        out_shape=[jax.ShapeDtypeStruct((4, rows, m), BF16)] * 2,
        in_specs=[block_spec(ka), whole((m, ka)), block_spec(kg), whole((m, kg))],
        out_specs=[near_spec(rows, m), far_spec(rows, m)],
        cost_estimate=cost(0, 0),
        name="back_dot",
    )(d_proj, w_a, d_gate, w_g)


def unpack_kernel(core_ref, all_ref, wg_ref, mine_ref, send_ref):
    rows, width = all_ref.shape[1:]
    part, cols = rows // 2, wg_ref.shape[1]
    for k in range(16):
        wg_ref[k * rows : (k + 1) * rows, :] = all_ref[k, :, :cols]

    def move(ref, side):
        for x in (2 * side, 2 * side + 1):
            for y in range(4):
                at = (4 * (x % 2) + y) * part
                for k in range(2):
                    piece = all_ref[4 * y + x, k * part : (k + 1) * part, cols:]
                    ref[at : at + part, k * (width - cols) : (k + 1) * (width - cols)] = piece

    for core in range(2):

        @pl.when(core_ref[0] == core)
        def _():
            move(mine_ref, core)
            move(send_ref, 1 - core)


def unpack(core, gathered, cols):
    _, rows, width = gathered.shape
    half = jax.ShapeDtypeStruct((4 * rows, 2 * (width - cols)), BF16)
    return pl.pallas_call(
        unpack_kernel,
        in_specs=[pl.BlockSpec(memory_space=pltpu.SMEM), whole(gathered.shape)],
        out_specs=[whole((16 * rows, cols)), whole(half.shape), whole(half.shape)],
        grid=(1,),
        out_shape=[jax.ShapeDtypeStruct((16 * rows, cols), BF16), half, half],
        cost_estimate=cost(0, 0),
        name="unpack",
    )(core, gathered)


def pack_kernel(core_ref, gate_ref, keep_ref, got_ref, out_ref):
    del gate_ref
    rows, width = out_ref.shape[1:]
    part = rows // 2

    def move(ref, side):
        for x in (2 * side, 2 * side + 1):
            for y in range(4):
                at = (4 * (x % 2) + y) * part
                for k in range(2):
                    out_ref[4 * y + x, k * part : (k + 1) * part, :] = ref[at : at + part, k * width : (k + 1) * width]

    for core in range(2):

        @pl.when(core_ref[0] == core)
        def _():
            move(keep_ref, core)
            move(got_ref, 1 - core)


def pack(core, g_gate, keep, got):
    _, rows, width = g_gate.shape
    return pl.pallas_call(
        pack_kernel,
        in_specs=[
            pl.BlockSpec(memory_space=pltpu.SMEM),
            pl.BlockSpec(memory_space=pl.ANY),
            whole(keep.shape),
            whole(got.shape),
        ],
        out_specs=pl.BlockSpec((16, rows, width // 2), lambda *_: (0, 0, 1)),
        grid=(1,),
        out_shape=jax.ShapeDtypeStruct(g_gate.shape, BF16),
        input_output_aliases={1: 0},
        cost_estimate=cost(0, 0),
        name="pack",
    )(core, g_gate, keep, got)


def assemble_kernel(
    at_ref, near_ref, far_ref, win_ref, gain_ref, gwin_ref, gwo_ref, norm_ref, convw_ref, convb_ref, dtb_ref, alog_ref,
    skip_ref, outg_ref, conv_ref, wide_ref, *, mine, nst, my_heads,
):
    z, core, shard = at_ref[0], at_ref[1], at_ref[2]
    rows, wide = win_ref.shape
    inner = 8 * mine
    part = gwo_ref.shape[0] // 4
    width = mine + 2 * nst + 128
    bc = jnp.zeros((rows, 2 * nst), F32)
    conv_bc = jnp.zeros((8, 2 * nst), F32)
    heads = jnp.zeros((8, 128), F32)
    width_c = mine + 2 * nst
    raw = jnp.zeros((rows, 128), F32)
    lane = iota((rows, 128), 1)
    for zz in range(4):
        r = lax.rem(zz - z + 4, 4)
        for cc in range(2):
            j = 2 * zz + cc
            both = jnp.where(core == cc, near_ref[r].astype(F32), far_ref[r].astype(F32))
            v = both[rows : rows + 8] + both[rows + 8 : rows + 16]
            conv_ref[:, j * mine : (j + 1) * mine] = v[:, :mine]
            conv_bc = conv_bc + v[:, mine:width_c]
            h = jnp.where(iota((8, 128), 1) < my_heads, v[:, width_c : width_c + 128], 0.0)
            heads = heads + (pltpu.roll(h, j * my_heads, 1) if j else h)
            wide_ref[0:1, j * mine : (j + 1) * mine] = v[0:1, width_c + 128 : width_c + 128 + mine]
            wide_ref[1:2, j * mine : (j + 1) * mine] = v[0:1, width_c + 128 + mine :]
            both = both[:rows]
            a, b = both[:, :width], both[:, width:]
            gwin_ref[:, j * mine : (j + 1) * mine] = b[:, :mine]
            gwin_ref[:, inner + j * mine : inner + (j + 1) * mine] = a[:, :mine]
            bc = bc + a[:, mine : mine + 2 * nst]
            piece = a[:, mine + 2 * nst :]
            piece = jnp.where(lane < my_heads, piece, 0.0)
            raw = raw + (pltpu.roll(piece, j * my_heads, 1) if j else piece)
            for k in range(2):
                cols = (2 * cc + k) * (b.shape[1] - mine)
                gwo_ref[zz * part : (zz + 1) * part, cols : cols + b.shape[1] - mine] = b[k * part : (k + 1) * part, mine:]
    gwin_ref[:, 2 * inner : 2 * inner + 2 * nst] = bc
    gwin_ref[:, 2 * inner + 2 * nst :] = raw[:, : wide - 2 * inner - 2 * nst]
    conv_ref[:, inner:] = conv_bc
    k, kn, hn = convb_ref.shape[1], outg_ref.shape[1], dtb_ref.shape[1]

    def own(v, count):
        total = v.shape[1]
        return pltpu.roll(v, lax.rem(total - shard * count, total), 1)[:, :count]

    conv = own(conv_ref[...], k)
    convw_ref[...] = conv[:4]
    convb_ref[...] = conv[4:5]
    wide_own = own(wide_ref[...], kn)
    outg_ref[...] = wide_own[1:2]
    per = kn // hn
    skips = [jnp.sum(wide_own[0:1, i * per : (i + 1) * per], 1, keepdims=True) for i in range(hn)]
    skip_ref[...] = jnp.concatenate(skips, 1)
    heads = pltpu.roll(heads, lax.rem(128 - shard * hn, 128), 1)
    dtb_ref[...] = heads[0:1, :hn]
    alog_ref[...] = heads[1:2, :hn]
    norm = jnp.sum(gwin_ref[...] * win_ref[...].astype(F32), 1, keepdims=True)
    norm_ref[...] = jnp.broadcast_to(norm, (rows, 128)).T[0:1, :] / gain_ref[...].astype(F32)


def assemble(z, core, shard, near, far, w_in, norm_gain, w_out, k, kn, hn, mine, nst, my_heads):
    at = jnp.stack([z, core[0], shard]).astype(jnp.int32)
    arrays = (near, far, w_in, norm_gain[None])
    shapes = [w_in.shape, w_out.shape, (1, w_in.shape[0]), (4, k), (1, k), (1, hn), (1, hn), (1, hn), (1, kn)]
    return pl.pallas_call(
        functools.partial(assemble_kernel, mine=mine, nst=nst, my_heads=my_heads),
        in_specs=[pl.BlockSpec(memory_space=pltpu.SMEM)] + [whole(a.shape) for a in arrays],
        out_specs=[whole(a) for a in shapes],
        grid=(1,),
        out_shape=[jax.ShapeDtypeStruct(a, F32) for a in shapes],
        scratch_shapes=[pltpu.VMEM((8, 8 * mine + 2 * nst), F32), pltpu.VMEM((2, 8 * mine), F32)],
        cost_estimate=cost(0, 0),
        name="assemble",
    )(at, *arrays)


def dot(a, b, dims):
    return lax.dot_general(a, b, (dims, ((), ())), preferred_element_type=F32)


def local(inputs, segments, norm_gain, w_in, conv_w, conv_b, dt_bias, a_log, d_skip, out_gain, w_out, cotangent):
    z, y, x, c = (lax.axis_index(name) for name in AXES)
    member = 2 * z + c
    length, model = inputs.shape[1:]
    inner = 16 * out_gain.shape[0]
    heads = 16 * d_skip.shape[0]
    xwidth = 16 * conv_b.shape[0]
    nst = (xwidth - inner) // 2
    head = inner // heads
    mine = inner // 8
    my_heads = heads // 8
    core = c.astype(jnp.int32).reshape(1)
    rows_in = w_in.shape[0]

    w_x = lax.dynamic_slice_in_dim(w_in, inner + member * mine, mine, 1)
    w_dt = jnp.pad(
        lax.dynamic_slice_in_dim(w_in[:, inner + xwidth :], member * my_heads, my_heads, 1), ((0, 0), (0, 128 - my_heads))
    )
    w_bc = jnp.concatenate([w_in[:, inner + mine * 8 : inner + xwidth], w_dt], 1)
    block_a = jnp.concatenate([w_x, w_bc], 1)
    all_a = plane_all(block_a)
    w_a = all_a.reshape(model, -1)

    def lanes(a):
        return jnp.pad(a, ((0, 0), (0, -a.shape[1] % 128))).reshape(-1, 128)

    tiny = jnp.concatenate([dt_bias, a_log, d_skip])[None]
    small = jnp.concatenate([lanes(conv_w), lanes(conv_b[None]), lanes(out_gain[None]), lanes(norm_gain[None]), lanes(tiny)], 0)
    small = after(jnp.pad(small, ((0, -small.shape[0] % 16), (0, 0))), block_a)

    x_mine = inputs[0]
    one, three = ring_ends(x_mine)
    middle = ring_middle(one, three)
    seg_mine = after(segments.reshape(-1, 128), block_a)
    seg_all = jnp.stack((seg_mine,) + ring(seg_mine)).reshape(4, -1)
    aux, seg_rows = masks_of(seg_all)

    small = plane_all_small(small).astype(F32)
    k, kn, hn = conv_b.shape[0], out_gain.shape[0], d_skip.shape[0]
    lk, lg = -(-k // 128), -(-kn // 128)
    conv_wf = small[:, : 4 * lk].reshape(16, 4, lk * 128)[:, :, :k].transpose(1, 0, 2).reshape(4, xwidth)
    conv_bf = small[:, 4 * lk : 5 * lk].reshape(16, lk * 128)[:, :k].reshape(1, xwidth)
    gain_f = small[:, 5 * lk : 5 * lk + lg].reshape(16, lg * 128)[:, :kn].reshape(-1)
    norm_f = small[:, 5 * lk + lg, :rows_in].reshape(-1)
    dtb_f, alog_f, skip_f = (small[:, 5 * lk + lg + 1, i * hn : (i + 1) * hn].reshape(-1) for i in range(3))

    def own(a, count):
        return lax.dynamic_slice_in_dim(a, member * count, count, a.ndim - 1)

    conv_all = jnp.concatenate([conv_wf, conv_bf], 0)
    conv_mine = jnp.concatenate([own(conv_all[:, :inner], mine), conv_all[:, inner:]], 1)
    skip_mine = jnp.repeat(own(skip_f, my_heads), head)
    par = jnp.concatenate(
        [conv_mine, jnp.zeros((1, mine + 2 * nst), F32), jnp.pad(skip_mine, (0, 2 * nst))[None], jnp.zeros((1, mine + 2 * nst), F32)], 0
    )
    rates_mine = jnp.stack([own(dtb_f, my_heads), jnp.exp(own(alog_f, my_heads))])
    hp = jnp.pad(rates_mine, ((0, 6), (0, 128 - my_heads)))
    gain_mine = own(gain_f, mine)[None]

    w_g = lax.dynamic_slice_in_dim(w_in, member * mine, mine, 1)
    part = w_out.shape[0] // 4
    half = model // 2
    wo_piece = lax.dynamic_slice(w_out, (z * part, c * half), (part, half))
    wo_piece = transpose_zy(jnp.concatenate([wo_piece[:, : half // 2], wo_piece[:, half // 2 :]], 0))
    block_b = jnp.concatenate([w_g, wo_piece], 1)
    middle, block_b, norm_row, par, hp, gain_mine, aux, seg_rows = tie(
        middle, block_b, norm_f[None], par, hp, gain_mine, aux, seg_rows
    )
    all_b = plane_all(block_b)
    x_near = jnp.stack([x_mine, one, jnp.concatenate(middle, 0), three])
    x_far = swap(x_near)
    cot_ring = ring(after(cotangent[0], x_near))

    sizes_k = dict(inner=mine, nst=nst, head=head)
    normed, proj = enter(x_near, x_far, norm_row, w_a)
    mixed_ssd, s_in = ssd_fwd(core, proj, aux, seg_rows, par, hp, **sizes_k)
    mixed_ssd, cot_ring = tie(mixed_ssd, cot_ring)
    cot_near = jnp.stack((cotangent[0],) + cot_ring)
    cot_far = swap(cot_near)
    all_b = after(all_b, cot_near)
    w_g, w_o, w_t = unpack(core, all_b, mine)
    w_t = swap(w_t)
    gate, d_mixed, sums = gate_stage(core, normed, cot_near, cot_far, w_g, w_o, w_t, mixed_ssd, gain_mine)
    sums = sums + jnp.flip(swap(sums), 0)
    sums = sums + sum(jnp.roll(pull(sums, "z", d), d, 1) for d in (1, 2, 3))
    out_near, out_far, d_y, d_gate, wo_keep, wo_send, g_gate, g_gain = turn_stage(
        core, normed, cot_near, cot_far, w_o, w_t, mixed_ssd, gate, d_mixed, sums, gain_mine, inner
    )

    def core_sum(near, far):
        far = swap(far)
        return [(near[i].astype(F32) + far[i].astype(F32)).astype(BF16) for i in range(4)]

    def core_sum_whole(near, far):
        return (near.astype(F32) + swap(far).astype(F32)).astype(BF16)

    backward = functools.partial(ssd_bwd, core, proj, aux, seg_rows, par, hp, d_y, s_in, **sizes_k)
    so_far, wo_got = tie(backward(0, 1, None), swap(wo_send))
    g_b = pack(core, g_gate, wo_keep, wo_got)
    all_b = lax.all_to_all(g_b, ("y", "x"), 0, 0)
    so_far, out_both = tie(after(so_far, g_b), core_sum(out_near, out_far))
    out_ring = ring_back(out_both)
    d_proj, g_conv, g_head, g_skip = backward(1, 3, so_far)
    raw = jnp.pad(jnp.concatenate([g_conv, g_head, g_skip, g_gain], 1), ((0, 8), (0, 0)))
    d_proj, raw = tie(d_proj, raw)
    raw = jnp.sum(lax.all_gather(raw, ("y", "x"), axis=0), 0)[:8]
    d_near, d_far = back_dot(d_proj, w_a, d_gate, w_g)
    d_proj, d_far, d_near, all_b, out_ring = tie(d_proj, d_far, d_near, all_b, out_ring)
    flat = 8 * length
    g_a = dot(normed.reshape(flat, model), d_proj.reshape(flat, -1), ((0,), (0,))).astype(BF16)
    sum_b = jnp.sum(all_b.astype(F32), 0).astype(BF16)

    g_a, d_both = tie(g_a, core_sum_whole(d_near, d_far))
    all_sums = lax.all_to_all(g_a.reshape(16, rows_in, -1), ("y", "x"), 0, 0)
    d_ring = ring_back(d_both)
    wo_sum = transpose_zy(sum_b[:, mine:])
    output = (x_mine.astype(F32) + sum(p.astype(F32) for p in (out_both[0],) + out_ring)).astype(BF16)

    all_sums, wo_sum, raw, d_ring = tie(all_sums, wo_sum, raw, d_ring)
    last = jnp.concatenate([jnp.sum(all_sums.astype(F32), 0).astype(BF16), sum_b[:, :mine], wo_sum], 1)
    last = jnp.concatenate([last, *two_terms(raw)], 0)
    last_ring = ring(last)
    d_normed = sum(p.astype(F32) for p in (d_both[0],) + d_ring)
    x_f = x_mine.astype(F32)
    inverse = lax.rsqrt(jnp.mean(x_f * x_f, -1, keepdims=True) + EPS)
    scaled = x_f * inverse
    d_hat = d_normed * norm_f[None]
    d_x = inverse * (d_hat - scaled * jnp.mean(d_hat * scaled, -1, keepdims=True))
    input_grad = (cotangent[0].astype(F32) + d_x).astype(BF16)

    last_ring, input_grad = tie(last_ring, input_grad)
    near = jnp.stack((last,) + last_ring)
    shard = 4 * y + x
    w_in_grad, w_out_grad, *others = assemble(
        z, core, shard, near, swap(near), w_in, norm_gain, w_out, k, kn, hn, mine, nst, my_heads
    )
    norm_gain_grad, conv_w_grad = others[0][0], others[1]
    conv_b_grad, dt_bias_grad, a_log_grad, d_skip_grad, out_gain_grad = (o[0] for o in others[2:])
    return (
        output[None],
        input_grad[None],
        norm_gain_grad,
        w_in_grad,
        conv_w_grad,
        conv_b_grad,
        dt_bias_grad,
        a_log_grad,
        d_skip_grad,
        out_gain_grad,
        w_out_grad,
    )


def solution(mesh):
    cube = Mesh(mesh.devices.reshape(4, 4, 4, 2), AXES)
    rows, shard = P(("z", "y", "x"), "c", None), ("y", "x")
    return jax.shard_map(
        local,
        mesh=cube,
        in_specs=(
            rows,
            P(("z", "y", "x"), None),
            P(shard),
            P(shard, None),
            P(None, shard),
            P(shard),
            P(shard),
            P(shard),
            P(shard),
            P(shard),
            P(shard, None),
            rows,
        ),
        out_specs=(
            rows,
            rows,
            P(shard),
            P(shard, None),
            P(None, shard),
            P(shard),
            P(shard),
            P(shard),
            P(shard),
            P(shard),
            P(shard, None),
        ),
        check_vma=False,
    )
```
